32 devices in a mesh: group: 2 (over x), src: 16 (over z, y, core).
Axes of the slice: x: 2, y: 2, z: 4, core: 2. Of those that a mesh axis runs over, the one named last changes fastest.
Arguments:
- rcv_points: float32 [3, 4096], P(None, ('group', 'src')), parts along dimension 1, may hold values from -1 to 1
- rcv_normals: float32 [3, 4096], P(None, ('group', 'src')), parts along dimension 1, may hold values from -4 to 4
- left_modes: float32 [8, 4096], P(None, ('group', 'src')), parts along dimension 1, may hold values from -5 to 5
- vertices: float32 [3, 2048], P(None, ('group', 'src')), parts along dimension 1, may hold values from -1 to 1
- connect: int32 [2, 4096], P(None, ('group', 'src')), parts along dimension 1, may hold values from 0 to 1023, as said below
- right_modes: float32 [8, 4096], P(None, ('group', 'src')), parts along dimension 1, may hold values from -0.125 to 0.125
- mode_weights: float32 [16], P('group'), parts along dimension 0, may hold values from 0.25 to 1
Outputs:
- rcv_grad: float32 [6, 4096], P(None, ('group', 'src')), parts along dimension 1
- vert_grad: float32 [3, 2048], P(None, ('group', 'src')), parts along dimension 1
The draws below stay inside these ranges and needn't reach their ends.
There are 2 independent parts, one for each index of `group`. The reference program is written for one: setup_inputs(seed, part) draws one part's arguments, and reference() takes and returns one part's arrays. A program takes and returns all parts, laid end to end along the dimension named above; each array names one. Nothing has to cross between parts.
Inputs may be any that keep to these rules, and one draw needn't show every extreme that they name: `connect`: a panel's first vertex is one of the 64 vertices held at the same index of src as the panel, and its second vertex is the next vertex number.
All inputs are finite; a program needn't handle non-finite values.
Results may differ from the reference program's by a relative error of at most 0.0003.
Values sent between devices are 32-bit elements; how exact they have to be, the bound alone decides.
No kernel may reach another device: no remote copies, remote signals or barrier semaphores. Data moves between devices by JAX's collectives and lax.ppermute only.
A program may use at most 64 MiB of HBM per device.

```python
import math
import jax
import jax.numpy as jnp
from jax import lax

MODES = 8
SRC_DEV = 128
VERT_DEV = 64
RECEIVERS = 2048
PANELS = 2048
VERTICES = 1024


def draw_connect(key, part):
    devices = PANELS // SRC_DEV
    panel = jnp.arange(PANELS, dtype=jnp.int32)
    owner = panel // SRC_DEV
    local = panel % SRC_DEV
    last = owner == devices - 1
    offsets = jax.random.randint(jax.random.fold_in(key, 7), (PANELS,), 0, VERT_DEV, dtype=jnp.int32)
    offsets = jnp.where(last, offsets % (VERT_DEV - 1), offsets)
    offsets = jnp.where(local == 0, jnp.where(last, VERT_DEV - 2, VERT_DEV - 1), offsets)
    offsets = jnp.where(local == 1, 0, offsets)
    first = owner * VERT_DEV + offsets
    return jnp.stack([first, first + 1]).astype(jnp.int32)


def level_of(own_key, dims, cuts, low, high):
    def one(axis_at, parts):
        draws = jax.random.uniform(jax.random.fold_in(jax.random.fold_in(own_key, 6), axis_at), (parts,), jnp.float32, low / len(cuts), high / len(cuts))
        return jnp.repeat(jnp.exp(draws), dims[axis_at] // parts).reshape((-1,) + (1,) * (len(dims) - axis_at - 1))

    factor_of = one(*cuts[0])
    for cut in cuts[1:]:
        factor_of = factor_of * one(*cut)
    return factor_of


def scatter_about(own_key, shape, scale, reach, pieces=(), held_as=jnp.bfloat16):
    result = jax.random.normal(own_key, shape, jnp.float32) * scale
    if len(pieces) > 0:
        result = level_of(own_key, shape, pieces, -0.22, 0.18) * result
    return jnp.clip(result, min=-reach, max=reach).astype(held_as)


def setup_inputs(seed: int = 0, part: int = 0) -> dict:
    arg_keys = jax.random.split(jax.random.key(seed), 8)
    own_keys = jax.random.split(jax.random.fold_in(arg_keys[7], part), 8)
    rcv_points = jnp.clip(jax.random.uniform(own_keys[0], (3, RECEIVERS), jnp.float32, -1.0, 1.0) * level_of(own_keys[0], (3, RECEIVERS), ((1, 16),), -0.4, 0.0), -1.0, 1.0)
    rcv_normals = scatter_about(own_keys[1], (3, RECEIVERS), 1.0, 4.0, ((1, 16),), jnp.float32)
    left_modes = scatter_about(own_keys[2], (MODES, RECEIVERS), 1.0, 5.0, ((1, 16),), jnp.float32)
    vertices = jnp.clip(jax.random.uniform(own_keys[3], (3, VERTICES), jnp.float32, -1.0, 1.0) * level_of(own_keys[3], (3, VERTICES), ((1, 16),), -0.4, 0.0), -1.0, 1.0)
    connect = draw_connect(jax.random.fold_in(jax.random.fold_in(arg_keys[7], part), 71), part)
    right_modes = scatter_about(own_keys[5], (MODES, PANELS), PANELS ** -0.5, 0.125, ((1, 16),), jnp.float32)
    mode_weights = jnp.clip(jnp.exp(jax.random.uniform(own_keys[6], (MODES,), jnp.float32, math.log(0.25), math.log(1.0))), 0.25, 1.0)
    return {"rcv_points": rcv_points, "rcv_normals": rcv_normals, "left_modes": left_modes, "vertices": vertices, "connect": connect, "right_modes": right_modes, "mode_weights": mode_weights}


core_term = 0.05
inverse_four_pi = 0.25 / math.pi

def lift_points(raw):
    return jnp.stack([raw[0], raw[1], 0.5 + 0.2 * raw[2]])

def place_points(raw):
    return jnp.stack([raw[0], raw[1], 0.2 * raw[2]])

def tile_energy(points, normals, first_end, second_end, coefficient):
    rel_first = points[:, None, :] - first_end[:, :, None]
    rel_second = points[:, None, :] - second_end[:, :, None]
    segment = (second_end - first_end)[:, :, None]
    cross_x = rel_first[1] * rel_second[2] - rel_first[2] * rel_second[1]
    cross_y = rel_first[2] * rel_second[0] - rel_first[0] * rel_second[2]
    cross_z = rel_first[0] * rel_second[1] - rel_first[1] * rel_second[0]
    cross_sq = cross_x * cross_x + cross_y * cross_y + cross_z * cross_z
    dist_first = jnp.sqrt(lax.optimization_barrier(jnp.sum(rel_first * rel_first, axis=0)))
    dist_second = jnp.sqrt(lax.optimization_barrier(jnp.sum(rel_second * rel_second, axis=0)))
    along_term = lax.optimization_barrier(jnp.sum(segment * (rel_first / dist_first - rel_second / dist_second), axis=0))
    span_sq = lax.optimization_barrier(jnp.sum(segment * segment, axis=0))
    denominator = cross_sq + core_term * (span_sq + 1.0)
    normal_term = normals[0][None, :] * cross_x + normals[1][None, :] * cross_y + normals[2][None, :] * cross_z
    influence = inverse_four_pi * normal_term * along_term / denominator
    return jnp.sum(coefficient * influence)

def tile_gradients(points, normals, first_end, second_end, coefficient):
    return jax.grad(tile_energy, argnums=(0, 1, 2, 3))(points, normals, first_end, second_end, coefficient)

def reference(rcv_points, rcv_normals, left_modes, vertices, connect, right_modes, mode_weights):
    points = lift_points(rcv_points)
    places = place_points(vertices)
    first_end = places[:, connect[0]]
    second_end = places[:, connect[1]]
    weighted = right_modes * mode_weights[:, None]
    chain_scale = jnp.array([1.0, 1.0, 0.2], dtype=rcv_points.dtype)[:, None]
    width_rows = math.gcd(RECEIVERS, 512)

    def one_block(position):
        offset = position * width_rows
        block_points = lax.dynamic_slice_in_dim(points, offset, width_rows, 1)
        block_normals = lax.dynamic_slice_in_dim(rcv_normals, offset, width_rows, 1)
        block_left = lax.dynamic_slice_in_dim(left_modes, offset, width_rows, 1)
        coefficient = jnp.einsum('mj,mi->ji', weighted, block_left, precision=lax.Precision.HIGHEST)
        grads = tile_gradients(block_points, block_normals, first_end, second_end, coefficient)
        rows_out = jnp.concatenate([grads[0] * chain_scale, grads[1]], axis=0)
        return (rows_out, grads[2], grads[3])
    blocks_rcv, all_first, all_second = lax.map(one_block, jnp.arange(RECEIVERS // width_rows, dtype=jnp.int32))
    rcv_grad = jnp.transpose(blocks_rcv, (1, 0, 2)).reshape(6, RECEIVERS)
    sum_first = lax.optimization_barrier(jnp.sum(all_first, axis=0))
    sum_second = lax.optimization_barrier(jnp.sum(all_second, axis=0))
    vertex_total = jnp.zeros((3, VERTICES), dtype=rcv_points.dtype)
    vertex_total = vertex_total.at[:, connect[0]].add(sum_first).at[:, connect[1]].add(sum_second)
    return (rcv_grad, vertex_total * chain_scale)
```

```python
import functools
import math

import jax
import jax.numpy as jnp
from jax import lax
from jax.experimental import pallas as pl
from jax.experimental.pallas import tpu as pltpu
from jax.sharding import PartitionSpec as P

core_term = 0.05
inverse_four_pi = 0.25 / math.pi

LANES = 128
ROWS = 24
REC_ROWS = 14
SEG_ROWS = 11


def exchange_masks(count):
    masks = []
    step = count // 2
    while step >= 1:
        masks.append(step)
        step //= 2
    return masks


def position_of(mask_value, masks):
    place = 0
    for bit, step in enumerate(masks):
        place = place + (lax.shift_right_logical(mask_value, step.bit_length() - 1) & 1) * (1 << bit)
    return place


def split2(value):
    high = value.astype(jnp.bfloat16)
    low = (value - high.astype(jnp.float32)).astype(jnp.bfloat16)
    return high, low


def dot_nt(left, right):
    return lax.dot_general(
        left, right, (((1,), (1,)), ((), ())), preferred_element_type=jnp.float32
    )


def contract(values, features):
    vh, vl = split2(values)
    fh, fl = split2(features)
    return dot_nt(vh, fh) + (dot_nt(vh, fl) + dot_nt(vl, fh))


def pair_terms(normal_cross, dist_sq, along, span, scale, want_span):
    second_sq = dist_sq - 2.0 * along + span
    inv_first = lax.rsqrt(dist_sq)
    inv_second = lax.rsqrt(second_sq)
    inv_den = 1.0 / (span * dist_sq + (core_term * span + core_term) - along * along)
    other = along - span
    part_first = along * inv_first
    part_second = other * inv_second
    line = part_first - part_second
    scaled = scale * inv_den
    by_normal = scaled * line
    by_line = scaled * normal_cross
    by_den2 = -2.0 * (by_normal * normal_cross) * inv_den
    cube_first = part_first * (inv_first * inv_first)
    cube_second = part_second * (inv_second * inv_second)
    by_dist2 = by_line * (cube_second - cube_first) + by_den2 * span
    by_along = by_line * ((inv_first - inv_second) - cube_second) - by_den2 * along
    if not want_span:
        return by_normal, by_dist2, by_along
    by_span2 = by_line * (2.0 * inv_second + cube_second) + by_den2 * (dist_sq + core_term)
    return by_normal, by_dist2, by_along, by_span2


def kernel(count, own_seg, gathered_ref, rcv_out, vert_out, seg_ref, own_rec, own_segment):
    masks = exchange_masks(count)
    me = lax.axis_index("src")
    lane = lax.broadcasted_iota(jnp.int32, (1, LANES), 1)
    low_half = lane < own_seg

    def block_start(device):
        return pl.multiple_of(position_of(device ^ me, masks) * ROWS, 8)

    tiles = count // 2

    def fill(tile, carry):
        even = gathered_ref[pl.ds(block_start(2 * tile), ROWS), :][REC_ROWS : REC_ROWS + 6]
        odd = gathered_ref[pl.ds(block_start(2 * tile + 1), ROWS), :][REC_ROWS : REC_ROWS + 6]
        first_rows = jnp.where(low_half, even, pltpu.roll(odd, own_seg, 1))
        last_rows = jnp.where(low_half, pltpu.roll(even, own_seg, 1), odd)
        seg_ref[tile, 0:6, :] = first_rows
        seg_ref[tile, 6:12, :] = last_rows
        return carry

    lax.fori_loop(0, tiles, fill, 0)

    def fill_next(tile, carry):
        here = pltpu.roll(seg_ref[tile, 0:3, :], LANES - 1, 1)
        after = pltpu.roll(seg_ref[(tile + 1) % tiles, 0:3, :], LANES - 1, 1)
        seg_ref[tile, 12:15, :] = jnp.where(lane == LANES - 1, after, here)
        seg_ref[tile, 15:16, :] = jnp.zeros((1, LANES), jnp.float32)
        return carry

    lax.fori_loop(0, tiles, fill_next, 0)

    own_block = gathered_ref[0:16, :]
    own_rec[...] = jnp.transpose(own_block)

    own_tile = me // 2
    mine = seg_ref[own_tile]
    mine = jnp.where(me % 2 == 0, mine, pltpu.roll(mine, own_seg, 1))
    before_tile = (me + count - 1) % count
    before = seg_ref[before_tile // 2]
    before = jnp.where(before_tile % 2 == 0, pltpu.roll(before, 1, 1), pltpu.roll(before, own_seg + 1, 1))
    row = lax.broadcasted_iota(jnp.int32, (16, LANES), 0)
    is_weight = (row >= 3) & (row < 11)
    before = jnp.where(is_weight & (me == 0), 0.0, before)
    mine = jnp.where(lane < own_seg, mine, before)
    own_segment[...] = jnp.transpose(mine)
    mine_rows = mine

    rec = own_rec[...]
    px, py, pz = rec[:, 0:1], rec[:, 1:2], rec[:, 2:3]
    nx, ny, nz = rec[:, 3:4], rec[:, 4:5], rec[:, 5:6]
    left = rec[:, 6:14]

    def first_pass(tile, carry):
        seg = seg_ref[tile]
        ax, ay, az = seg[0:1], seg[1:2], seg[2:3]
        weights = seg[3:11]
        sx, sy, sz = seg[12:13] - ax, seg[13:14] - ay, seg[14:15] - az
        span = sx * sx + sy * sy + sz * sz
        scale = inverse_four_pi * lax.dot_general(
            left, weights, (((1,), (0,)), ((), ())), precision=lax.Precision.HIGHEST,
            preferred_element_type=jnp.float32)
        rx, ry, rz = px - ax, py - ay, pz - az
        normal_cross = nx * (sy * rz - sz * ry) + ny * (sz * rx - sx * rz) + nz * (sx * ry - sy * rx)
        dist_sq = rx * rx + ry * ry + rz * rz
        along = sx * rx + sy * ry + sz * rz
        by_normal, by_dist2, by_along = pair_terms(normal_cross, dist_sq, along, span, scale, False)
        tx, ty, tz = sy * az - sz * ay, sz * ax - sx * az, sx * ay - sy * ax
        ones = jnp.ones_like(ax)
        sum_n, sum_a, sum_u = carry
        sum_n = sum_n + contract(by_normal, jnp.concatenate([sx, sy, sz, tx, ty, tz, ones, ones], 0))
        sum_a = sum_a + contract(by_dist2, jnp.concatenate([ones, ax, ay, az, ones, ones, ones, ones], 0))
        sum_u = sum_u + contract(by_along, jnp.concatenate([sx, sy, sz, ones, ones, ones, ones, ones], 0))
        return sum_n, sum_a, sum_u

    zeros = jnp.zeros((LANES, 8), jnp.float32)
    sum_n, sum_a, sum_u = lax.fori_loop(0, tiles, first_pass, (zeros, zeros, zeros))
    totals = jnp.transpose(jnp.concatenate([sum_n, sum_a, sum_u, zeros] + [jnp.zeros((LANES, 96), jnp.float32)], 1))
    gx, gy, gz = totals[0:1], totals[1:2], totals[2:3]
    hx, hy, hz = totals[3:4], totals[4:5], totals[5:6]
    a1, aex, aey, aez = totals[8:9], totals[9:10], totals[10:11], totals[11:12]
    ux, uy, uz = totals[16:17], totals[17:18], totals[18:19]
    qx, qy, qz = own_block[0:1], own_block[1:2], own_block[2:3]
    mx, my, mz = own_block[3:4], own_block[4:5], own_block[5:6]
    rcv_out[0:1, :] = my * gz - mz * gy + a1 * qx - aex + ux
    rcv_out[1:2, :] = mz * gx - mx * gz + a1 * qy - aey + uy
    rcv_out[2:3, :] = 0.2 * (mx * gy - my * gx + a1 * qz - aez + uz)
    rcv_out[3:4, :] = gy * qz - gz * qy - hx
    rcv_out[4:5, :] = gz * qx - gx * qz - hy
    rcv_out[5:6, :] = gx * qy - gy * qx - hz

    used = own_seg + 8
    cols = own_segment[...][0:used]
    ax, ay, az = cols[:, 0:1], cols[:, 1:2], cols[:, 2:3]
    weights = cols[:, 3:11]
    sx, sy, sz = cols[:, 12:13] - ax, cols[:, 13:14] - ay, cols[:, 14:15] - az
    span = sx * sx + sy * sy + sz * sz

    def second_pass(block, carry):
        rec_rows = gathered_ref[pl.ds(pl.multiple_of(block * ROWS, 8), 16), :]
        px, py, pz = rec_rows[0:1], rec_rows[1:2], rec_rows[2:3]
        nx, ny, nz = rec_rows[3:4], rec_rows[4:5], rec_rows[5:6]
        scale = inverse_four_pi * lax.dot_general(
            weights, rec_rows[6:14], (((1,), (0,)), ((), ())), precision=lax.Precision.HIGHEST,
            preferred_element_type=jnp.float32)
        rx, ry, rz = px - ax, py - ay, pz - az
        normal_cross = nx * (sy * rz - sz * ry) + ny * (sz * rx - sx * rz) + nz * (sx * ry - sy * rx)
        dist_sq = rx * rx + ry * ry + rz * rz
        along = sx * rx + sy * ry + sz * rz
        by_normal, by_dist2, by_along, by_span2 = pair_terms(normal_cross, dist_sq, along, span, scale, True)
        tx, ty, tz = py * nz - pz * ny, pz * nx - px * nz, px * ny - py * nx
        ones = jnp.ones_like(px)
        sum_n, sum_a, sum_u, sum_q = carry
        points_rows = jnp.concatenate([ones, px, py, pz, ones, ones, ones, ones], 0)
        sum_n = sum_n + contract(by_normal, jnp.concatenate([nx, ny, nz, tx, ty, tz, ones, ones], 0))
        sum_a = sum_a + contract(by_dist2, points_rows)
        sum_u = sum_u + contract(by_along, points_rows)
        sum_q = sum_q + by_span2
        return sum_n, sum_a, sum_u, sum_q

    zeros = jnp.zeros((used, 8), jnp.float32)
    sum_n, sum_a, sum_u, sum_q = lax.fori_loop(
        0, count, second_pass, (zeros, zeros, zeros, jnp.zeros((used, LANES), jnp.float32)))
    sum_q = jnp.sum(sum_q, axis=1, keepdims=True)
    totals = jnp.concatenate([sum_n, sum_a, sum_u, sum_q, jnp.zeros((used, LANES - 25), jnp.float32)], 1)
    totals = jnp.transpose(jnp.concatenate([totals, jnp.zeros((LANES - used, LANES), jnp.float32)], 0))
    gx, gy, gz = totals[0:1], totals[1:2], totals[2:3]
    hx, hy, hz = totals[3:4], totals[4:5], totals[5:6]
    a1, apx, apy, apz = totals[8:9], totals[9:10], totals[10:11], totals[11:12]
    u1, upx, upy, upz = totals[16:17], totals[17:18], totals[18:19], totals[19:20]
    q2 = totals[24:25]
    ex, ey, ez = mine_rows[0:1], mine_rows[1:2], mine_rows[2:3]
    sx, sy, sz = mine_rows[12:13] - ex, mine_rows[13:14] - ey, mine_rows[14:15] - ez
    by_s = (
        hx - (ey * gz - ez * gy) + upx - ex * u1 + sx * q2,
        hy - (ez * gx - ex * gz) + upy - ey * u1 + sy * q2,
        hz - (ex * gy - ey * gx) + upz - ez * u1 + sz * q2,
    )
    by_r = (
        gy * sz - gz * sy + apx - ex * a1 + sx * u1,
        gz * sx - gx * sz + apy - ey * a1 + sy * u1,
        gx * sy - gy * sx + apz - ez * a1 + sz * u1,
    )
    for axis in range(3):
        by_second = by_s[axis]
        by_first = -(by_s[axis] + by_r[axis])
        carried = jnp.where(
            lane == 0,
            pltpu.roll(jnp.broadcast_to(by_second, (8, LANES)), LANES - own_seg, 1)[0:1],
            pltpu.roll(jnp.broadcast_to(by_second, (8, LANES)), 1, 1)[0:1],
        )
        result = by_first + carried
        if axis == 2:
            result = 0.2 * result
        vert_out[axis : axis + 1, :] = result[:, 0:own_seg]


def on_device(rcv_points, rcv_normals, left_modes, vertices, connect, right_modes, mode_weights):
    count = lax.axis_size("src")
    own_count = vertices.shape[1]
    base_vertex = lax.axis_index("src") * own_count
    local_first = connect[0] - base_vertex
    weighted = right_modes * mode_weights[:, None]
    one_hot = (local_first[:, None] == jnp.arange(own_count, dtype=jnp.int32)[None, :]).astype(jnp.float32)
    folded = jnp.dot(weighted, one_hot, precision=lax.Precision.HIGHEST)
    lift = jnp.array([1.0, 1.0, 0.2], jnp.float32)[:, None]
    base = jnp.array([0.0, 0.0, 0.5], jnp.float32)[:, None]
    segment_rows = jnp.concatenate([vertices * lift, folded, jnp.zeros((1, own_count), jnp.float32)], 0)
    value = jnp.concatenate(
        [
            rcv_points * lift + base,
            rcv_normals,
            left_modes,
            jnp.concatenate([segment_rows[0:6], segment_rows[6:12]], 1),
            jnp.zeros((ROWS - REC_ROWS - 6, LANES), jnp.float32),
        ],
        0,
    )
    for step in exchange_masks(count):
        other = lax.ppermute(value, "src", [(s, s ^ step) for s in range(count)])
        value = jnp.concatenate([value, other], 0)
    return pl.pallas_call(
        functools.partial(kernel, count, own_count),
        out_shape=(
            jax.ShapeDtypeStruct((6, LANES), jnp.float32),
            jax.ShapeDtypeStruct((3, own_count), jnp.float32),
        ),
        in_specs=[pl.BlockSpec(memory_space=pltpu.VMEM)],
        out_specs=(pl.BlockSpec(memory_space=pltpu.VMEM), pl.BlockSpec(memory_space=pltpu.VMEM)),
        scratch_shapes=[
            pltpu.VMEM((count // 2, 16, LANES), jnp.float32),
            pltpu.VMEM((LANES, 16), jnp.float32),
            pltpu.VMEM((LANES, 16), jnp.float32),
        ],
        compiler_params=pltpu.CompilerParams(vmem_limit_bytes=16 << 20),
    )(value)


def solution(mesh):
    split = P(None, ("group", "src"))
    return jax.shard_map(
        on_device, mesh=mesh, in_specs=(split,) * 6 + (P("group"),), out_specs=(split, split), check_vma=False
    )
```

```python
import functools
import math

import jax
import jax.numpy as jnp
from jax import lax
from jax.experimental import pallas as pl
from jax.experimental.pallas import tpu as pltpu
from jax.sharding import PartitionSpec as P

core_term = 0.05
inverse_four_pi = 0.25 / math.pi

LANES = 128
ROWS = 24
CHUNK = 16
VMEM = pl.BlockSpec(memory_space=pltpu.VMEM)


def exchange_masks(count):
    masks = []
    step = count // 2
    while step > 1:
        masks.append(step + 1)
        step //= 2
    return masks + [1]


def mask_at(place, masks):
    value = 0
    for bit, mask in enumerate(masks):
        if place >> bit & 1:
            value ^= mask
    return value


def place_of(value, masks):
    place = 0
    rest = value & 1
    for bit, mask in enumerate(masks[:-1]):
        taken = lax.shift_right_logical(value, mask.bit_length() - 1) & 1
        place = place + taken * (1 << bit)
        rest = rest ^ taken
    return place + rest * (1 << (len(masks) - 1))


def high_low(value):
    high = value.astype(jnp.bfloat16).astype(jnp.float32)
    return high, value - high


def dot_nt(left, right):
    return lax.dot_general(left, right, (((1,), (1,)), ((), ())), preferred_element_type=jnp.float32)


def cross(a, b):
    return (a[1] * b[2] - a[2] * b[1], a[2] * b[0] - a[0] * b[2], a[0] * b[1] - a[1] * b[0])


def pair_terms(point, normal, moment, first, segment, turn, span, span_core, scale, want_span):
    rel = tuple(p - e for p, e in zip(point, first))
    cross_n = (moment[0] * segment[0] + moment[1] * segment[1] + moment[2] * segment[2]) - (
        normal[0] * turn[0] + normal[1] * turn[1] + normal[2] * turn[2]
    )
    dist_sq = rel[0] * rel[0] + rel[1] * rel[1] + rel[2] * rel[2]
    along = segment[0] * rel[0] + segment[1] * rel[1] + segment[2] * rel[2]
    other = along - span
    second_sq = dist_sq - along - other
    inv_first = lax.rsqrt(dist_sq)
    inv_second = lax.rsqrt(second_sq)
    inv_den = 1.0 / ((span * dist_sq + span_core) - along * along)
    part_first = along * inv_first
    part_second = other * inv_second
    line = part_first - part_second
    scaled = scale * inv_den
    by_normal = scaled * line
    by_line = scaled * cross_n
    by_den = (by_normal * cross_n) * inv_den
    by_den2 = by_den + by_den
    cube_first = part_first * (inv_first * inv_first)
    cube_second = part_second * (inv_second * inv_second)
    by_dist2 = by_line * (cube_second - cube_first) - by_den2 * span
    by_along = by_line * ((inv_first - inv_second) - cube_second) + by_den2 * along
    if not want_span:
        return rel, by_normal, by_dist2, by_along
    by_span2 = by_line * ((inv_second + inv_second) + cube_second) - by_den2 * (dist_sq + core_term)
    return rel, by_normal, by_dist2, by_along, by_span2


def segment_terms(first, second):
    segment = tuple(b - a for a, b in zip(first, second))
    span = segment[0] * segment[0] + segment[1] * segment[1] + segment[2] * segment[2]
    return segment, cross(segment, first), span, core_term * span + core_term


def pack_kernel(own_seg, points_ref, normals_ref, left_ref, vertices_ref, connect_ref, right_ref, weights_ref, out_ref):
    base = lax.axis_index("src") * own_seg
    row8 = lax.broadcasted_iota(jnp.int32, (8, LANES), 0)
    weight = jnp.zeros((8, LANES), jnp.float32)
    for mode in range(8):
        weight = jnp.where(row8 == mode, weights_ref[mode], weight)
    weighted = right_ref[...] * (weight * inverse_four_pi)
    high, rest = high_low(weighted)
    middle, low = high_low(rest)
    parts = jnp.concatenate([high, middle, low, jnp.zeros_like(low)], 0).astype(jnp.bfloat16)
    local = connect_ref[0:1, :] - base
    hit = lax.broadcasted_iota(jnp.int32, (LANES, LANES), 0) == local
    folded = dot_nt(parts, hit.astype(jnp.float32).astype(jnp.bfloat16))
    folded = folded[0:8] + (folded[8:16] + folded[16:24])
    out_ref[0:8, :] = left_ref[...]
    out_ref[8:10, :] = points_ref[0:2, :]
    out_ref[10:11, :] = 0.5 + 0.2 * points_ref[2:3, :]
    out_ref[11:14, :] = normals_ref[...]
    out_ref[14:16, :] = jnp.zeros((2, LANES), jnp.float32)
    out_ref[16:24, :] = folded
    out_ref[16:18, own_seg : 2 * own_seg] = vertices_ref[0:2, :]
    out_ref[18:19, own_seg : 2 * own_seg] = 0.2 * vertices_ref[2:3, :]


def pair_kernel(count, own_seg, data_ref, rcv_out, vert_out, seg_ref, rec_ref, scale1_ref, scale2_ref, total_ref):
    masks = exchange_masks(count)
    tiles = count // 2
    me = lax.axis_index("src")
    lane = lax.broadcasted_iota(jnp.int32, (1, LANES), 1)
    low_half = lane < own_seg

    def device_block(device):
        return data_ref[place_of(device ^ me, masks), 16:24, :]

    folded = []
    for tile in range(tiles):
        block_a, block_b = data_ref[tile, 16:24, :], data_ref[tile + tiles, 16:24, :]
        after_a = device_block(((me ^ mask_at(tile, masks)) + 1) & (count - 1))
        after_b = device_block(((me ^ mask_at(tile + tiles, masks)) + 1) & (count - 1))
        folded.append(jnp.where(low_half, block_a, pltpu.roll(block_b, own_seg, 1)))
        first = jnp.where(low_half, pltpu.roll(block_a, own_seg, 1), block_b)
        second = jnp.where(
            lane < own_seg - 1,
            pltpu.roll(block_a, own_seg - 1, 1),
            jnp.where(
                low_half,
                pltpu.roll(after_a, LANES - 1, 1),
                jnp.where(lane < LANES - 1, pltpu.roll(block_b, LANES - 1, 1), pltpu.roll(after_b, own_seg - 1, 1)),
            ),
        )
        for axis in range(3):
            seg_ref[axis, tile : tile + 1, :] = first[axis : axis + 1]
            seg_ref[3 + axis, tile : tile + 1, :] = second[axis : axis + 1]
    first = tuple(seg_ref[axis] for axis in range(3))
    segment, turn, span, span_core = segment_terms(first, tuple(seg_ref[3 + axis] for axis in range(3)))
    for axis in range(3):
        seg_ref[3 + axis] = segment[axis]
        seg_ref[6 + axis] = turn[axis]
    seg_ref[9] = span
    seg_ref[10] = span_core

    point = tuple(data_ref[:, 8 + axis, :] for axis in range(3))
    normal = tuple(data_ref[:, 11 + axis, :] for axis in range(3))
    moment = cross(point, normal)
    for axis in range(3):
        rec_ref[axis] = point[axis]
        rec_ref[3 + axis] = normal[axis]
        rec_ref[6 + axis] = moment[axis]

    def stack_hhll(rows):
        high, low = high_low(rows)
        return jnp.transpose(jnp.concatenate([high, high, low, low], 0)).astype(jnp.bfloat16)

    def stack_hlhl(rows):
        high, low = high_low(rows)
        both = jnp.concatenate([high, low], 0).astype(jnp.bfloat16)
        return jnp.concatenate([both, both], 0)

    left_own = stack_hhll(data_ref[0, 0:8, :])
    seg_own = stack_hhll(data_ref[0, 16:24, :])[0:own_seg]
    scale1_ref[...] = jnp.dot(
        left_own, stack_hlhl(jnp.concatenate(folded, 1)), preferred_element_type=jnp.float32)
    scale2_ref[...] = jnp.dot(
        seg_own, stack_hlhl(jnp.concatenate([data_ref[b, 0:8, :] for b in range(count)], 1)),
        preferred_element_type=jnp.float32)

    own_p = tuple(rec_ref[axis, 0:1, :] for axis in range(3))
    own_n = tuple(rec_ref[3 + axis, 0:1, :] for axis in range(3))
    own_m = tuple(rec_ref[6 + axis, 0:1, :] for axis in range(3))
    pad = jnp.zeros((7, LANES), jnp.float32)
    total_ref[...] = jnp.transpose(jnp.concatenate([*own_p, *own_n, *own_m, pad], 0))

    def gather_totals(sums, start):
        packed = jnp.zeros((CHUNK, 16), jnp.float32)
        column = lax.broadcasted_iota(jnp.int32, (CHUNK, 16), 1)
        for index, value in enumerate(sums):
            packed = jnp.where(column == index, jnp.sum(value, axis=1, keepdims=True), packed)
        total_ref[pl.ds(start, CHUNK), :] = packed

    def first_chunk(chunk, carry):
        start = pl.multiple_of(chunk * CHUNK, CHUNK)
        cols = total_ref[pl.ds(start, CHUNK), :]
        col = [jnp.broadcast_to(cols[:, k : k + 1], (CHUNK, LANES)) for k in range(9)]
        sums = [jnp.zeros((CHUNK, LANES), jnp.float32) for _ in range(9)]
        for tile in range(tiles):
            row = [seg_ref[k, tile : tile + 1, :] for k in range(11)]
            scale = scale1_ref[pl.ds(start, CHUNK), tile * LANES : (tile + 1) * LANES]
            rel, by_normal, by_dist2, by_along = pair_terms(
                col[0:3], col[3:6], col[6:9], row[0:3], row[3:6], row[6:9], row[9], row[10], scale, False)
            for axis in range(3):
                sums[axis] += by_normal * row[3 + axis]
                sums[3 + axis] += by_normal * row[6 + axis]
                sums[6 + axis] += by_dist2 * rel[axis] + by_along * row[3 + axis]
        gather_totals(sums, start)
        return carry

    lax.fori_loop(0, LANES // CHUNK, first_chunk, 0)
    totals = jnp.transpose(total_ref[...])
    sum_s = tuple(totals[axis : axis + 1] for axis in range(3))
    by_point = tuple(
        a + totals[6 + axis : 7 + axis] for axis, a in enumerate(cross(own_n, sum_s)))
    by_norm = tuple(
        a - totals[3 + axis : 4 + axis] for axis, a in enumerate(cross(sum_s, own_p)))
    rcv_out[0:1, :] = by_point[0]
    rcv_out[1:2, :] = by_point[1]
    rcv_out[2:3, :] = 0.2 * by_point[2]
    for axis in range(3):
        rcv_out[3 + axis : 4 + axis, :] = by_norm[axis]

    own_rows = [seg_ref[k, 0:1, :] for k in range(11)]
    total_ref[...] = jnp.transpose(jnp.concatenate(own_rows + [pad[0:5]], 0))

    def second_chunk(chunk, carry):
        start = pl.multiple_of(chunk * CHUNK, CHUNK)
        cols = total_ref[pl.ds(start, CHUNK), :]
        col = [jnp.broadcast_to(cols[:, k : k + 1], (CHUNK, LANES)) for k in range(11)]
        sums = [jnp.zeros((CHUNK, LANES), jnp.float32) for _ in range(11)]
        for block in range(count):
            row = [rec_ref[k, block : block + 1, :] for k in range(9)]
            scale = scale2_ref[pl.ds(start, CHUNK), block * LANES : (block + 1) * LANES]
            rel, by_normal, by_dist2, by_along, by_span2 = pair_terms(
                row[0:3], row[3:6], row[6:9], col[0:3], col[3:6], col[6:9], col[9], col[10], scale, True)
            for axis in range(3):
                sums[axis] += by_normal * row[3 + axis]
                sums[3 + axis] += by_normal * row[6 + axis] + by_along * rel[axis]
                sums[6 + axis] += by_dist2 * rel[axis]
            sums[9] += by_along
            sums[10] += by_span2
        gather_totals(sums, start)
        return carry

    lax.fori_loop(0, own_seg // CHUNK, second_chunk, 0)
    totals = jnp.transpose(total_ref[...])
    sum_n = tuple(totals[axis : axis + 1] for axis in range(3))
    own_e, own_s = own_rows[0:3], own_rows[3:6]
    turned, swept = cross(own_e, sum_n), cross(sum_n, own_s)

    before = device_block((me + count - 1) & (count - 1))
    here = data_ref[0, 16:24, :]
    edge_e = tuple(before[axis : axis + 1, LANES - 1 :] for axis in range(3))
    edge_e2 = tuple(here[axis : axis + 1, own_seg : own_seg + 1] for axis in range(3))
    edge_w = jnp.where(me == 0, 0.0, before[:, own_seg - 1 : own_seg])
    edge_s, edge_t, edge_span, edge_core = segment_terms(edge_e, edge_e2)
    scale = jnp.zeros((count, LANES), jnp.float32)
    for mode in range(8):
        scale += edge_w[mode : mode + 1] * data_ref[:, mode, :]
    point = tuple(rec_ref[axis] for axis in range(3))
    normal = tuple(rec_ref[3 + axis] for axis in range(3))
    moment = tuple(rec_ref[6 + axis] for axis in range(3))
    rel, by_normal, _, by_along, by_span2 = pair_terms(
        point, normal, moment, edge_e, edge_s, edge_t, edge_span, edge_core, scale, True)
    swung = cross(rel, normal)
    for axis in range(3):
        edge = jnp.sum(by_normal * swung[axis] + by_along * rel[axis] + by_span2 * edge_s[axis])
        by_second = totals[3 + axis : 4 + axis] - turned[axis] + own_s[axis] * totals[10:11]
        by_rel = swept[axis] + totals[6 + axis : 7 + axis] + own_s[axis] * totals[9:10]
        result = jnp.where(lane == 0, edge, pltpu.roll(by_second, 1, 1)) - (by_second + by_rel)
        if axis == 2:
            result = 0.2 * result
        vert_out[axis : axis + 1, :] = result[:, 0:own_seg]


def on_device(rcv_points, rcv_normals, left_modes, vertices, connect, right_modes, mode_weights):
    count = lax.axis_size("src")
    own_seg = vertices.shape[1]
    tiles = count // 2
    value = pl.pallas_call(
        functools.partial(pack_kernel, own_seg),
        out_shape=jax.ShapeDtypeStruct((ROWS, LANES), jnp.float32),
        in_specs=[VMEM] * 6 + [pl.BlockSpec(memory_space=pltpu.SMEM)],
        out_specs=VMEM,
    )(rcv_points, rcv_normals, left_modes, vertices, connect, right_modes, mode_weights)[None]
    for mask in exchange_masks(count):
        other = lax.ppermute(value, "src", [(s, s ^ mask) for s in range(count)])
        value = jnp.concatenate([value, other], 0)
    return pl.pallas_call(
        functools.partial(pair_kernel, count, own_seg),
        out_shape=(
            jax.ShapeDtypeStruct((6, LANES), jnp.float32),
            jax.ShapeDtypeStruct((3, own_seg), jnp.float32),
        ),
        in_specs=[VMEM],
        out_specs=(VMEM, VMEM),
        scratch_shapes=[
            pltpu.VMEM((11, tiles, LANES), jnp.float32),
            pltpu.VMEM((9, count, LANES), jnp.float32),
            pltpu.VMEM((LANES, tiles * LANES), jnp.float32),
            pltpu.VMEM((own_seg, count * LANES), jnp.float32),
            pltpu.VMEM((LANES, 16), jnp.float32),
        ],
        compiler_params=pltpu.CompilerParams(vmem_limit_bytes=24 << 20),
    )(value)


def solution(mesh):
    split = P(None, ("group", "src"))
    return jax.shard_map(
        on_device, mesh=mesh, in_specs=(split,) * 6 + (P("group"),), out_specs=(split, split), check_vma=False
    )
```

```python
import functools
import math

import jax
import jax.numpy as jnp
from jax import lax
from jax.experimental import pallas as pl
from jax.experimental.pallas import tpu as pltpu
from jax.sharding import PartitionSpec as P

core_term = 0.05
inverse_four_pi = 0.25 / math.pi

LANES = 128
ROWS = 24
CHUNK = 32
VMEM = pl.BlockSpec(memory_space=pltpu.VMEM)


def exchange_masks(count):
    masks = []
    step = count // 2
    while step > 1:
        masks.append(step + 1)
        step //= 2
    return masks + [1]


def mask_at(place, masks):
    value = 0
    for bit, mask in enumerate(masks):
        if place >> bit & 1:
            value ^= mask
    return value


def place_of(value, masks):
    place = 0
    rest = value & 1
    for bit, mask in enumerate(masks[:-1]):
        taken = lax.shift_right_logical(value, mask.bit_length() - 1) & 1
        place = place + taken * (1 << bit)
        rest = rest ^ taken
    return place + rest * (1 << (len(masks) - 1))


def high_low(value):
    high = value.astype(jnp.bfloat16).astype(jnp.float32)
    return high, value - high


def dot_nt(left, right):
    return lax.dot_general(left, right, (((1,), (1,)), ((), ())), preferred_element_type=jnp.float32)


def cross(a, b):
    return (a[1] * b[2] - a[2] * b[1], a[2] * b[0] - a[0] * b[2], a[0] * b[1] - a[1] * b[0])


def pair_terms(point, normal, moment, first, segment, turn, span, span_core, scale, want_span):
    rel = tuple(p - e for p, e in zip(point, first))
    cross_n = (moment[0] * segment[0] + moment[1] * segment[1] + moment[2] * segment[2]) - (
        normal[0] * turn[0] + normal[1] * turn[1] + normal[2] * turn[2]
    )
    dist_sq = rel[0] * rel[0] + rel[1] * rel[1] + rel[2] * rel[2]
    along = segment[0] * rel[0] + segment[1] * rel[1] + segment[2] * rel[2]
    other = along - span
    second_sq = dist_sq - along - other
    inv_first = lax.rsqrt(dist_sq)
    inv_second = lax.rsqrt(second_sq)
    inv_den = 1.0 / ((span * dist_sq + span_core) - along * along)
    part_first = along * inv_first
    part_second = other * inv_second
    line = part_first - part_second
    scaled = scale * inv_den
    by_normal = scaled * line
    by_line = scaled * cross_n
    by_den = (by_normal * cross_n) * inv_den
    by_den2 = by_den + by_den
    cube_first = part_first * (inv_first * inv_first)
    cube_second = part_second * (inv_second * inv_second)
    by_dist2 = by_line * (cube_second - cube_first) - by_den2 * span
    by_along = by_line * ((inv_first - inv_second) - cube_second) + by_den2 * along
    if not want_span:
        return rel, by_normal, by_dist2, by_along
    by_span2 = by_line * ((inv_second + inv_second) + cube_second) - by_den2 * (dist_sq + core_term)
    return rel, by_normal, by_dist2, by_along, by_span2


def segment_terms(first, second):
    segment = tuple(b - a for a, b in zip(first, second))
    span = segment[0] * segment[0] + segment[1] * segment[1] + segment[2] * segment[2]
    return segment, cross(segment, first), span, core_term * span + core_term


def pack_kernel(own_seg, points_ref, normals_ref, left_ref, vertices_ref, connect_ref, right_ref, weights_ref, out_ref):
    base = lax.axis_index("src") * own_seg
    row8 = lax.broadcasted_iota(jnp.int32, (8, LANES), 0)
    weight = jnp.zeros((8, LANES), jnp.float32)
    for mode in range(8):
        weight = jnp.where(row8 == mode, weights_ref[mode], weight)
    weighted = right_ref[...] * (weight * inverse_four_pi)
    high, rest = high_low(weighted)
    middle, low = high_low(rest)
    parts = jnp.concatenate([high, middle, low, jnp.zeros_like(low)], 0).astype(jnp.bfloat16)
    local = connect_ref[0:1, :] - base
    hit = lax.broadcasted_iota(jnp.int32, (LANES, LANES), 0) == local
    folded = dot_nt(parts, hit.astype(jnp.float32).astype(jnp.bfloat16))
    folded = folded[0:8] + (folded[8:16] + folded[16:24])
    out_ref[0:8, :] = left_ref[...]
    out_ref[8:10, :] = points_ref[0:2, :]
    out_ref[10:11, :] = 0.5 + 0.2 * points_ref[2:3, :]
    out_ref[11:14, :] = normals_ref[...]
    out_ref[14:16, :] = jnp.zeros((2, LANES), jnp.float32)
    out_ref[16:24, :] = folded
    out_ref[16:18, own_seg : 2 * own_seg] = vertices_ref[0:2, :]
    out_ref[18:19, own_seg : 2 * own_seg] = 0.2 * vertices_ref[2:3, :]


def pair_kernel(count, own_seg, data_ref, rcv_out, vert_out, seg_ref, rec_ref, scale1_ref, scale2_ref, total_ref):
    masks = exchange_masks(count)
    tiles = count // 2
    me = lax.axis_index("src")
    lane = lax.broadcasted_iota(jnp.int32, (1, LANES), 1)
    low_half = lane < own_seg

    def device_block(device):
        return data_ref[place_of(device ^ me, masks), 16:24, :]

    folded = []
    for tile in range(tiles):
        block_a, block_b = data_ref[tile, 16:24, :], data_ref[tile + tiles, 16:24, :]
        after_a = device_block(((me ^ mask_at(tile, masks)) + 1) & (count - 1))
        after_b = device_block(((me ^ mask_at(tile + tiles, masks)) + 1) & (count - 1))
        folded.append(jnp.where(low_half, block_a, pltpu.roll(block_b, own_seg, 1)))
        first = jnp.where(low_half, pltpu.roll(block_a, own_seg, 1), block_b)
        second = jnp.where(
            lane < own_seg - 1,
            pltpu.roll(block_a, own_seg - 1, 1),
            jnp.where(
                low_half,
                pltpu.roll(after_a, LANES - 1, 1),
                jnp.where(lane < LANES - 1, pltpu.roll(block_b, LANES - 1, 1), pltpu.roll(after_b, own_seg - 1, 1)),
            ),
        )
        for axis in range(3):
            seg_ref[axis, tile : tile + 1, :] = first[axis : axis + 1]
            seg_ref[3 + axis, tile : tile + 1, :] = second[axis : axis + 1]
    first = tuple(seg_ref[axis] for axis in range(3))
    segment, turn, span, span_core = segment_terms(first, tuple(seg_ref[3 + axis] for axis in range(3)))
    for axis in range(3):
        seg_ref[3 + axis] = segment[axis]
        seg_ref[6 + axis] = turn[axis]
    seg_ref[9] = span
    seg_ref[10] = span_core

    point = tuple(data_ref[:, 8 + axis, :] for axis in range(3))
    normal = tuple(data_ref[:, 11 + axis, :] for axis in range(3))
    moment = cross(point, normal)
    for axis in range(3):
        rec_ref[axis] = point[axis]
        rec_ref[3 + axis] = normal[axis]
        rec_ref[6 + axis] = moment[axis]

    def stack_hhll(rows):
        high, low = high_low(rows)
        return jnp.transpose(jnp.concatenate([high, high, low, low], 0)).astype(jnp.bfloat16)

    def stack_hlhl(rows):
        high, low = high_low(rows)
        both = jnp.concatenate([high, low], 0).astype(jnp.bfloat16)
        return jnp.concatenate([both, both], 0)

    left_own = stack_hhll(data_ref[0, 0:8, :])
    seg_own = stack_hhll(data_ref[0, 16:24, :])[0:own_seg]
    scale1_ref[...] = jnp.dot(
        left_own, stack_hlhl(jnp.concatenate(folded, 1)), preferred_element_type=jnp.float32)
    scale2_ref[...] = jnp.dot(
        seg_own, stack_hlhl(jnp.concatenate([data_ref[b, 0:8, :] for b in range(count)], 1)),
        preferred_element_type=jnp.float32)

    own_p = tuple(rec_ref[axis, 0:1, :] for axis in range(3))
    own_n = tuple(rec_ref[3 + axis, 0:1, :] for axis in range(3))
    own_m = tuple(rec_ref[6 + axis, 0:1, :] for axis in range(3))
    pad = jnp.zeros((7, LANES), jnp.float32)
    total_ref[...] = jnp.transpose(jnp.concatenate([*own_p, *own_n, *own_m, pad], 0))

    def gather_totals(sums, start):
        packed = jnp.zeros((CHUNK, 16), jnp.float32)
        column = lax.broadcasted_iota(jnp.int32, (CHUNK, 16), 1)
        for index, value in enumerate(sums):
            packed = jnp.where(column == index, jnp.sum(value, axis=1, keepdims=True), packed)
        total_ref[pl.ds(start, CHUNK), :] = packed

    def first_chunk(chunk, carry):
        start = pl.multiple_of(chunk * CHUNK, CHUNK)
        cols = total_ref[pl.ds(start, CHUNK), :]
        col = [jnp.broadcast_to(cols[:, k : k + 1], (CHUNK, LANES)) for k in range(9)]
        sums = [jnp.zeros((CHUNK, LANES), jnp.float32) for _ in range(9)]
        for tile in range(tiles):
            row = [seg_ref[k, tile : tile + 1, :] for k in range(11)]
            scale = scale1_ref[pl.ds(start, CHUNK), tile * LANES : (tile + 1) * LANES]
            rel, by_normal, by_dist2, by_along = pair_terms(
                col[0:3], col[3:6], col[6:9], row[0:3], row[3:6], row[6:9], row[9], row[10], scale, False)
            for axis in range(3):
                sums[axis] += by_normal * row[3 + axis]
                sums[3 + axis] += by_normal * row[6 + axis]
                sums[6 + axis] += by_dist2 * rel[axis] + by_along * row[3 + axis]
        gather_totals(sums, start)
        return carry

    lax.fori_loop(0, LANES // CHUNK, first_chunk, 0, unroll=True)
    totals = jnp.transpose(total_ref[...])
    sum_s = tuple(totals[axis : axis + 1] for axis in range(3))
    by_point = tuple(
        a + totals[6 + axis : 7 + axis] for axis, a in enumerate(cross(own_n, sum_s)))
    by_norm = tuple(
        a - totals[3 + axis : 4 + axis] for axis, a in enumerate(cross(sum_s, own_p)))
    rcv_out[0:1, :] = by_point[0]
    rcv_out[1:2, :] = by_point[1]
    rcv_out[2:3, :] = 0.2 * by_point[2]
    for axis in range(3):
        rcv_out[3 + axis : 4 + axis, :] = by_norm[axis]

    own_rows = [seg_ref[k, 0:1, :] for k in range(11)]
    total_ref[...] = jnp.transpose(jnp.concatenate(own_rows + [pad[0:5]], 0))

    def second_chunk(chunk, carry):
        start = pl.multiple_of(chunk * CHUNK, CHUNK)
        cols = total_ref[pl.ds(start, CHUNK), :]
        col = [jnp.broadcast_to(cols[:, k : k + 1], (CHUNK, LANES)) for k in range(11)]
        sums = [jnp.zeros((CHUNK, LANES), jnp.float32) for _ in range(11)]
        for block in range(count):
            row = [rec_ref[k, block : block + 1, :] for k in range(9)]
            scale = scale2_ref[pl.ds(start, CHUNK), block * LANES : (block + 1) * LANES]
            rel, by_normal, by_dist2, by_along, by_span2 = pair_terms(
                row[0:3], row[3:6], row[6:9], col[0:3], col[3:6], col[6:9], col[9], col[10], scale, True)
            for axis in range(3):
                sums[axis] += by_normal * row[3 + axis]
                sums[3 + axis] += by_normal * row[6 + axis] + by_along * rel[axis]
                sums[6 + axis] += by_dist2 * rel[axis]
            sums[9] += by_along
            sums[10] += by_span2
        gather_totals(sums, start)
        return carry

    lax.fori_loop(0, own_seg // CHUNK, second_chunk, 0, unroll=True)
    totals = jnp.transpose(total_ref[...])
    sum_n = tuple(totals[axis : axis + 1] for axis in range(3))
    own_e, own_s = own_rows[0:3], own_rows[3:6]
    turned, swept = cross(own_e, sum_n), cross(sum_n, own_s)

    before = device_block((me + count - 1) & (count - 1))
    here = data_ref[0, 16:24, :]
    edge_e = tuple(before[axis : axis + 1, LANES - 1 :] for axis in range(3))
    edge_e2 = tuple(here[axis : axis + 1, own_seg : own_seg + 1] for axis in range(3))
    edge_w = jnp.where(me == 0, 0.0, before[:, own_seg - 1 : own_seg])
    edge_s, edge_t, edge_span, edge_core = segment_terms(edge_e, edge_e2)
    scale = jnp.zeros((count, LANES), jnp.float32)
    for mode in range(8):
        scale += edge_w[mode : mode + 1] * data_ref[:, mode, :]
    point = tuple(rec_ref[axis] for axis in range(3))
    normal = tuple(rec_ref[3 + axis] for axis in range(3))
    moment = tuple(rec_ref[6 + axis] for axis in range(3))
    rel, by_normal, _, by_along, by_span2 = pair_terms(
        point, normal, moment, edge_e, edge_s, edge_t, edge_span, edge_core, scale, True)
    swung = cross(rel, normal)
    for axis in range(3):
        edge = jnp.sum(by_normal * swung[axis] + by_along * rel[axis] + by_span2 * edge_s[axis])
        by_second = totals[3 + axis : 4 + axis] - turned[axis] + own_s[axis] * totals[10:11]
        by_rel = swept[axis] + totals[6 + axis : 7 + axis] + own_s[axis] * totals[9:10]
        result = jnp.where(lane == 0, edge, pltpu.roll(by_second, 1, 1)) - (by_second + by_rel)
        if axis == 2:
            result = 0.2 * result
        vert_out[axis : axis + 1, :] = result[:, 0:own_seg]


def on_device(rcv_points, rcv_normals, left_modes, vertices, connect, right_modes, mode_weights):
    count = lax.axis_size("src")
    own_seg = vertices.shape[1]
    tiles = count // 2
    value = pl.pallas_call(
        functools.partial(pack_kernel, own_seg),
        out_shape=pltpu.VMEM((ROWS, LANES), jnp.float32),
        in_specs=[VMEM] * 6 + [pl.BlockSpec(memory_space=pltpu.SMEM)],
        out_specs=VMEM,
    )(rcv_points, rcv_normals, left_modes, vertices, connect, right_modes, mode_weights)[None]
    for mask in exchange_masks(count):
        other = lax.ppermute(value, "src", [(s, s ^ mask) for s in range(count)])
        value = jnp.concatenate([value, other], 0)
    return pl.pallas_call(
        functools.partial(pair_kernel, count, own_seg),
        out_shape=(
            jax.ShapeDtypeStruct((6, LANES), jnp.float32),
            jax.ShapeDtypeStruct((3, own_seg), jnp.float32),
        ),
        in_specs=[VMEM],
        out_specs=(VMEM, VMEM),
        scratch_shapes=[
            pltpu.VMEM((11, tiles, LANES), jnp.float32),
            pltpu.VMEM((9, count, LANES), jnp.float32),
            pltpu.VMEM((LANES, tiles * LANES), jnp.float32),
            pltpu.VMEM((own_seg, count * LANES), jnp.float32),
            pltpu.VMEM((LANES, 16), jnp.float32),
        ],
        compiler_params=pltpu.CompilerParams(vmem_limit_bytes=24 << 20),
    )(value)


def solution(mesh):
    split = P(None, ("group", "src"))
    return jax.shard_map(
        on_device, mesh=mesh, in_specs=(split,) * 6 + (P("group"),), out_specs=(split, split), check_vma=False
    )
```

```python
import functools
import math

import jax
import jax.numpy as jnp
from jax import lax
from jax.experimental import pallas as pl
from jax.experimental.pallas import tpu as pltpu
from jax.sharding import PartitionSpec as P

core_term = 0.05
inverse_four_pi = 0.25 / math.pi

LANES = 128
ROWS = 24
CHUNK = 32
VMEM = pl.BlockSpec(memory_space=pltpu.VMEM)


def exchange_masks(count):
    masks = []
    step = count // 2
    while step > 1:
        masks.append(step + 1)
        step //= 2
    return masks + [1]


def mask_at(place, masks):
    value = 0
    for bit, mask in enumerate(masks):
        if place >> bit & 1:
            value ^= mask
    return value


def place_of(value, masks):
    place = 0
    rest = value & 1
    for bit, mask in enumerate(masks[:-1]):
        taken = lax.shift_right_logical(value, mask.bit_length() - 1) & 1
        place = place + taken * (1 << bit)
        rest = rest ^ taken
    return place + rest * (1 << (len(masks) - 1))


def high_low(value):
    high = value.astype(jnp.bfloat16).astype(jnp.float32)
    return high, value - high


def dot_nt(left, right):
    return lax.dot_general(left, right, (((1,), (1,)), ((), ())), preferred_element_type=jnp.float32)


def cross(a, b):
    return (a[1] * b[2] - a[2] * b[1], a[2] * b[0] - a[0] * b[2], a[0] * b[1] - a[1] * b[0])


def pair_terms(point, normal, moment, first, segment, turn, span, span_core, scale, want_span):
    rel = tuple(p - e for p, e in zip(point, first))
    cross_n = (moment[0] * segment[0] + moment[1] * segment[1] + moment[2] * segment[2]) - (
        normal[0] * turn[0] + normal[1] * turn[1] + normal[2] * turn[2]
    )
    dist_sq = rel[0] * rel[0] + rel[1] * rel[1] + rel[2] * rel[2]
    along = segment[0] * rel[0] + segment[1] * rel[1] + segment[2] * rel[2]
    other = along - span
    second_sq = dist_sq - along - other
    inv_first = lax.rsqrt(dist_sq)
    inv_second = lax.rsqrt(second_sq)
    inv_den = 1.0 / ((span * dist_sq + span_core) - along * along)
    part_first = along * inv_first
    part_second = other * inv_second
    line = part_first - part_second
    scaled = scale * inv_den
    by_normal = scaled * line
    by_line = scaled * cross_n
    by_den = (by_normal * cross_n) * inv_den
    by_den2 = by_den + by_den
    cube_first = part_first * (inv_first * inv_first)
    cube_second = part_second * (inv_second * inv_second)
    by_dist2 = by_line * (cube_second - cube_first) - by_den2 * span
    by_along = by_line * ((inv_first - inv_second) - cube_second) + by_den2 * along
    if not want_span:
        return rel, by_normal, by_dist2, by_along
    by_span2 = by_line * ((inv_second + inv_second) + cube_second) - by_den2 * (dist_sq + core_term)
    return rel, by_normal, by_dist2, by_along, by_span2


def segment_terms(first, second):
    segment = tuple(b - a for a, b in zip(first, second))
    span = segment[0] * segment[0] + segment[1] * segment[1] + segment[2] * segment[2]
    return segment, cross(segment, first), span, core_term * span + core_term


def pack_kernel(own_seg, points_ref, normals_ref, left_ref, vertices_ref, connect_ref, right_ref, weights_ref, out_ref):
    base = lax.axis_index("src") * own_seg
    row8 = lax.broadcasted_iota(jnp.int32, (8, LANES), 0)
    weight = jnp.zeros((8, LANES), jnp.float32)
    for mode in range(8):
        weight = jnp.where(row8 == mode, weights_ref[mode], weight)
    weighted = right_ref[...] * (weight * inverse_four_pi)
    high, rest = high_low(weighted)
    middle, low = high_low(rest)
    parts = jnp.concatenate([high, middle, low, jnp.zeros_like(low)], 0).astype(jnp.bfloat16)
    local = connect_ref[0:1, :] - base
    hit = lax.broadcasted_iota(jnp.int32, (LANES, LANES), 0) == local
    folded = dot_nt(parts, hit.astype(jnp.float32).astype(jnp.bfloat16))
    folded = folded[0:8] + (folded[8:16] + folded[16:24])
    out_ref[0:8, :] = left_ref[...]
    out_ref[8:10, :] = points_ref[0:2, :]
    out_ref[10:11, :] = 0.5 + 0.2 * points_ref[2:3, :]
    out_ref[11:14, :] = normals_ref[...]
    out_ref[14:16, :] = jnp.zeros((2, LANES), jnp.float32)
    out_ref[16:24, :] = folded
    out_ref[16:18, own_seg : 2 * own_seg] = vertices_ref[0:2, :]
    out_ref[18:19, own_seg : 2 * own_seg] = 0.2 * vertices_ref[2:3, :]


def pair_sums(data_ref, begin, end, own_seg, scratch, old1, old2):
    seg_ref, rec_ref, scale1_ref, scale2_ref, total1_ref, total2_ref = scratch
    blocks = end - begin
    tiles = blocks // 2
    lane = lax.broadcasted_iota(jnp.int32, (1, LANES), 1)
    low_half = lane < own_seg
    at_edge = (lane == own_seg - 1) | (lane == 2 * own_seg - 1)

    folded = []
    for tile in range(tiles):
        block_a, block_b = data_ref[begin + 2 * tile, 16:24, :], data_ref[begin + 2 * tile + 1, 16:24, :]
        both = jnp.where(low_half, block_a, pltpu.roll(block_b, own_seg, 1))
        folded.append(jnp.where(at_edge, 0.0, both))
        first = jnp.where(low_half, pltpu.roll(block_a, own_seg, 1), block_b)
        second = jnp.where(at_edge, first, pltpu.roll(first, LANES - 1, 1))
        for axis in range(3):
            seg_ref[axis, tile : tile + 1, :] = first[axis : axis + 1]
            seg_ref[3 + axis, tile : tile + 1, :] = second[axis : axis + 1]
    first = tuple(seg_ref[axis] for axis in range(3))
    segment, turn, span, span_core = segment_terms(first, tuple(seg_ref[3 + axis] for axis in range(3)))
    for axis in range(3):
        seg_ref[3 + axis] = segment[axis]
        seg_ref[6 + axis] = turn[axis]
    seg_ref[9] = span
    seg_ref[10] = span_core

    point = tuple(data_ref[begin:end, 8 + axis, :] for axis in range(3))
    normal = tuple(data_ref[begin:end, 11 + axis, :] for axis in range(3))
    moment = cross(point, normal)
    for axis in range(3):
        rec_ref[axis] = point[axis]
        rec_ref[3 + axis] = normal[axis]
        rec_ref[6 + axis] = moment[axis]

    def stack_hhll(rows):
        high, low = high_low(rows)
        return jnp.transpose(jnp.concatenate([high, high, low, low], 0)).astype(jnp.bfloat16)

    def stack_hlhl(rows):
        high, low = high_low(rows)
        both = jnp.concatenate([high, low], 0).astype(jnp.bfloat16)
        return jnp.concatenate([both, both], 0)

    own_block = data_ref[0, 16:24, :]
    left_own = stack_hhll(data_ref[0, 0:8, :])
    seg_own = stack_hhll(jnp.where(at_edge, 0.0, own_block))[0:own_seg]
    scale1_ref[...] = jnp.dot(
        left_own, stack_hlhl(jnp.concatenate(folded, 1)), preferred_element_type=jnp.float32)
    scale2_ref[...] = jnp.dot(
        seg_own, stack_hlhl(jnp.concatenate([data_ref[b, 0:8, :] for b in range(begin, end)], 1)),
        preferred_element_type=jnp.float32)

    def columns(rows):
        pad = jnp.zeros((16 - len(rows), LANES), jnp.float32)
        return jnp.transpose(jnp.concatenate(list(rows) + [pad], 0))

    own_p, own_n, own_m = own_receivers(data_ref)
    own_e, own_s, own_t, own_span, own_core = own_segments(own_block, own_seg)
    cols1 = columns([*own_p, *own_n, *own_m])
    cols2 = columns([*own_e, *own_s, *own_t, own_span, own_core])

    def packed(sums):
        result = jnp.zeros((CHUNK, 16), jnp.float32)
        column = lax.broadcasted_iota(jnp.int32, (CHUNK, 16), 1)
        for index, value in enumerate(sums):
            result = jnp.where(column == index, jnp.sum(value, axis=1, keepdims=True), result)
        return result

    for start in range(0, LANES, CHUNK):
        cols = cols1[start : start + CHUNK]
        col = [jnp.broadcast_to(cols[:, k : k + 1], (CHUNK, LANES)) for k in range(9)]
        sums = [jnp.zeros((CHUNK, LANES), jnp.float32) for _ in range(9)]
        for tile in range(tiles):
            row = [seg_ref[k, tile : tile + 1, :] for k in range(11)]
            scale = scale1_ref[start : start + CHUNK, tile * LANES : (tile + 1) * LANES]
            rel, by_normal, by_dist2, by_along = pair_terms(
                col[0:3], col[3:6], col[6:9], row[0:3], row[3:6], row[6:9], row[9], row[10], scale, False)
            for axis in range(3):
                sums[axis] += by_normal * row[3 + axis]
                sums[3 + axis] += by_normal * row[6 + axis]
                sums[6 + axis] += by_dist2 * rel[axis] + by_along * row[3 + axis]
        total1_ref[start : start + CHUNK, :] = packed(sums)

    for start in range(0, own_seg, CHUNK):
        cols = cols2[start : start + CHUNK]
        col = [jnp.broadcast_to(cols[:, k : k + 1], (CHUNK, LANES)) for k in range(11)]
        sums = [jnp.zeros((CHUNK, LANES), jnp.float32) for _ in range(11)]
        for block in range(blocks):
            row = [rec_ref[k, block : block + 1, :] for k in range(9)]
            scale = scale2_ref[start : start + CHUNK, block * LANES : (block + 1) * LANES]
            rel, by_normal, by_dist2, by_along, by_span2 = pair_terms(
                row[0:3], row[3:6], row[6:9], col[0:3], col[3:6], col[6:9], col[9], col[10], scale, True)
            for axis in range(3):
                sums[axis] += by_normal * row[3 + axis]
                sums[3 + axis] += by_normal * row[6 + axis] + by_along * rel[axis]
                sums[6 + axis] += by_dist2 * rel[axis]
            sums[9] += by_along
            sums[10] += by_span2
        total2_ref[start : start + CHUNK, :] = packed(sums)
    total1, total2 = total1_ref[...], total2_ref[...]
    if old1 is not None:
        total1, total2 = total1 + old1[...], total2 + old2[...]
    return total1, total2


def own_receivers(data_ref):
    point = tuple(data_ref[0, 8 + axis : 9 + axis, :] for axis in range(3))
    normal = tuple(data_ref[0, 11 + axis : 12 + axis, :] for axis in range(3))
    return point, normal, cross(point, normal)


def own_segments(own_block, own_seg):
    lane = lax.broadcasted_iota(jnp.int32, (1, LANES), 1)
    first = pltpu.roll(own_block, own_seg, 1)
    second = jnp.where(lane == own_seg - 1, first, pltpu.roll(first, LANES - 1, 1))
    own_e = tuple(first[axis : axis + 1] for axis in range(3))
    segment, turn, span, span_core = segment_terms(own_e, tuple(second[axis : axis + 1] for axis in range(3)))
    return own_e, segment, turn, span, span_core


def early_kernel(begin, end, own_seg, *refs):
    data_ref, rest = refs[0], refs[1:]
    olds = rest[0:2] if begin else (None, None)
    rest = rest[2:] if begin else rest
    rest[0][...], rest[1][...] = pair_sums(data_ref, begin, end, own_seg, rest[2:], *olds)


def last_kernel(count, own_seg, data_ref, old1_ref, old2_ref, rcv_out, vert_out, after_ref, *scratch):
    masks = exchange_masks(count)
    me = lax.axis_index("src")
    lane = lax.broadcasted_iota(jnp.int32, (1, LANES), 1)

    def place(device):
        return place_of((device & (count - 1)) ^ me, masks)

    for block in range(count):
        after_ref[block] = data_ref[place((me ^ mask_at(block, masks)) + 1), 16:24, :]
    edge_e = tuple(data_ref[:, 16 + axis, 2 * own_seg - 1 : 2 * own_seg] for axis in range(3))
    edge_e2 = tuple(after_ref[:, axis, own_seg : own_seg + 1] for axis in range(3))
    edge_s, edge_t, edge_span, edge_core = segment_terms(edge_e, edge_e2)
    own_p, own_n, own_m = own_receivers(data_ref)
    scale = jnp.zeros((count, LANES), jnp.float32)
    for mode in range(8):
        scale += data_ref[:, 16 + mode, own_seg - 1 : own_seg] * data_ref[0, mode : mode + 1, :]
    rel, by_normal, by_dist2, by_along = pair_terms(
        own_p, own_n, own_m, edge_e, edge_s, edge_t, edge_span, edge_core, scale, False)

    def down(value):
        return jnp.sum(value, axis=0, keepdims=True)

    edge_sum_s = tuple(down(by_normal * edge_s[axis]) for axis in range(3))
    edge_sum_t = tuple(down(by_normal * edge_t[axis]) for axis in range(3))
    edge_sum_p = tuple(down(by_dist2 * rel[axis] + by_along * edge_s[axis]) for axis in range(3))

    point = tuple(data_ref[:, 8 + axis, :] for axis in range(3))
    normal = tuple(data_ref[:, 11 + axis, :] for axis in range(3))
    moment = cross(point, normal)
    own_block = data_ref[0, 16:24, :]
    before = data_ref[place(me + count - 1), 16:24, :]
    mine_last = tuple(own_block[axis : axis + 1, 2 * own_seg - 1 : 2 * own_seg] for axis in range(3))
    mine_next = tuple(after_ref[0, axis : axis + 1, own_seg : own_seg + 1] for axis in range(3))
    before_last = tuple(before[axis : axis + 1, 2 * own_seg - 1 : 2 * own_seg] for axis in range(3))
    mine_first = tuple(own_block[axis : axis + 1, own_seg : own_seg + 1] for axis in range(3))

    def edge_against_all(first, second, weight):
        segment, turn, span, span_core = segment_terms(first, second)
        scale = jnp.zeros((count, LANES), jnp.float32)
        for mode in range(8):
            scale += weight[mode : mode + 1] * data_ref[:, mode, :]
        rel, by_normal, by_dist2, by_along, by_span2 = pair_terms(
            point, normal, moment, first, segment, turn, span, span_core, scale, True)
        swung, swept = cross(rel, normal), cross(normal, segment)
        by_s = [by_normal * swung[k] + by_along * rel[k] + by_span2 * segment[k] for k in range(3)]
        by_r = [by_normal * swept[k] + by_dist2 * rel[k] + by_along * segment[k] for k in range(3)]
        return by_s, by_r

    by_s, by_r = edge_against_all(mine_last, mine_next, own_block[:, own_seg - 1 : own_seg])
    leaving = [-jnp.sum(by_s[axis] + by_r[axis]) for axis in range(3)]
    by_s, _ = edge_against_all(
        before_last, mine_first, jnp.where(me == 0, 0.0, before[:, own_seg - 1 : own_seg]))
    arriving = [jnp.sum(by_s[axis]) for axis in range(3)]

    total1, total2 = pair_sums(data_ref, count // 2, count, own_seg, scratch, old1_ref, old2_ref)
    totals = jnp.transpose(total1)
    sum_s = tuple(totals[axis : axis + 1] + edge_sum_s[axis] for axis in range(3))
    by_point, by_norm = cross(own_n, sum_s), cross(sum_s, own_p)
    for axis in range(3):
        value = by_point[axis] + (totals[6 + axis : 7 + axis] + edge_sum_p[axis])
        rcv_out[axis : axis + 1, :] = 0.2 * value if axis == 2 else value
        rcv_out[3 + axis : 4 + axis, :] = by_norm[axis] - (totals[3 + axis : 4 + axis] + edge_sum_t[axis])

    totals = jnp.transpose(total2)
    sum_n = tuple(totals[axis : axis + 1] for axis in range(3))
    own_e, own_s, _, _, _ = own_segments(own_block, own_seg)
    own_e = tuple(value[:, 0:own_seg] for value in own_e)
    own_s = tuple(value[:, 0:own_seg] for value in own_s)
    turned, swept = cross(own_e, sum_n), cross(sum_n, own_s)
    lane = lane[:, 0:own_seg]
    for axis in range(3):
        by_second = totals[3 + axis : 4 + axis] - turned[axis] + own_s[axis] * totals[10:11]
        by_rel = swept[axis] + totals[6 + axis : 7 + axis] + own_s[axis] * totals[9:10]
        shifted = jnp.concatenate([by_second[:, own_seg - 1 :], by_second[:, : own_seg - 1]], 1)
        result = jnp.where(lane == 0, arriving[axis], shifted) - (by_second + by_rel)
        result = result + jnp.where(lane == own_seg - 1, leaving[axis], 0.0)
        vert_out[axis : axis + 1, :] = 0.2 * result if axis == 2 else result


def pair_scratch(blocks, own_seg):
    return [
        pltpu.VMEM((11, blocks // 2, LANES), jnp.float32),
        pltpu.VMEM((9, blocks, LANES), jnp.float32),
        pltpu.VMEM((LANES, blocks // 2 * LANES), jnp.float32),
        pltpu.VMEM((own_seg, blocks * LANES), jnp.float32),
        pltpu.VMEM((LANES, 16), jnp.float32),
        pltpu.VMEM((own_seg, 16), jnp.float32),
    ]


def pair_cost(blocks, own_seg):
    pairs = 2 * blocks * own_seg * LANES
    return pl.CostEstimate(flops=100 * pairs, bytes_accessed=blocks * ROWS * LANES * 4, transcendentals=3 * pairs)


def on_device(rcv_points, rcv_normals, left_modes, vertices, connect, right_modes, mode_weights):
    count = lax.axis_size("src")
    own_seg = vertices.shape[1]
    value = pl.pallas_call(
        functools.partial(pack_kernel, own_seg),
        out_shape=pltpu.VMEM((ROWS, LANES), jnp.float32),
        in_specs=[VMEM] * 6 + [pl.BlockSpec(memory_space=pltpu.SMEM)],
        out_specs=VMEM,
    )(rcv_points, rcv_normals, left_modes, vertices, connect, right_modes, mode_weights)[None]
    params = pltpu.CompilerParams(vmem_limit_bytes=24 << 20)
    sums = ()
    for mask in exchange_masks(count):
        held = value.shape[0]
        other = lax.ppermute(value, "src", [(s, s ^ mask) for s in range(count)])
        if held in (count // 4, count // 2):
            begin = 0 if held == count // 4 else count // 4
            sums = pl.pallas_call(
                functools.partial(early_kernel, begin, held, own_seg),
                out_shape=(pltpu.VMEM((LANES, 16), jnp.float32), pltpu.VMEM((own_seg, 16), jnp.float32)),
                in_specs=[VMEM] * (1 + len(sums)),
                out_specs=(VMEM, VMEM),
                scratch_shapes=pair_scratch(held - begin, own_seg),
                cost_estimate=pair_cost(held - begin, own_seg),
                compiler_params=params,
            )(value, *sums)
        value = jnp.concatenate([value, other], 0)
    return pl.pallas_call(
        functools.partial(last_kernel, count, own_seg),
        out_shape=(
            jax.ShapeDtypeStruct((6, LANES), jnp.float32),
            jax.ShapeDtypeStruct((3, own_seg), jnp.float32),
        ),
        in_specs=[VMEM] * 3,
        out_specs=(VMEM, VMEM),
        scratch_shapes=[pltpu.VMEM((count, 8, LANES), jnp.float32)] + pair_scratch(count // 2, own_seg),
        cost_estimate=pair_cost(count // 2, own_seg),
        compiler_params=params,
    )(value, *sums)


def solution(mesh):
    split = P(None, ("group", "src"))
    return jax.shard_map(
        on_device, mesh=mesh, in_specs=(split,) * 6 + (P("group"),), out_specs=(split, split), check_vma=False
    )
```

```python
import functools
import math

import jax
import jax.numpy as jnp
from jax import lax
from jax.experimental import pallas as pl
from jax.experimental.pallas import tpu as pltpu
from jax.sharding import PartitionSpec as P

core_term = 0.05
inverse_four_pi = 0.25 / math.pi

LANES = 128
ROWS = 24
CHUNK = 32
VMEM = pl.BlockSpec(memory_space=pltpu.VMEM)


def exchange_masks(count):
    masks = []
    step = count // 2
    while step > 1:
        masks.append(step + 1)
        step //= 2
    return masks + [1]


def mask_at(place, masks):
    value = 0
    for bit, mask in enumerate(masks):
        if place >> bit & 1:
            value ^= mask
    return value


def place_of(value, masks):
    place = 0
    rest = value & 1
    for bit, mask in enumerate(masks[:-1]):
        taken = lax.shift_right_logical(value, mask.bit_length() - 1) & 1
        place = place + taken * (1 << bit)
        rest = rest ^ taken
    return place + rest * (1 << (len(masks) - 1))


def high_low(value):
    high = value.astype(jnp.bfloat16).astype(jnp.float32)
    return high, value - high


def dot_nt(left, right):
    return lax.dot_general(left, right, (((1,), (1,)), ((), ())), preferred_element_type=jnp.float32)


def cross(a, b):
    return (a[1] * b[2] - a[2] * b[1], a[2] * b[0] - a[0] * b[2], a[0] * b[1] - a[1] * b[0])


def pair_terms(point, normal, moment, first, segment, turn, span, span_core, scale, want_span):
    rel = tuple(p - e for p, e in zip(point, first))
    cross_n = (moment[0] * segment[0] + moment[1] * segment[1] + moment[2] * segment[2]) - (
        normal[0] * turn[0] + normal[1] * turn[1] + normal[2] * turn[2]
    )
    dist_sq = rel[0] * rel[0] + rel[1] * rel[1] + rel[2] * rel[2]
    along = segment[0] * rel[0] + segment[1] * rel[1] + segment[2] * rel[2]
    other = along - span
    second_sq = dist_sq - along - other
    inv_first = lax.rsqrt(dist_sq)
    inv_second = lax.rsqrt(second_sq)
    inv_den = 1.0 / ((span * dist_sq + span_core) - along * along)
    part_first = along * inv_first
    part_second = other * inv_second
    line = part_first - part_second
    scaled = scale * inv_den
    by_normal = scaled * line
    by_line = scaled * cross_n
    by_den = (by_normal * cross_n) * inv_den
    by_den2 = by_den + by_den
    cube_first = part_first * (inv_first * inv_first)
    cube_second = part_second * (inv_second * inv_second)
    by_dist2 = by_line * (cube_second - cube_first) - by_den2 * span
    by_along = by_line * ((inv_first - inv_second) - cube_second) + by_den2 * along
    if not want_span:
        return rel, by_normal, by_dist2, by_along
    by_span2 = by_line * ((inv_second + inv_second) + cube_second) - by_den2 * (dist_sq + core_term)
    return rel, by_normal, by_dist2, by_along, by_span2


def segment_terms(first, second):
    segment = tuple(b - a for a, b in zip(first, second))
    span = segment[0] * segment[0] + segment[1] * segment[1] + segment[2] * segment[2]
    return segment, cross(segment, first), span, core_term * span + core_term


def pack_kernel(own_seg, points_ref, normals_ref, left_ref, vertices_ref, connect_ref, right_ref, weights_ref, out_ref):
    base = lax.axis_index("src") * own_seg
    row8 = lax.broadcasted_iota(jnp.int32, (8, LANES), 0)
    weight = jnp.zeros((8, LANES), jnp.float32)
    for mode in range(8):
        weight = jnp.where(row8 == mode, weights_ref[mode], weight)
    weighted = right_ref[...] * (weight * inverse_four_pi)
    high, rest = high_low(weighted)
    middle, low = high_low(rest)
    parts = jnp.concatenate([high, middle, low, jnp.zeros_like(low)], 0).astype(jnp.bfloat16)
    local = connect_ref[0:1, :] - base
    hit = lax.broadcasted_iota(jnp.int32, (LANES, LANES), 0) == local
    folded = dot_nt(parts, hit.astype(jnp.float32).astype(jnp.bfloat16))
    folded = folded[0:8] + (folded[8:16] + folded[16:24])
    out_ref[0:8, :] = left_ref[...]
    out_ref[8:10, :] = points_ref[0:2, :]
    out_ref[10:11, :] = 0.5 + 0.2 * points_ref[2:3, :]
    out_ref[11:14, :] = normals_ref[...]
    out_ref[14:16, :] = jnp.zeros((2, LANES), jnp.float32)
    out_ref[16:24, :] = folded
    out_ref[16:18, own_seg : 2 * own_seg] = vertices_ref[0:2, :]
    out_ref[18:19, own_seg : 2 * own_seg] = 0.2 * vertices_ref[2:3, :]


def pair_sums(data_ref, begin, end, own_seg, scratch, old1, old2):
    seg_ref, rec_ref, scale1_ref, scale2_ref, total1_ref, total2_ref = scratch
    blocks = end - begin
    tiles = blocks // 2
    lane = lax.broadcasted_iota(jnp.int32, (1, LANES), 1)
    low_half = lane < own_seg
    at_edge = (lane == own_seg - 1) | (lane == 2 * own_seg - 1)

    folded = []
    for tile in range(tiles):
        block_a, block_b = data_ref[begin + 2 * tile, 16:24, :], data_ref[begin + 2 * tile + 1, 16:24, :]
        both = jnp.where(low_half, block_a, pltpu.roll(block_b, own_seg, 1))
        folded.append(jnp.where(at_edge, 0.0, both))
        first = jnp.where(low_half, pltpu.roll(block_a, own_seg, 1), block_b)
        second = jnp.where(at_edge, first, pltpu.roll(first, LANES - 1, 1))
        for axis in range(3):
            seg_ref[axis, tile : tile + 1, :] = first[axis : axis + 1]
            seg_ref[3 + axis, tile : tile + 1, :] = second[axis : axis + 1]
    first = tuple(seg_ref[axis] for axis in range(3))
    segment, turn, span, span_core = segment_terms(first, tuple(seg_ref[3 + axis] for axis in range(3)))
    for axis in range(3):
        seg_ref[3 + axis] = segment[axis]
        seg_ref[6 + axis] = turn[axis]
    seg_ref[9] = span
    seg_ref[10] = span_core

    point = tuple(data_ref[begin:end, 8 + axis, :] for axis in range(3))
    normal = tuple(data_ref[begin:end, 11 + axis, :] for axis in range(3))
    moment = cross(point, normal)
    for axis in range(3):
        rec_ref[axis] = point[axis]
        rec_ref[3 + axis] = normal[axis]
        rec_ref[6 + axis] = moment[axis]

    def stack_hhll(rows):
        high, low = high_low(rows)
        return jnp.transpose(jnp.concatenate([high, high, low, low], 0)).astype(jnp.bfloat16)

    def stack_hlhl(rows):
        high, low = high_low(rows)
        both = jnp.concatenate([high, low], 0).astype(jnp.bfloat16)
        return jnp.concatenate([both, both], 0)

    own_block = data_ref[0, 16:24, :]
    left_own = stack_hhll(data_ref[0, 0:8, :])
    seg_own = stack_hhll(jnp.where(at_edge, 0.0, own_block))[0:own_seg]
    scale1_ref[...] = jnp.dot(
        left_own, stack_hlhl(jnp.concatenate(folded, 1)), preferred_element_type=jnp.float32)
    scale2_ref[...] = jnp.dot(
        seg_own, stack_hlhl(jnp.concatenate([data_ref[b, 0:8, :] for b in range(begin, end)], 1)),
        preferred_element_type=jnp.float32)

    def columns(rows):
        pad = jnp.zeros((16 - len(rows), LANES), jnp.float32)
        return jnp.transpose(jnp.concatenate(list(rows) + [pad], 0))

    own_p, own_n, own_m = own_receivers(data_ref)
    own_e, own_s, own_t, own_span, own_core = own_segments(own_block, own_seg)
    cols1 = columns([*own_p, *own_n, *own_m])
    cols2 = columns([*own_e, *own_s, *own_t, own_span, own_core])

    def packed(sums):
        result = jnp.zeros((CHUNK, 16), jnp.float32)
        column = lax.broadcasted_iota(jnp.int32, (CHUNK, 16), 1)
        for index, value in enumerate(sums):
            result = jnp.where(column == index, jnp.sum(value, axis=1, keepdims=True), result)
        return result

    for start in range(0, LANES, CHUNK):
        cols = cols1[start : start + CHUNK]
        col = [jnp.broadcast_to(cols[:, k : k + 1], (CHUNK, LANES)) for k in range(9)]
        sums = [jnp.zeros((CHUNK, LANES), jnp.float32) for _ in range(9)]
        for tile in range(tiles):
            row = [seg_ref[k, tile : tile + 1, :] for k in range(11)]
            scale = scale1_ref[start : start + CHUNK, tile * LANES : (tile + 1) * LANES]
            rel, by_normal, by_dist2, by_along = pair_terms(
                col[0:3], col[3:6], col[6:9], row[0:3], row[3:6], row[6:9], row[9], row[10], scale, False)
            for axis in range(3):
                sums[axis] += by_normal * row[3 + axis]
                sums[3 + axis] += by_normal * row[6 + axis]
                sums[6 + axis] += by_dist2 * rel[axis] + by_along * row[3 + axis]
        total1_ref[start : start + CHUNK, :] = packed(sums)

    for start in range(0, own_seg, CHUNK):
        cols = cols2[start : start + CHUNK]
        col = [jnp.broadcast_to(cols[:, k : k + 1], (CHUNK, LANES)) for k in range(11)]
        sums = [jnp.zeros((CHUNK, LANES), jnp.float32) for _ in range(11)]
        for block in range(blocks):
            row = [rec_ref[k, block : block + 1, :] for k in range(9)]
            scale = scale2_ref[start : start + CHUNK, block * LANES : (block + 1) * LANES]
            rel, by_normal, by_dist2, by_along, by_span2 = pair_terms(
                row[0:3], row[3:6], row[6:9], col[0:3], col[3:6], col[6:9], col[9], col[10], scale, True)
            for axis in range(3):
                sums[axis] += by_normal * row[3 + axis]
                sums[3 + axis] += by_normal * row[6 + axis] + by_along * rel[axis]
                sums[6 + axis] += by_dist2 * rel[axis]
            sums[9] += by_along
            sums[10] += by_span2
        total2_ref[start : start + CHUNK, :] = packed(sums)
    total1, total2 = total1_ref[...], total2_ref[...]
    if old1 is not None:
        total1, total2 = total1 + old1[...], total2 + old2[...]
    return total1, total2


def own_receivers(data_ref):
    point = tuple(data_ref[0, 8 + axis : 9 + axis, :] for axis in range(3))
    normal = tuple(data_ref[0, 11 + axis : 12 + axis, :] for axis in range(3))
    return point, normal, cross(point, normal)


def own_segments(own_block, own_seg):
    lane = lax.broadcasted_iota(jnp.int32, (1, LANES), 1)
    first = pltpu.roll(own_block, own_seg, 1)
    second = jnp.where(lane == own_seg - 1, first, pltpu.roll(first, LANES - 1, 1))
    own_e = tuple(first[axis : axis + 1] for axis in range(3))
    segment, turn, span, span_core = segment_terms(own_e, tuple(second[axis : axis + 1] for axis in range(3)))
    return own_e, segment, turn, span, span_core


def early_kernel(begin, end, own_seg, *refs):
    data_ref, rest = refs[0], refs[1:]
    olds = rest[0:2] if begin else (None, None)
    rest = rest[2:] if begin else rest
    rest[0][...], rest[1][...] = pair_sums(data_ref, begin, end, own_seg, rest[2:], *olds)


def last_kernel(count, own_seg, data_ref, old1_ref, old2_ref, rcv_out, vert_out, after_ref, *scratch):
    masks = exchange_masks(count)
    me = lax.axis_index("src")
    lane = lax.broadcasted_iota(jnp.int32, (1, LANES), 1)

    def place(device):
        return place_of((device & (count - 1)) ^ me, masks)

    total1, total2 = pair_sums(data_ref, count // 2, count, own_seg, scratch, old1_ref, old2_ref)
    for block in range(count):
        after_ref[block] = data_ref[place((me ^ mask_at(block, masks)) + 1), 16:24, :]

    def spread(column):
        return jnp.broadcast_to(column, (column.shape[0], LANES))

    own_block = data_ref[0, 16:24, :]
    before = data_ref[place(me + count - 1), 16:24, :]
    own_p, own_n, own_m = own_receivers(data_ref)
    point = tuple(data_ref[:, 8 + axis, :] for axis in range(3))
    normal = tuple(data_ref[:, 11 + axis, :] for axis in range(3))
    moment = cross(point, normal)
    mine_last = spread(own_block[:, 2 * own_seg - 1 : 2 * own_seg])
    mine_next = spread(after_ref[0, :, own_seg : own_seg + 1])
    mine_weight = spread(own_block[:, own_seg - 1 : own_seg])
    before_last = spread(before[:, 2 * own_seg - 1 : 2 * own_seg])
    before_weight = spread(jnp.where(me == 0, 0.0, before[:, own_seg - 1 : own_seg]))
    mine_first = spread(own_block[:, own_seg : own_seg + 1])

    def rows(value, axis):
        return jnp.broadcast_to(value[axis : axis + 1], (count, LANES))

    def stacked(own, every):
        return tuple(
            jnp.concatenate([jnp.broadcast_to(a, (count, LANES)), b, b], 0) for a, b in zip(own, every))

    first = tuple(
        jnp.concatenate(
            [spread(data_ref[:, 16 + axis, 2 * own_seg - 1 : 2 * own_seg]), rows(mine_last, axis), rows(before_last, axis)], 0)
        for axis in range(3))
    second = tuple(
        jnp.concatenate(
            [spread(after_ref[:, axis, own_seg : own_seg + 1]), rows(mine_next, axis), rows(mine_first, axis)], 0)
        for axis in range(3))
    scales = [jnp.zeros((count, LANES), jnp.float32)] * 3
    for mode in range(8):
        left = data_ref[:, mode, :]
        scales[0] += spread(data_ref[:, 16 + mode, own_seg - 1 : own_seg]) * data_ref[0, mode : mode + 1, :]
        scales[1] += mine_weight[mode : mode + 1] * left
        scales[2] += before_weight[mode : mode + 1] * left
    segment, turn, span, span_core = segment_terms(first, second)
    normals = stacked(own_n, normal)
    rel, by_normal, by_dist2, by_along, by_span2 = pair_terms(
        stacked(own_p, point), normals, stacked(own_m, moment),
        first, segment, turn, span, span_core, jnp.concatenate(scales, 0), True)

    def down(value):
        return jnp.sum(value, axis=0, keepdims=True)

    against_own, mine, ahead = slice(0, count), slice(count, 2 * count), slice(2 * count, 3 * count)
    swung, swept = cross(rel, normals), cross(normals, segment)
    edge_sum_s, edge_sum_t, edge_sum_p, leaving, arriving = [], [], [], [], []
    for axis in range(3):
        by_s = by_normal * swung[axis] + by_along * rel[axis] + by_span2 * segment[axis]
        by_p = by_dist2 * rel[axis] + by_along * segment[axis]
        by_r = by_normal * swept[axis] + by_p
        edge_sum_s.append(down((by_normal * segment[axis])[against_own]))
        edge_sum_t.append(down((by_normal * turn[axis])[against_own]))
        edge_sum_p.append(down(by_p[against_own]))
        leaving.append(down((by_s + by_r)[mine]))
        arriving.append(down(by_s[ahead]))
    edges = jnp.concatenate(leaving + arriving + leaving[0:2], 0)
    edges = jnp.broadcast_to(jnp.sum(edges, axis=1, keepdims=True), (8, LANES))[:, 0:own_seg]

    totals = jnp.transpose(total1)
    sum_s = tuple(totals[axis : axis + 1] + edge_sum_s[axis] for axis in range(3))
    by_point, by_norm = cross(own_n, sum_s), cross(sum_s, own_p)
    for axis in range(3):
        value = by_point[axis] + (totals[6 + axis : 7 + axis] + edge_sum_p[axis])
        rcv_out[axis : axis + 1, :] = 0.2 * value if axis == 2 else value
        rcv_out[3 + axis : 4 + axis, :] = by_norm[axis] - (totals[3 + axis : 4 + axis] + edge_sum_t[axis])

    totals = jnp.transpose(total2)
    sum_n = tuple(totals[axis : axis + 1] for axis in range(3))
    own_e, own_s, _, _, _ = own_segments(own_block, own_seg)
    own_e = tuple(value[:, 0:own_seg] for value in own_e)
    own_s = tuple(value[:, 0:own_seg] for value in own_s)
    turned, swept = cross(own_e, sum_n), cross(sum_n, own_s)
    lane = lane[:, 0:own_seg]
    for axis in range(3):
        by_second = totals[3 + axis : 4 + axis] - turned[axis] + own_s[axis] * totals[10:11]
        by_rel = swept[axis] + totals[6 + axis : 7 + axis] + own_s[axis] * totals[9:10]
        shifted = jnp.concatenate([by_second[:, own_seg - 1 :], by_second[:, : own_seg - 1]], 1)
        result = jnp.where(lane == 0, edges[3 + axis : 4 + axis], shifted) - (by_second + by_rel)
        result = result - jnp.where(lane == own_seg - 1, edges[axis : axis + 1], 0.0)
        vert_out[axis : axis + 1, :] = 0.2 * result if axis == 2 else result


def pair_scratch(blocks, own_seg):
    return [
        pltpu.VMEM((11, blocks // 2, LANES), jnp.float32),
        pltpu.VMEM((9, blocks, LANES), jnp.float32),
        pltpu.VMEM((LANES, blocks // 2 * LANES), jnp.float32),
        pltpu.VMEM((own_seg, blocks * LANES), jnp.float32),
        pltpu.VMEM((LANES, 16), jnp.float32),
        pltpu.VMEM((own_seg, 16), jnp.float32),
    ]


def pair_cost(blocks, own_seg):
    pairs = 2 * blocks * own_seg * LANES
    return pl.CostEstimate(flops=100 * pairs, bytes_accessed=blocks * ROWS * LANES * 4, transcendentals=3 * pairs)


def on_device(rcv_points, rcv_normals, left_modes, vertices, connect, right_modes, mode_weights):
    count = lax.axis_size("src")
    own_seg = vertices.shape[1]
    value = pl.pallas_call(
        functools.partial(pack_kernel, own_seg),
        out_shape=pltpu.VMEM((ROWS, LANES), jnp.float32),
        in_specs=[VMEM] * 6 + [pl.BlockSpec(memory_space=pltpu.SMEM)],
        out_specs=VMEM,
    )(rcv_points, rcv_normals, left_modes, vertices, connect, right_modes, mode_weights)[None]
    params = pltpu.CompilerParams(vmem_limit_bytes=24 << 20)
    sums = ()
    for mask in exchange_masks(count):
        held = value.shape[0]
        other = lax.ppermute(value, "src", [(s, s ^ mask) for s in range(count)])
        if held in (count // 4, count // 2):
            begin = 0 if held == count // 4 else count // 4
            sums = pl.pallas_call(
                functools.partial(early_kernel, begin, held, own_seg),
                out_shape=(pltpu.VMEM((LANES, 16), jnp.float32), pltpu.VMEM((own_seg, 16), jnp.float32)),
                in_specs=[VMEM] * (1 + len(sums)),
                out_specs=(VMEM, VMEM),
                scratch_shapes=pair_scratch(held - begin, own_seg),
                cost_estimate=pair_cost(held - begin, own_seg),
                compiler_params=params,
            )(value, *sums)
        value = jnp.concatenate([value, other], 0)
    return pl.pallas_call(
        functools.partial(last_kernel, count, own_seg),
        out_shape=(
            jax.ShapeDtypeStruct((6, LANES), jnp.float32),
            jax.ShapeDtypeStruct((3, own_seg), jnp.float32),
        ),
        in_specs=[VMEM] * 3,
        out_specs=(VMEM, VMEM),
        scratch_shapes=[pltpu.VMEM((count, 8, LANES), jnp.float32)] + pair_scratch(count // 2, own_seg),
        cost_estimate=pair_cost(count // 2, own_seg),
        compiler_params=params,
    )(value, *sums)


def solution(mesh):
    split = P(None, ("group", "src"))
    return jax.shard_map(
        on_device, mesh=mesh, in_specs=(split,) * 6 + (P("group"),), out_specs=(split, split), check_vma=False
    )
```

```python
import functools
import math

import jax
import jax.numpy as jnp
from jax import lax
from jax.experimental import pallas as pl
from jax.experimental.pallas import tpu as pltpu
from jax.sharding import PartitionSpec as P

core_term = 0.05
inverse_four_pi = 0.25 / math.pi

LANES = 128
ROWS = 24
CHUNK = 64
VMEM = pl.BlockSpec(memory_space=pltpu.VMEM)


def exchange_masks(count):
    masks = []
    step = count // 2
    while step > 1:
        masks.append(step + 1)
        step //= 2
    return masks + [1]


def mask_at(place, masks):
    value = 0
    for bit, mask in enumerate(masks):
        if place >> bit & 1:
            value ^= mask
    return value


def place_of(value, masks):
    place = 0
    rest = value & 1
    for bit, mask in enumerate(masks[:-1]):
        taken = lax.shift_right_logical(value, mask.bit_length() - 1) & 1
        place = place + taken * (1 << bit)
        rest = rest ^ taken
    return place + rest * (1 << (len(masks) - 1))


def high_low(value):
    high = value.astype(jnp.bfloat16).astype(jnp.float32)
    return high, value - high


def dot_nt(left, right):
    return lax.dot_general(left, right, (((1,), (1,)), ((), ())), preferred_element_type=jnp.float32)


def cross(a, b):
    return (a[1] * b[2] - a[2] * b[1], a[2] * b[0] - a[0] * b[2], a[0] * b[1] - a[1] * b[0])


def pair_terms(point, normal, moment, first, segment, turn, span, span_core, scale, want_span):
    rel = tuple(p - e for p, e in zip(point, first))
    cross_n = (moment[0] * segment[0] + moment[1] * segment[1] + moment[2] * segment[2]) - (
        normal[0] * turn[0] + normal[1] * turn[1] + normal[2] * turn[2]
    )
    dist_sq = rel[0] * rel[0] + rel[1] * rel[1] + rel[2] * rel[2]
    along = segment[0] * rel[0] + segment[1] * rel[1] + segment[2] * rel[2]
    other = along - span
    second_sq = dist_sq - along - other
    inv_first = lax.rsqrt(dist_sq)
    inv_second = lax.rsqrt(second_sq)
    inv_den = 1.0 / ((span * dist_sq + span_core) - along * along)
    part_first = along * inv_first
    part_second = other * inv_second
    line = part_first - part_second
    scaled = scale * inv_den
    by_normal = scaled * line
    by_line = scaled * cross_n
    by_den = (by_normal * cross_n) * inv_den
    by_den2 = by_den + by_den
    cube_first = part_first * (inv_first * inv_first)
    cube_second = part_second * (inv_second * inv_second)
    by_dist2 = by_line * (cube_second - cube_first) - by_den2 * span
    by_along = by_line * ((inv_first - inv_second) - cube_second) + by_den2 * along
    if not want_span:
        return rel, by_normal, by_dist2, by_along
    by_span2 = by_line * ((inv_second + inv_second) + cube_second) - by_den2 * (dist_sq + core_term)
    return rel, by_normal, by_dist2, by_along, by_span2


def segment_terms(first, second):
    segment = tuple(b - a for a, b in zip(first, second))
    span = segment[0] * segment[0] + segment[1] * segment[1] + segment[2] * segment[2]
    return segment, cross(segment, first), span, core_term * span + core_term


def pack_kernel(own_seg, points_ref, normals_ref, left_ref, vertices_ref, connect_ref, right_ref, weights_ref, out_ref):
    base = lax.axis_index("src") * own_seg
    row8 = lax.broadcasted_iota(jnp.int32, (8, LANES), 0)
    weight = jnp.zeros((8, LANES), jnp.float32)
    for mode in range(8):
        weight = jnp.where(row8 == mode, weights_ref[mode], weight)
    weighted = right_ref[...] * (weight * inverse_four_pi)
    high, rest = high_low(weighted)
    middle, low = high_low(rest)
    parts = jnp.concatenate([high, middle, low, jnp.zeros_like(low)], 0).astype(jnp.bfloat16)
    local = connect_ref[0:1, :] - base
    hit = lax.broadcasted_iota(jnp.int32, (LANES, LANES), 0) == local
    folded = dot_nt(parts, hit.astype(jnp.float32).astype(jnp.bfloat16))
    folded = folded[0:8] + (folded[8:16] + folded[16:24])
    out_ref[0:8, :] = left_ref[...]
    out_ref[8:10, :] = points_ref[0:2, :]
    out_ref[10:11, :] = 0.5 + 0.2 * points_ref[2:3, :]
    out_ref[11:14, :] = normals_ref[...]
    out_ref[14:16, :] = jnp.zeros((2, LANES), jnp.float32)
    out_ref[16:24, :] = folded
    out_ref[16:18, own_seg : 2 * own_seg] = vertices_ref[0:2, :]
    out_ref[18:19, own_seg : 2 * own_seg] = 0.2 * vertices_ref[2:3, :]


def stack_hhll(rows):
    high, low = high_low(rows)
    return jnp.transpose(jnp.concatenate([high, high, low, low], 0)).astype(jnp.bfloat16)


def stack_hlhl(rows):
    high, low = high_low(rows)
    both = jnp.concatenate([high, low], 0).astype(jnp.bfloat16)
    return jnp.concatenate([both, both], 0)


def lane_edges(own_seg):
    lane = lax.broadcasted_iota(jnp.int32, (1, LANES), 1)
    return (lane == own_seg - 1) | (lane == 2 * own_seg - 1)


def own_kernel(own_seg, data_ref, col1_ref, col2_ref, left_ref, right_ref, pick_ref):
    def columns(rows, out_ref):
        pad = jnp.zeros((16 - len(rows), LANES), jnp.float32)
        cols = jnp.transpose(jnp.concatenate(list(rows) + [pad], 0))
        count = out_ref.shape[1]
        for k in range(len(rows)):
            out_ref[k] = jnp.broadcast_to(cols[0:count, k : k + 1], (count, LANES))

    own_block = data_ref[0, 16:24, :]
    point, normal, moment = own_receivers(data_ref)
    columns([*point, *normal, *moment], col1_ref)
    own_e, own_s, own_t, span, span_core = own_segments(own_block, own_seg)
    columns([*own_e, *own_s, *own_t, span, span_core], col2_ref)
    left_ref[...] = stack_hhll(data_ref[0, 0:8, :])
    right_ref[...] = stack_hhll(jnp.where(lane_edges(own_seg), 0.0, own_block))[0:own_seg]
    group = lax.broadcasted_iota(jnp.int32, pick_ref.shape, 0) // LANES
    picked = group == lax.broadcasted_iota(jnp.int32, pick_ref.shape, 1)
    pick_ref[...] = picked.astype(jnp.float32).astype(jnp.bfloat16)


def pair_sums(data_ref, own_refs, begin, end, own_seg, scratch, old1, old2, new1, new2):
    seg_ref, rec_ref, scale1_ref, scale2_ref = scratch
    col1_ref, col2_ref, left_ref, right_ref = own_refs[0:4]
    blocks = end - begin
    tiles = blocks // 2
    lane = lax.broadcasted_iota(jnp.int32, (1, LANES), 1)
    low_half = lane < own_seg
    at_edge = lane_edges(own_seg)

    folded = []
    for tile in range(tiles):
        block_a, block_b = data_ref[begin + 2 * tile, 16:24, :], data_ref[begin + 2 * tile + 1, 16:24, :]
        both = jnp.where(low_half, block_a, pltpu.roll(block_b, own_seg, 1))
        folded.append(jnp.where(at_edge, 0.0, both))
        first = jnp.where(low_half, pltpu.roll(block_a, own_seg, 1), block_b)
        second = jnp.where(at_edge, first, pltpu.roll(first, LANES - 1, 1))
        for axis in range(3):
            seg_ref[axis, tile : tile + 1, :] = first[axis : axis + 1]
            seg_ref[3 + axis, tile : tile + 1, :] = second[axis : axis + 1]
    first = tuple(seg_ref[axis] for axis in range(3))
    segment, turn, span, span_core = segment_terms(first, tuple(seg_ref[3 + axis] for axis in range(3)))
    for axis in range(3):
        seg_ref[3 + axis] = segment[axis]
        seg_ref[6 + axis] = turn[axis]
    seg_ref[9] = span
    seg_ref[10] = span_core

    point = tuple(data_ref[begin:end, 8 + axis, :] for axis in range(3))
    normal = tuple(data_ref[begin:end, 11 + axis, :] for axis in range(3))
    moment = cross(point, normal)
    for axis in range(3):
        rec_ref[axis] = point[axis]
        rec_ref[3 + axis] = normal[axis]
        rec_ref[6 + axis] = moment[axis]

    scale1_ref[...] = jnp.dot(
        left_ref[...], stack_hlhl(jnp.concatenate(folded, 1)), preferred_element_type=jnp.float32)
    scale2_ref[...] = jnp.dot(
        right_ref[...], stack_hlhl(jnp.concatenate([data_ref[b, 0:8, :] for b in range(begin, end)], 1)),
        preferred_element_type=jnp.float32)

    def initial(old, count, start):
        if old is None:
            return [jnp.zeros((CHUNK, LANES), jnp.float32) for _ in range(count)]
        return [old[k, start : start + CHUNK, :] for k in range(count)]

    for start in range(0, LANES, CHUNK):
        col = [col1_ref[k, start : start + CHUNK, :] for k in range(9)]
        sums = initial(old1, 9, start)
        for tile in range(tiles):
            row = [seg_ref[k, tile : tile + 1, :] for k in range(11)]
            scale = scale1_ref[start : start + CHUNK, tile * LANES : (tile + 1) * LANES]
            rel, by_normal, by_dist2, by_along = pair_terms(
                col[0:3], col[3:6], col[6:9], row[0:3], row[3:6], row[6:9], row[9], row[10], scale, False)
            for axis in range(3):
                sums[axis] += by_normal * row[3 + axis]
                sums[3 + axis] += by_normal * row[6 + axis]
                sums[6 + axis] += by_dist2 * rel[axis] + by_along * row[3 + axis]
        for k in range(9):
            new1[k, start : start + CHUNK, :] = sums[k]

    for start in range(0, own_seg, CHUNK):
        col = [col2_ref[k, start : start + CHUNK, :] for k in range(11)]
        sums = initial(old2, 11, start)
        for block in range(blocks):
            row = [rec_ref[k, block : block + 1, :] for k in range(9)]
            scale = scale2_ref[start : start + CHUNK, block * LANES : (block + 1) * LANES]
            rel, by_normal, by_dist2, by_along, by_span2 = pair_terms(
                row[0:3], row[3:6], row[6:9], col[0:3], col[3:6], col[6:9], col[9], col[10], scale, True)
            for axis in range(3):
                sums[axis] += by_normal * row[3 + axis]
                sums[3 + axis] += by_normal * row[6 + axis] + by_along * rel[axis]
                sums[6 + axis] += by_dist2 * rel[axis]
            sums[9] += by_along
            sums[10] += by_span2
        for k in range(11):
            new2[k, start : start + CHUNK, :] = sums[k]


def lane_sums(sums_ref, pick_ref):
    count = sums_ref.shape[0]
    parts = [high_low(sums_ref[k]) for k in range(count)]
    pick = pick_ref[0 : count * LANES, :]
    high = jnp.concatenate([part[0] for part in parts], 1).astype(jnp.bfloat16)
    low = jnp.concatenate([part[1] for part in parts], 1).astype(jnp.bfloat16)
    return jnp.dot(high, pick, preferred_element_type=jnp.float32) + jnp.dot(
        low, pick, preferred_element_type=jnp.float32)


def own_receivers(data_ref):
    point = tuple(data_ref[0, 8 + axis : 9 + axis, :] for axis in range(3))
    normal = tuple(data_ref[0, 11 + axis : 12 + axis, :] for axis in range(3))
    return point, normal, cross(point, normal)


def own_segments(own_block, own_seg):
    lane = lax.broadcasted_iota(jnp.int32, (1, LANES), 1)
    first = pltpu.roll(own_block, own_seg, 1)
    second = jnp.where(lane == own_seg - 1, first, pltpu.roll(first, LANES - 1, 1))
    own_e = tuple(first[axis : axis + 1] for axis in range(3))
    segment, turn, span, span_core = segment_terms(own_e, tuple(second[axis : axis + 1] for axis in range(3)))
    return own_e, segment, turn, span, span_core


def early_kernel(begin, end, own_seg, *refs):
    data_ref, own_refs, rest = refs[0], refs[1:6], refs[6:]
    olds = rest[0:2] if begin else (None, None)
    rest = rest[2:] if begin else rest
    pair_sums(data_ref, own_refs, begin, end, own_seg, rest[2:], *olds, rest[0], rest[1])


def last_kernel(count, own_seg, *refs):
    data_ref, own_refs, old1_ref, old2_ref, rcv_out, vert_out, after_ref, new1_ref, new2_ref = (
        refs[0], refs[1:6], *refs[6:13])
    scratch = refs[13:]
    masks = exchange_masks(count)
    me = lax.axis_index("src")
    lane = lax.broadcasted_iota(jnp.int32, (1, LANES), 1)

    def place(device):
        return place_of((device & (count - 1)) ^ me, masks)

    pair_sums(
        data_ref, own_refs, count // 2, count, own_seg, scratch, old1_ref, old2_ref, new1_ref, new2_ref)
    total1 = lane_sums(new1_ref, own_refs[4])
    total2 = lane_sums(new2_ref, own_refs[4])
    for block in range(count):
        after_ref[block] = data_ref[place((me ^ mask_at(block, masks)) + 1), 16:24, :]

    def spread(column):
        return jnp.broadcast_to(column, (column.shape[0], LANES))

    own_block = data_ref[0, 16:24, :]
    before = data_ref[place(me + count - 1), 16:24, :]
    own_p, own_n, own_m = own_receivers(data_ref)
    point = tuple(data_ref[:, 8 + axis, :] for axis in range(3))
    normal = tuple(data_ref[:, 11 + axis, :] for axis in range(3))
    moment = cross(point, normal)
    mine_last = spread(own_block[:, 2 * own_seg - 1 : 2 * own_seg])
    mine_next = spread(after_ref[0, :, own_seg : own_seg + 1])
    mine_weight = spread(own_block[:, own_seg - 1 : own_seg])
    before_last = spread(before[:, 2 * own_seg - 1 : 2 * own_seg])
    before_weight = spread(jnp.where(me == 0, 0.0, before[:, own_seg - 1 : own_seg]))
    mine_first = spread(own_block[:, own_seg : own_seg + 1])

    def rows(value, axis):
        return jnp.broadcast_to(value[axis : axis + 1], (count, LANES))

    def stacked(own, every):
        return tuple(
            jnp.concatenate([jnp.broadcast_to(a, (count, LANES)), b, b], 0) for a, b in zip(own, every))

    first = tuple(
        jnp.concatenate(
            [spread(data_ref[:, 16 + axis, 2 * own_seg - 1 : 2 * own_seg]), rows(mine_last, axis), rows(before_last, axis)], 0)
        for axis in range(3))
    second = tuple(
        jnp.concatenate(
            [spread(after_ref[:, axis, own_seg : own_seg + 1]), rows(mine_next, axis), rows(mine_first, axis)], 0)
        for axis in range(3))
    scales = [jnp.zeros((count, LANES), jnp.float32)] * 3
    for mode in range(8):
        left = data_ref[:, mode, :]
        scales[0] += spread(data_ref[:, 16 + mode, own_seg - 1 : own_seg]) * data_ref[0, mode : mode + 1, :]
        scales[1] += mine_weight[mode : mode + 1] * left
        scales[2] += before_weight[mode : mode + 1] * left
    segment, turn, span, span_core = segment_terms(first, second)
    normals = stacked(own_n, normal)
    rel, by_normal, by_dist2, by_along, by_span2 = pair_terms(
        stacked(own_p, point), normals, stacked(own_m, moment),
        first, segment, turn, span, span_core, jnp.concatenate(scales, 0), True)

    def down(value):
        return jnp.sum(value, axis=0, keepdims=True)

    against_own, mine, ahead = slice(0, count), slice(count, 2 * count), slice(2 * count, 3 * count)
    swung, swept = cross(rel, normals), cross(normals, segment)
    edge_sum_s, edge_sum_t, edge_sum_p, leaving, arriving = [], [], [], [], []
    for axis in range(3):
        by_s = by_normal * swung[axis] + by_along * rel[axis] + by_span2 * segment[axis]
        by_p = by_dist2 * rel[axis] + by_along * segment[axis]
        by_r = by_normal * swept[axis] + by_p
        edge_sum_s.append(down((by_normal * segment[axis])[against_own]))
        edge_sum_t.append(down((by_normal * turn[axis])[against_own]))
        edge_sum_p.append(down(by_p[against_own]))
        leaving.append(down((by_s + by_r)[mine]))
        arriving.append(down(by_s[ahead]))
    edges = jnp.concatenate(leaving + arriving + leaving[0:2], 0)
    edges = jnp.broadcast_to(jnp.sum(edges, axis=1, keepdims=True), (8, LANES))[:, 0:own_seg]

    totals = jnp.transpose(total1)
    sum_s = tuple(totals[axis : axis + 1] + edge_sum_s[axis] for axis in range(3))
    by_point, by_norm = cross(own_n, sum_s), cross(sum_s, own_p)
    for axis in range(3):
        value = by_point[axis] + (totals[6 + axis : 7 + axis] + edge_sum_p[axis])
        rcv_out[axis : axis + 1, :] = 0.2 * value if axis == 2 else value
        rcv_out[3 + axis : 4 + axis, :] = by_norm[axis] - (totals[3 + axis : 4 + axis] + edge_sum_t[axis])

    totals = jnp.transpose(total2)
    sum_n = tuple(totals[axis : axis + 1] for axis in range(3))
    own_e, own_s, _, _, _ = own_segments(own_block, own_seg)
    own_e = tuple(value[:, 0:own_seg] for value in own_e)
    own_s = tuple(value[:, 0:own_seg] for value in own_s)
    turned, swept = cross(own_e, sum_n), cross(sum_n, own_s)
    lane = lane[:, 0:own_seg]
    for axis in range(3):
        by_second = totals[3 + axis : 4 + axis] - turned[axis] + own_s[axis] * totals[10:11]
        by_rel = swept[axis] + totals[6 + axis : 7 + axis] + own_s[axis] * totals[9:10]
        shifted = jnp.concatenate([by_second[:, own_seg - 1 :], by_second[:, : own_seg - 1]], 1)
        result = jnp.where(lane == 0, edges[3 + axis : 4 + axis], shifted) - (by_second + by_rel)
        result = result - jnp.where(lane == own_seg - 1, edges[axis : axis + 1], 0.0)
        vert_out[axis : axis + 1, :] = 0.2 * result if axis == 2 else result


def pair_scratch(blocks, own_seg):
    return [
        pltpu.VMEM((11, blocks // 2, LANES), jnp.float32),
        pltpu.VMEM((9, blocks, LANES), jnp.float32),
        pltpu.VMEM((LANES, blocks // 2 * LANES), jnp.float32),
        pltpu.VMEM((own_seg, blocks * LANES), jnp.float32),
    ]


def sum_shapes(own_seg):
    return [pltpu.VMEM((9, LANES, LANES), jnp.float32), pltpu.VMEM((11, own_seg, LANES), jnp.float32)]


def last_scratch(count, own_seg):
    return [pltpu.VMEM((count, 8, LANES), jnp.float32)] + sum_shapes(own_seg) + pair_scratch(count // 2, own_seg)


def pair_cost(blocks, own_seg):
    pairs = 2 * blocks * own_seg * LANES
    return pl.CostEstimate(flops=100 * pairs, bytes_accessed=blocks * ROWS * LANES * 4, transcendentals=3 * pairs)


def on_device(rcv_points, rcv_normals, left_modes, vertices, connect, right_modes, mode_weights):
    count = lax.axis_size("src")
    own_seg = vertices.shape[1]
    value = pl.pallas_call(
        functools.partial(pack_kernel, own_seg),
        out_shape=pltpu.VMEM((ROWS, LANES), jnp.float32),
        in_specs=[VMEM] * 6 + [pl.BlockSpec(memory_space=pltpu.SMEM)],
        out_specs=VMEM,
    )(rcv_points, rcv_normals, left_modes, vertices, connect, right_modes, mode_weights)[None]
    params = pltpu.CompilerParams(vmem_limit_bytes=24 << 20)
    own = pl.pallas_call(
        functools.partial(own_kernel, own_seg),
        out_shape=(
            *sum_shapes(own_seg),
            pltpu.VMEM((LANES, 32), jnp.bfloat16),
            pltpu.VMEM((own_seg, 32), jnp.bfloat16),
            pltpu.VMEM((11 * LANES, 16), jnp.bfloat16),
        ),
        in_specs=[VMEM],
        out_specs=(VMEM,) * 5,
        cost_estimate=pair_cost(2, own_seg),
        compiler_params=params,
    )(value)
    sums = ()
    for mask in exchange_masks(count):
        held = value.shape[0]
        other = lax.ppermute(value, "src", [(s, s ^ mask) for s in range(count)])
        if held in (count // 4, count // 2):
            begin = 0 if held == count // 4 else count // 4
            sums = pl.pallas_call(
                functools.partial(early_kernel, begin, held, own_seg),
                out_shape=tuple(sum_shapes(own_seg)),
                in_specs=[VMEM] * (6 + len(sums)),
                out_specs=(VMEM, VMEM),
                scratch_shapes=pair_scratch(held - begin, own_seg),
                cost_estimate=pair_cost(held - begin, own_seg),
                compiler_params=params,
            )(value, *own, *sums)
        value = jnp.concatenate([value, other], 0)
    return pl.pallas_call(
        functools.partial(last_kernel, count, own_seg),
        out_shape=(
            jax.ShapeDtypeStruct((6, LANES), jnp.float32),
            jax.ShapeDtypeStruct((3, own_seg), jnp.float32),
        ),
        in_specs=[VMEM] * 8,
        out_specs=(VMEM, VMEM),
        scratch_shapes=last_scratch(count, own_seg),
        cost_estimate=pair_cost(count // 2, own_seg),
        compiler_params=params,
    )(value, *own, *sums)


def solution(mesh):
    split = P(None, ("group", "src"))
    return jax.shard_map(
        on_device, mesh=mesh, in_specs=(split,) * 6 + (P("group"),), out_specs=(split, split), check_vma=False
    )
```

```python
import functools
import math

import jax
import jax.numpy as jnp
from jax import lax
from jax.experimental import pallas as pl
from jax.experimental.pallas import tpu as pltpu
from jax.sharding import PartitionSpec as P

core_term = 0.05
inverse_four_pi = 0.25 / math.pi

LANES = 128
ROWS = 24
CHUNK = 64
FINISH = 32
VMEM = pl.BlockSpec(memory_space=pltpu.VMEM)


def exchange_masks(count):
    masks = []
    step = count // 2
    while step > 1:
        masks.append(step + 1)
        step //= 2
    return masks + [1]


def mask_at(place, masks):
    value = 0
    for bit, mask in enumerate(masks):
        if place >> bit & 1:
            value ^= mask
    return value


def place_of(value, masks):
    place = 0
    rest = value & 1
    for bit, mask in enumerate(masks[:-1]):
        taken = lax.shift_right_logical(value, mask.bit_length() - 1) & 1
        place = place + taken * (1 << bit)
        rest = rest ^ taken
    return place + rest * (1 << (len(masks) - 1))


def high_low(value):
    high = value.astype(jnp.bfloat16).astype(jnp.float32)
    return high, value - high


def dot_nt(left, right):
    return lax.dot_general(left, right, (((1,), (1,)), ((), ())), preferred_element_type=jnp.float32)


def cross(a, b):
    return (a[1] * b[2] - a[2] * b[1], a[2] * b[0] - a[0] * b[2], a[0] * b[1] - a[1] * b[0])


def pair_terms(point, normal, moment, first, segment, turn, span, span_core, scale, want_span):
    rel = tuple(p - e for p, e in zip(point, first))
    cross_n = (moment[0] * segment[0] + moment[1] * segment[1] + moment[2] * segment[2]) - (
        normal[0] * turn[0] + normal[1] * turn[1] + normal[2] * turn[2]
    )
    dist_sq = rel[0] * rel[0] + rel[1] * rel[1] + rel[2] * rel[2]
    along = segment[0] * rel[0] + segment[1] * rel[1] + segment[2] * rel[2]
    other = along - span
    second_sq = dist_sq - along - other
    inv_first = lax.rsqrt(dist_sq)
    inv_second = lax.rsqrt(second_sq)
    inv_den = 1.0 / ((span * dist_sq + span_core) - along * along)
    part_first = along * inv_first
    part_second = other * inv_second
    line = part_first - part_second
    scaled = scale * inv_den
    by_normal = scaled * line
    by_line = scaled * cross_n
    by_den = (by_normal * cross_n) * inv_den
    by_den2 = by_den + by_den
    cube_first = part_first * (inv_first * inv_first)
    cube_second = part_second * (inv_second * inv_second)
    by_dist2 = by_line * (cube_second - cube_first) - by_den2 * span
    by_along = by_line * ((inv_first - inv_second) - cube_second) + by_den2 * along
    if not want_span:
        return rel, by_normal, by_dist2, by_along
    by_span2 = by_line * ((inv_second + inv_second) + cube_second) - by_den2 * (dist_sq + core_term)
    return rel, by_normal, by_dist2, by_along, by_span2


def segment_terms(first, second):
    segment = tuple(b - a for a, b in zip(first, second))
    span = segment[0] * segment[0] + segment[1] * segment[1] + segment[2] * segment[2]
    return segment, cross(segment, first), span, core_term * span + core_term


def pack_kernel(own_seg, points_ref, normals_ref, left_ref, vertices_ref, connect_ref, right_ref, weights_ref, out_ref):
    base = lax.axis_index("src") * own_seg
    row8 = lax.broadcasted_iota(jnp.int32, (8, LANES), 0)
    weight = jnp.zeros((8, LANES), jnp.float32)
    for mode in range(8):
        weight = jnp.where(row8 == mode, weights_ref[mode], weight)
    weighted = right_ref[...] * (weight * inverse_four_pi)
    high, rest = high_low(weighted)
    middle, low = high_low(rest)
    parts = jnp.concatenate([high, middle, low, jnp.zeros_like(low)], 0).astype(jnp.bfloat16)
    local = connect_ref[0:1, :] - base
    hit = lax.broadcasted_iota(jnp.int32, (LANES, LANES), 0) == local
    folded = dot_nt(parts, hit.astype(jnp.float32).astype(jnp.bfloat16))
    folded = folded[0:8] + (folded[8:16] + folded[16:24])
    out_ref[0:8, :] = left_ref[...]
    out_ref[8:10, :] = points_ref[0:2, :]
    out_ref[10:11, :] = 0.5 + 0.2 * points_ref[2:3, :]
    out_ref[11:14, :] = normals_ref[...]
    out_ref[14:16, :] = jnp.zeros((2, LANES), jnp.float32)
    out_ref[16:24, :] = folded
    out_ref[16:18, own_seg : 2 * own_seg] = vertices_ref[0:2, :]
    out_ref[18:19, own_seg : 2 * own_seg] = 0.2 * vertices_ref[2:3, :]


def stack_hhll(rows):
    high, low = high_low(rows)
    return jnp.transpose(jnp.concatenate([high, high, low, low], 0)).astype(jnp.bfloat16)


def stack_hlhl(rows):
    high, low = high_low(rows)
    both = jnp.concatenate([high, low], 0).astype(jnp.bfloat16)
    return jnp.concatenate([both, both], 0)


def lane_edges(own_seg):
    lane = lax.broadcasted_iota(jnp.int32, (1, LANES), 1)
    return (lane == own_seg - 1) | (lane == 2 * own_seg - 1)


def own_kernel(own_seg, data_ref, col1_ref, col2_ref, left_ref, right_ref):
    def columns(rows, out_ref):
        pad = jnp.zeros((16 - len(rows), LANES), jnp.float32)
        cols = jnp.transpose(jnp.concatenate(list(rows) + [pad], 0))
        count = out_ref.shape[1]
        for k in range(len(rows)):
            out_ref[k] = jnp.broadcast_to(cols[0:count, k : k + 1], (count, LANES))

    own_block = data_ref[0, 16:24, :]
    point, normal, moment = own_receivers(data_ref)
    columns([*point, *normal, *moment], col1_ref)
    own_e, own_s, own_t, span, span_core = own_segments(own_block, own_seg)
    columns([*own_e, *own_s, *own_t, span, span_core], col2_ref)
    left_ref[...] = stack_hhll(data_ref[0, 0:8, :])
    right_ref[...] = stack_hhll(jnp.where(lane_edges(own_seg), 0.0, own_block))[0:own_seg]


def pair_sums(data_ref, own_refs, begin, end, own_seg, scratch, old1, old2, new1, new2):
    seg_ref, rec_ref, scale1_ref, scale2_ref = scratch
    col1_ref, col2_ref, left_ref, right_ref = own_refs
    blocks = end - begin
    tiles = blocks // 2
    lane = lax.broadcasted_iota(jnp.int32, (1, LANES), 1)
    low_half = lane < own_seg
    at_edge = lane_edges(own_seg)

    folded = []
    for tile in range(tiles):
        block_a, block_b = data_ref[begin + 2 * tile, 16:24, :], data_ref[begin + 2 * tile + 1, 16:24, :]
        both = jnp.where(low_half, block_a, pltpu.roll(block_b, own_seg, 1))
        folded.append(jnp.where(at_edge, 0.0, both))
        first = jnp.where(low_half, pltpu.roll(block_a, own_seg, 1), block_b)
        second = jnp.where(at_edge, first, pltpu.roll(first, LANES - 1, 1))
        for axis in range(3):
            seg_ref[axis, tile : tile + 1, :] = first[axis : axis + 1]
            seg_ref[3 + axis, tile : tile + 1, :] = second[axis : axis + 1]
    first = tuple(seg_ref[axis] for axis in range(3))
    segment, turn, span, span_core = segment_terms(first, tuple(seg_ref[3 + axis] for axis in range(3)))
    for axis in range(3):
        seg_ref[3 + axis] = segment[axis]
        seg_ref[6 + axis] = turn[axis]
    seg_ref[9] = span
    seg_ref[10] = span_core

    point = tuple(data_ref[begin:end, 8 + axis, :] for axis in range(3))
    normal = tuple(data_ref[begin:end, 11 + axis, :] for axis in range(3))
    moment = cross(point, normal)
    for axis in range(3):
        rec_ref[axis] = point[axis]
        rec_ref[3 + axis] = normal[axis]
        rec_ref[6 + axis] = moment[axis]

    scale1_ref[...] = jnp.dot(
        left_ref[...], stack_hlhl(jnp.concatenate(folded, 1)), preferred_element_type=jnp.float32)
    scale2_ref[...] = jnp.dot(
        right_ref[...], stack_hlhl(jnp.concatenate([data_ref[b, 0:8, :] for b in range(begin, end)], 1)),
        preferred_element_type=jnp.float32)

    def initial(old, count, start):
        if old is None:
            return [jnp.zeros((CHUNK, LANES), jnp.float32) for _ in range(count)]
        return [old[k, start : start + CHUNK, :] for k in range(count)]

    for start in range(0, LANES, CHUNK):
        col = [col1_ref[k, start : start + CHUNK, :] for k in range(9)]
        sums = initial(old1, 9, start)
        for tile in range(tiles):
            row = [seg_ref[k, tile : tile + 1, :] for k in range(11)]
            scale = scale1_ref[start : start + CHUNK, tile * LANES : (tile + 1) * LANES]
            rel, by_normal, by_dist2, by_along = pair_terms(
                col[0:3], col[3:6], col[6:9], row[0:3], row[3:6], row[6:9], row[9], row[10], scale, False)
            for axis in range(3):
                sums[axis] += by_normal * row[3 + axis]
                sums[3 + axis] += by_normal * row[6 + axis]
                sums[6 + axis] += by_dist2 * rel[axis] + by_along * row[3 + axis]
        for k in range(9):
            new1[k, start : start + CHUNK, :] = sums[k]

    for start in range(0, own_seg, CHUNK):
        col = [col2_ref[k, start : start + CHUNK, :] for k in range(11)]
        sums = initial(old2, 11, start)
        for block in range(blocks):
            row = [rec_ref[k, block : block + 1, :] for k in range(9)]
            scale = scale2_ref[start : start + CHUNK, block * LANES : (block + 1) * LANES]
            rel, by_normal, by_dist2, by_along, by_span2 = pair_terms(
                row[0:3], row[3:6], row[6:9], col[0:3], col[3:6], col[6:9], col[9], col[10], scale, True)
            for axis in range(3):
                sums[axis] += by_normal * row[3 + axis]
                sums[3 + axis] += by_normal * row[6 + axis] + by_along * rel[axis]
                sums[6 + axis] += by_dist2 * rel[axis]
            sums[9] += by_along
            sums[10] += by_span2
        for k in range(11):
            new2[k, start : start + CHUNK, :] = sums[k]


def lane_sums(values):
    rows = values[0].shape[0]
    column = lax.broadcasted_iota(jnp.int32, (rows, 16), 1)
    result = jnp.zeros((rows, 16), jnp.float32)
    for index, value in enumerate(values):
        result = jnp.where(column == index, jnp.sum(value, axis=1, keepdims=True), result)
    return result


def receiver_totals(sums_ref, col_ref):
    parts = []
    for start in range(0, LANES, FINISH):
        sums = [sums_ref[k, start : start + FINISH, :] for k in range(9)]
        col = [col_ref[k, start : start + FINISH, :] for k in range(6)]
        by_point = [a + b for a, b in zip(cross(col[3:6], sums[0:3]), sums[6:9])]
        by_normal = [a - b for a, b in zip(cross(sums[0:3], col[0:3]), sums[3:6])]
        parts.append(lane_sums(by_point + by_normal))
    return jnp.transpose(jnp.concatenate(parts, 0))


def segment_totals(sums_ref, col_ref, own_seg):
    parts = []
    for start in range(0, own_seg, FINISH):
        sums = [sums_ref[k, start : start + FINISH, :] for k in range(11)]
        col = [col_ref[k, start : start + FINISH, :] for k in range(6)]
        turned, swept = cross(col[0:3], sums[0:3]), cross(sums[0:3], col[3:6])
        by_s = [sums[3 + k] - turned[k] + col[3 + k] * sums[10] for k in range(3)]
        by_both = [by_s[k] + (swept[k] + sums[6 + k] + col[3 + k] * sums[9]) for k in range(3)]
        parts.append(lane_sums(by_s + by_both))
    return jnp.transpose(jnp.concatenate(parts, 0))


def own_receivers(data_ref):
    point = tuple(data_ref[0, 8 + axis : 9 + axis, :] for axis in range(3))
    normal = tuple(data_ref[0, 11 + axis : 12 + axis, :] for axis in range(3))
    return point, normal, cross(point, normal)


def own_segments(own_block, own_seg):
    lane = lax.broadcasted_iota(jnp.int32, (1, LANES), 1)
    first = pltpu.roll(own_block, own_seg, 1)
    second = jnp.where(lane == own_seg - 1, first, pltpu.roll(first, LANES - 1, 1))
    own_e = tuple(first[axis : axis + 1] for axis in range(3))
    segment, turn, span, span_core = segment_terms(own_e, tuple(second[axis : axis + 1] for axis in range(3)))
    return own_e, segment, turn, span, span_core


def early_kernel(chained, own_seg, *refs):
    data_ref, own_refs, rest = refs[0], refs[1:5], refs[5:]
    olds = rest[0:2] if chained else (None, None)
    rest = rest[2:] if chained else rest
    pair_sums(data_ref, own_refs, 0, data_ref.shape[0], own_seg, rest[2:], *olds, rest[0], rest[1])


def last_kernel(count, own_seg, *refs):
    data_ref, own_refs, old1_ref, old2_ref, rcv_out, vert_out, after_ref, new1_ref, new2_ref = (
        refs[0], refs[1:5], *refs[5:12])
    scratch = refs[12:]
    masks = exchange_masks(count)
    me = lax.axis_index("src")
    lane = lax.broadcasted_iota(jnp.int32, (1, LANES), 1)

    def place(device):
        return place_of((device & (count - 1)) ^ me, masks)

    pair_sums(
        data_ref, own_refs, count - count // 4, count, own_seg, scratch, old1_ref, old2_ref, new1_ref, new2_ref)
    for block in range(count):
        after_ref[block] = data_ref[place((me ^ mask_at(block, masks)) + 1), 16:24, :]

    def spread(column):
        return jnp.broadcast_to(column, (column.shape[0], LANES))

    own_block = data_ref[0, 16:24, :]
    before = data_ref[place(me + count - 1), 16:24, :]
    own_p, own_n, own_m = own_receivers(data_ref)
    point = tuple(data_ref[:, 8 + axis, :] for axis in range(3))
    normal = tuple(data_ref[:, 11 + axis, :] for axis in range(3))
    moment = cross(point, normal)
    mine_last = spread(own_block[:, 2 * own_seg - 1 : 2 * own_seg])
    mine_next = spread(after_ref[0, :, own_seg : own_seg + 1])
    mine_weight = spread(own_block[:, own_seg - 1 : own_seg])
    before_last = spread(before[:, 2 * own_seg - 1 : 2 * own_seg])
    before_weight = spread(jnp.where(me == 0, 0.0, before[:, own_seg - 1 : own_seg]))
    mine_first = spread(own_block[:, own_seg : own_seg + 1])

    def rows(value, axis):
        return jnp.broadcast_to(value[axis : axis + 1], (count, LANES))

    def stacked(own, every):
        return tuple(
            jnp.concatenate([jnp.broadcast_to(a, (count, LANES)), b, b], 0) for a, b in zip(own, every))

    first = tuple(
        jnp.concatenate(
            [spread(data_ref[:, 16 + axis, 2 * own_seg - 1 : 2 * own_seg]), rows(mine_last, axis), rows(before_last, axis)], 0)
        for axis in range(3))
    second = tuple(
        jnp.concatenate(
            [spread(after_ref[:, axis, own_seg : own_seg + 1]), rows(mine_next, axis), rows(mine_first, axis)], 0)
        for axis in range(3))
    scales = [jnp.zeros((count, LANES), jnp.float32)] * 3
    for mode in range(8):
        left = data_ref[:, mode, :]
        scales[0] += spread(data_ref[:, 16 + mode, own_seg - 1 : own_seg]) * data_ref[0, mode : mode + 1, :]
        scales[1] += mine_weight[mode : mode + 1] * left
        scales[2] += before_weight[mode : mode + 1] * left
    segment, turn, span, span_core = segment_terms(first, second)
    normals = stacked(own_n, normal)
    rel, by_normal, by_dist2, by_along, by_span2 = pair_terms(
        stacked(own_p, point), normals, stacked(own_m, moment),
        first, segment, turn, span, span_core, jnp.concatenate(scales, 0), True)

    def down(value):
        return jnp.sum(value, axis=0, keepdims=True)

    against_own, mine, ahead = slice(0, count), slice(count, 2 * count), slice(2 * count, 3 * count)
    swung, swept = cross(rel, normals), cross(normals, segment)
    edge_sum_s, edge_sum_t, edge_sum_p, leaving, arriving = [], [], [], [], []
    for axis in range(3):
        by_s = by_normal * swung[axis] + by_along * rel[axis] + by_span2 * segment[axis]
        by_p = by_dist2 * rel[axis] + by_along * segment[axis]
        by_r = by_normal * swept[axis] + by_p
        edge_sum_s.append(down((by_normal * segment[axis])[against_own]))
        edge_sum_t.append(down((by_normal * turn[axis])[against_own]))
        edge_sum_p.append(down(by_p[against_own]))
        leaving.append(down((by_s + by_r)[mine]))
        arriving.append(down(by_s[ahead]))
    edges = jnp.concatenate(leaving + arriving + leaving[0:2], 0)
    edges = jnp.broadcast_to(jnp.sum(edges, axis=1, keepdims=True), (8, LANES))[:, 0:own_seg]

    totals = receiver_totals(new1_ref, own_refs[0])
    by_point, by_norm = cross(own_n, edge_sum_s), cross(edge_sum_s, own_p)
    for axis in range(3):
        value = totals[axis : axis + 1] + (by_point[axis] + edge_sum_p[axis])
        rcv_out[axis : axis + 1, :] = 0.2 * value if axis == 2 else value
        rcv_out[3 + axis : 4 + axis, :] = totals[3 + axis : 4 + axis] + (by_norm[axis] - edge_sum_t[axis])

    totals = segment_totals(new2_ref, own_refs[1], own_seg)
    lane = lane[:, 0:own_seg]
    for axis in range(3):
        by_second = totals[axis : axis + 1]
        shifted = jnp.concatenate([by_second[:, own_seg - 1 :], by_second[:, : own_seg - 1]], 1)
        result = jnp.where(lane == 0, edges[3 + axis : 4 + axis], shifted) - totals[3 + axis : 4 + axis]
        result = result - jnp.where(lane == own_seg - 1, edges[axis : axis + 1], 0.0)
        vert_out[axis : axis + 1, :] = 0.2 * result if axis == 2 else result


def pair_scratch(blocks, own_seg):
    return [
        pltpu.VMEM((11, blocks // 2, LANES), jnp.float32),
        pltpu.VMEM((9, blocks, LANES), jnp.float32),
        pltpu.VMEM((LANES, blocks // 2 * LANES), jnp.float32),
        pltpu.VMEM((own_seg, blocks * LANES), jnp.float32),
    ]


def sum_shapes(own_seg):
    return [pltpu.VMEM((9, LANES, LANES), jnp.float32), pltpu.VMEM((11, own_seg, LANES), jnp.float32)]


def last_scratch(count, own_seg):
    return [pltpu.VMEM((count, 8, LANES), jnp.float32)] + sum_shapes(own_seg) + pair_scratch(count // 4, own_seg)


def pair_cost(blocks, own_seg):
    pairs = 2 * blocks * own_seg * LANES
    return pl.CostEstimate(flops=100 * pairs, bytes_accessed=blocks * ROWS * LANES * 4, transcendentals=3 * pairs)


def on_device(rcv_points, rcv_normals, left_modes, vertices, connect, right_modes, mode_weights):
    count = lax.axis_size("src")
    own_seg = vertices.shape[1]
    value = pl.pallas_call(
        functools.partial(pack_kernel, own_seg),
        out_shape=pltpu.VMEM((ROWS, LANES), jnp.float32),
        in_specs=[VMEM] * 6 + [pl.BlockSpec(memory_space=pltpu.SMEM)],
        out_specs=VMEM,
    )(rcv_points, rcv_normals, left_modes, vertices, connect, right_modes, mode_weights)[None]
    params = pltpu.CompilerParams(vmem_limit_bytes=24 << 20)
    own = pl.pallas_call(
        functools.partial(own_kernel, own_seg),
        out_shape=(
            *sum_shapes(own_seg),
            pltpu.VMEM((LANES, 32), jnp.bfloat16),
            pltpu.VMEM((own_seg, 32), jnp.bfloat16),
        ),
        in_specs=[VMEM],
        out_specs=(VMEM,) * 4,
        cost_estimate=pair_cost(2, own_seg),
        compiler_params=params,
    )(value)

    def exchange(block, mask):
        return lax.ppermute(block, "src", [(s, s ^ mask) for s in range(count)])

    def add_pairs(block, *sums):
        return pl.pallas_call(
            functools.partial(early_kernel, len(sums) > 0, own_seg),
            out_shape=tuple(sum_shapes(own_seg)),
            in_specs=[VMEM] * (5 + len(sums)),
            out_specs=(VMEM, VMEM),
            scratch_shapes=pair_scratch(block.shape[0], own_seg),
            cost_estimate=pair_cost(block.shape[0], own_seg),
            compiler_params=params,
        )(block, *own, *sums)

    masks = exchange_masks(count)
    for mask in masks[:-2]:
        value = jnp.concatenate([value, exchange(value, mask)], 0)
    across, beside = exchange(value, masks[-2]), exchange(value, masks[-1])
    sums = add_pairs(value)
    sums = add_pairs(beside, *sums)
    across, sums = lax.optimization_barrier((across, sums))
    opposite = exchange(across, masks[-1])
    sums = add_pairs(across, *sums)
    value = jnp.concatenate([value, across, beside, opposite], 0)
    return pl.pallas_call(
        functools.partial(last_kernel, count, own_seg),
        out_shape=(
            jax.ShapeDtypeStruct((6, LANES), jnp.float32),
            jax.ShapeDtypeStruct((3, own_seg), jnp.float32),
        ),
        in_specs=[VMEM] * 7,
        out_specs=(VMEM, VMEM),
        scratch_shapes=last_scratch(count, own_seg),
        cost_estimate=pair_cost(count // 4, own_seg),
        compiler_params=params,
    )(value, *own, *sums)


def solution(mesh):
    split = P(None, ("group", "src"))
    return jax.shard_map(
        on_device, mesh=mesh, in_specs=(split,) * 6 + (P("group"),), out_specs=(split, split), check_vma=False
    )
```

```python
import functools
import math

import jax
import jax.numpy as jnp
from jax import lax
from jax.experimental import pallas as pl
from jax.experimental.pallas import tpu as pltpu
from jax.sharding import PartitionSpec as P

core_term = 0.05
inverse_four_pi = 0.25 / math.pi

LANES = 128
ROWS = 24
CHUNK = 64
FINISH = 32
VMEM = pl.BlockSpec(memory_space=pltpu.VMEM)


def exchange_masks(count):
    masks = []
    step = count // 2
    while step > 1:
        masks.append(step + 1)
        step //= 2
    return masks + [1]


def mask_at(place, masks):
    value = 0
    for bit, mask in enumerate(masks):
        if place >> bit & 1:
            value ^= mask
    return value


def place_of(value, masks):
    place = 0
    rest = value & 1
    for bit, mask in enumerate(masks[:-1]):
        taken = lax.shift_right_logical(value, mask.bit_length() - 1) & 1
        place = place + taken * (1 << bit)
        rest = rest ^ taken
    return place + rest * (1 << (len(masks) - 1))


def high_low(value):
    high = value.astype(jnp.bfloat16).astype(jnp.float32)
    return high, value - high


def dot_nt(left, right):
    return lax.dot_general(left, right, (((1,), (1,)), ((), ())), preferred_element_type=jnp.float32)


def cross(a, b):
    return (a[1] * b[2] - a[2] * b[1], a[2] * b[0] - a[0] * b[2], a[0] * b[1] - a[1] * b[0])


def pair_terms(point, normal, moment, first, segment, turn, span, span_core, scale, want_span):
    rel = tuple(p - e for p, e in zip(point, first))
    cross_n = (moment[0] * segment[0] + moment[1] * segment[1] + moment[2] * segment[2]) - (
        normal[0] * turn[0] + normal[1] * turn[1] + normal[2] * turn[2]
    )
    dist_sq = rel[0] * rel[0] + rel[1] * rel[1] + rel[2] * rel[2]
    along = segment[0] * rel[0] + segment[1] * rel[1] + segment[2] * rel[2]
    other = along - span
    second_sq = dist_sq - along - other
    inv_first = lax.rsqrt(dist_sq)
    inv_second = lax.rsqrt(second_sq)
    inv_den = 1.0 / ((span * dist_sq + span_core) - along * along)
    part_first = along * inv_first
    part_second = other * inv_second
    line = part_first - part_second
    scaled = scale * inv_den
    by_normal = scaled * line
    by_line = scaled * cross_n
    by_den = (by_normal * cross_n) * inv_den
    by_den2 = by_den + by_den
    cube_first = part_first * (inv_first * inv_first)
    cube_second = part_second * (inv_second * inv_second)
    by_dist2 = by_line * (cube_second - cube_first) - by_den2 * span
    by_along = by_line * ((inv_first - inv_second) - cube_second) + by_den2 * along
    if not want_span:
        return rel, by_normal, by_dist2, by_along
    by_span2 = by_line * ((inv_second + inv_second) + cube_second) - by_den2 * (dist_sq + core_term)
    return rel, by_normal, by_dist2, by_along, by_span2


def segment_terms(first, second):
    segment = tuple(b - a for a, b in zip(first, second))
    span = segment[0] * segment[0] + segment[1] * segment[1] + segment[2] * segment[2]
    return segment, cross(segment, first), span, core_term * span + core_term


def pack_kernel(own_seg, points_ref, normals_ref, left_ref, vertices_ref, connect_ref, right_ref, weights_ref, out_ref):
    base = lax.axis_index("src") * own_seg
    row8 = lax.broadcasted_iota(jnp.int32, (8, LANES), 0)
    weight = jnp.zeros((8, LANES), jnp.float32)
    for mode in range(8):
        weight = jnp.where(row8 == mode, weights_ref[mode], weight)
    weighted = right_ref[...] * (weight * inverse_four_pi)
    high, rest = high_low(weighted)
    middle, low = high_low(rest)
    parts = jnp.concatenate([high, middle, low, jnp.zeros_like(low)], 0).astype(jnp.bfloat16)
    local = connect_ref[0:1, :] - base
    hit = lax.broadcasted_iota(jnp.int32, (LANES, LANES), 0) == local
    folded = dot_nt(parts, hit.astype(jnp.float32).astype(jnp.bfloat16))
    folded = folded[0:8] + (folded[8:16] + folded[16:24])
    out_ref[0:8, :] = left_ref[...]
    out_ref[8:10, :] = points_ref[0:2, :]
    out_ref[10:11, :] = 0.5 + 0.2 * points_ref[2:3, :]
    out_ref[11:14, :] = normals_ref[...]
    out_ref[14:16, :] = jnp.zeros((2, LANES), jnp.float32)
    out_ref[16:24, :] = folded
    out_ref[16:18, own_seg : 2 * own_seg] = vertices_ref[0:2, :]
    out_ref[18:19, own_seg : 2 * own_seg] = 0.2 * vertices_ref[2:3, :]


def stack_hhll(rows):
    high, low = high_low(rows)
    return jnp.transpose(jnp.concatenate([high, high, low, low], 0)).astype(jnp.bfloat16)


def stack_hlhl(rows):
    high, low = high_low(rows)
    both = jnp.concatenate([high, low], 0).astype(jnp.bfloat16)
    return jnp.concatenate([both, both], 0)


def lane_edges(own_seg):
    lane = lax.broadcasted_iota(jnp.int32, (1, LANES), 1)
    return (lane == own_seg - 1) | (lane == 2 * own_seg - 1)


def own_kernel(own_seg, data_ref, col1_ref, col2_ref, left_ref, right_ref):
    def columns(rows, out_ref):
        pad = jnp.zeros((16 - len(rows), LANES), jnp.float32)
        cols = jnp.transpose(jnp.concatenate(list(rows) + [pad], 0))
        count = out_ref.shape[1]
        for k in range(len(rows)):
            out_ref[k] = jnp.broadcast_to(cols[0:count, k : k + 1], (count, LANES))

    own_block = data_ref[0, 16:24, :]
    point, normal, moment = own_receivers(data_ref)
    columns([*point, *normal, *moment], col1_ref)
    own_e, own_s, own_t, span, span_core = own_segments(own_block, own_seg)
    columns([*own_e, *own_s, *own_t, span, span_core], col2_ref)
    left_ref[...] = stack_hhll(data_ref[0, 0:8, :])
    right_ref[...] = stack_hhll(jnp.where(lane_edges(own_seg), 0.0, own_block))[0:own_seg]


def pair_sums(data_ref, own_refs, begin, end, own_seg, scratch, old1, old2, new1, new2, between=None):
    seg_ref, rec_ref, scale1_ref, scale2_ref = scratch
    col1_ref, col2_ref, left_ref, right_ref = own_refs
    blocks = end - begin
    tiles = blocks // 2
    lane = lax.broadcasted_iota(jnp.int32, (1, LANES), 1)
    low_half = lane < own_seg
    at_edge = lane_edges(own_seg)

    folded = []
    for tile in range(tiles):
        block_a, block_b = data_ref[begin + 2 * tile, 16:24, :], data_ref[begin + 2 * tile + 1, 16:24, :]
        both = jnp.where(low_half, block_a, pltpu.roll(block_b, own_seg, 1))
        folded.append(jnp.where(at_edge, 0.0, both))
        first = jnp.where(low_half, pltpu.roll(block_a, own_seg, 1), block_b)
        second = jnp.where(at_edge, first, pltpu.roll(first, LANES - 1, 1))
        for axis in range(3):
            seg_ref[axis, tile : tile + 1, :] = first[axis : axis + 1]
            seg_ref[3 + axis, tile : tile + 1, :] = second[axis : axis + 1]
    first = tuple(seg_ref[axis] for axis in range(3))
    segment, turn, span, span_core = segment_terms(first, tuple(seg_ref[3 + axis] for axis in range(3)))
    for axis in range(3):
        seg_ref[3 + axis] = segment[axis]
        seg_ref[6 + axis] = turn[axis]
    seg_ref[9] = span
    seg_ref[10] = span_core

    point = tuple(data_ref[begin:end, 8 + axis, :] for axis in range(3))
    normal = tuple(data_ref[begin:end, 11 + axis, :] for axis in range(3))
    moment = cross(point, normal)
    for axis in range(3):
        rec_ref[axis] = point[axis]
        rec_ref[3 + axis] = normal[axis]
        rec_ref[6 + axis] = moment[axis]

    scale1_ref[...] = jnp.dot(
        left_ref[...], stack_hlhl(jnp.concatenate(folded, 1)), preferred_element_type=jnp.float32)
    scale2_ref[...] = jnp.dot(
        right_ref[...], stack_hlhl(jnp.concatenate([data_ref[b, 0:8, :] for b in range(begin, end)], 1)),
        preferred_element_type=jnp.float32)

    def initial(old, count, start):
        if old is None:
            return [jnp.zeros((CHUNK, LANES), jnp.float32) for _ in range(count)]
        return [old[k, start : start + CHUNK, :] for k in range(count)]

    for start in range(0, LANES, CHUNK):
        col = [col1_ref[k, start : start + CHUNK, :] for k in range(9)]
        sums = initial(old1, 9, start)
        for tile in range(tiles):
            row = [seg_ref[k, tile : tile + 1, :] for k in range(11)]
            scale = scale1_ref[start : start + CHUNK, tile * LANES : (tile + 1) * LANES]
            rel, by_normal, by_dist2, by_along = pair_terms(
                col[0:3], col[3:6], col[6:9], row[0:3], row[3:6], row[6:9], row[9], row[10], scale, False)
            for axis in range(3):
                sums[axis] += by_normal * row[3 + axis]
                sums[3 + axis] += by_normal * row[6 + axis]
                sums[6 + axis] += by_dist2 * rel[axis] + by_along * row[3 + axis]
        for k in range(9):
            new1[k, start : start + CHUNK, :] = sums[k]

    if between is not None:
        between()

    for start in range(0, own_seg, CHUNK):
        col = [col2_ref[k, start : start + CHUNK, :] for k in range(11)]
        sums = initial(old2, 11, start)
        for block in range(blocks):
            row = [rec_ref[k, block : block + 1, :] for k in range(9)]
            scale = scale2_ref[start : start + CHUNK, block * LANES : (block + 1) * LANES]
            rel, by_normal, by_dist2, by_along, by_span2 = pair_terms(
                row[0:3], row[3:6], row[6:9], col[0:3], col[3:6], col[6:9], col[9], col[10], scale, True)
            for axis in range(3):
                sums[axis] += by_normal * row[3 + axis]
                sums[3 + axis] += by_normal * row[6 + axis] + by_along * rel[axis]
                sums[6 + axis] += by_dist2 * rel[axis]
            sums[9] += by_along
            sums[10] += by_span2
        for k in range(11):
            new2[k, start : start + CHUNK, :] = sums[k]


def lane_sums(values):
    rows = values[0].shape[0]
    column = lax.broadcasted_iota(jnp.int32, (rows, 16), 1)
    result = jnp.zeros((rows, 16), jnp.float32)
    for index, value in enumerate(values):
        result = jnp.where(column == index, jnp.sum(value, axis=1, keepdims=True), result)
    return result


def receiver_totals(sums_ref, col_ref):
    parts = []
    for start in range(0, LANES, FINISH):
        sums = [sums_ref[k, start : start + FINISH, :] for k in range(9)]
        col = [col_ref[k, start : start + FINISH, :] for k in range(6)]
        by_point = [a + b for a, b in zip(cross(col[3:6], sums[0:3]), sums[6:9])]
        by_normal = [a - b for a, b in zip(cross(sums[0:3], col[0:3]), sums[3:6])]
        parts.append(lane_sums(by_point + by_normal))
    return jnp.transpose(jnp.concatenate(parts, 0))


def segment_totals(sums_ref, col_ref, own_seg, arriving, leaving):
    parts = []
    for start in range(0, own_seg, FINISH):
        sums = [sums_ref[k, start : start + FINISH, :] for k in range(11)]
        col = [col_ref[k, start : start + FINISH, :] for k in range(6)]
        turned, swept = cross(col[0:3], sums[0:3]), cross(sums[0:3], col[3:6])
        by_s = [sums[3 + k] - turned[k] + col[3 + k] * sums[10] for k in range(3)]
        by_both = [by_s[k] + (swept[k] + sums[6 + k] + col[3 + k] * sums[9]) for k in range(3)]
        if start + FINISH == own_seg:
            last = lax.broadcasted_iota(jnp.int32, (FINISH, LANES), 0) == FINISH - 1
            by_s = [jnp.where(last, a, b) for a, b in zip(arriving, by_s)]
            by_both = [jnp.where(last, a, b) for a, b in zip(leaving, by_both)]
        parts.append(lane_sums(by_s + by_both))
    return jnp.transpose(jnp.concatenate(parts, 0))


def own_receivers(data_ref):
    point = tuple(data_ref[0, 8 + axis : 9 + axis, :] for axis in range(3))
    normal = tuple(data_ref[0, 11 + axis : 12 + axis, :] for axis in range(3))
    return point, normal, cross(point, normal)


def own_segments(own_block, own_seg):
    lane = lax.broadcasted_iota(jnp.int32, (1, LANES), 1)
    first = pltpu.roll(own_block, own_seg, 1)
    second = jnp.where(lane == own_seg - 1, first, pltpu.roll(first, LANES - 1, 1))
    own_e = tuple(first[axis : axis + 1] for axis in range(3))
    segment, turn, span, span_core = segment_terms(own_e, tuple(second[axis : axis + 1] for axis in range(3)))
    return own_e, segment, turn, span, span_core


def early_kernel(chained, own_seg, *refs):
    data_ref, own_refs, rest = refs[0], refs[1:5], refs[5:]
    olds = rest[0:2] if chained else (None, None)
    rest = rest[2:] if chained else rest
    pair_sums(data_ref, own_refs, 0, data_ref.shape[0], own_seg, rest[2:], *olds, rest[0], rest[1])


def last_kernel(count, own_seg, *refs):
    data_ref, own_refs, old1_ref, old2_ref, rcv_out, vert_out, after_ref, new1_ref, new2_ref = (
        refs[0], refs[1:5], *refs[5:12])
    scratch = refs[12:]
    masks = exchange_masks(count)
    me = lax.axis_index("src")
    lane = lax.broadcasted_iota(jnp.int32, (1, LANES), 1)

    def place(device):
        return place_of((device & (count - 1)) ^ me, masks)

    def edge_sums():
        for block in range(count):
            after_ref[block] = data_ref[place((me ^ mask_at(block, masks)) + 1), 16:24, :]

        def spread(column):
            return jnp.broadcast_to(column, (column.shape[0], LANES))

        own_block = data_ref[0, 16:24, :]
        before = data_ref[place(me + count - 1), 16:24, :]
        own_p, own_n, own_m = own_receivers(data_ref)
        point = tuple(data_ref[:, 8 + axis, :] for axis in range(3))
        normal = tuple(data_ref[:, 11 + axis, :] for axis in range(3))
        moment = cross(point, normal)
        mine_last = spread(own_block[:, 2 * own_seg - 1 : 2 * own_seg])
        mine_next = spread(after_ref[0, :, own_seg : own_seg + 1])
        mine_weight = spread(own_block[:, own_seg - 1 : own_seg])
        before_last = spread(before[:, 2 * own_seg - 1 : 2 * own_seg])
        before_weight = spread(jnp.where(me == 0, 0.0, before[:, own_seg - 1 : own_seg]))
        mine_first = spread(own_block[:, own_seg : own_seg + 1])

        def rows(value, axis):
            return jnp.broadcast_to(value[axis : axis + 1], (count, LANES))

        def stacked(own, every):
            return tuple(
                jnp.concatenate([jnp.broadcast_to(a, (count, LANES)), b, b], 0) for a, b in zip(own, every))

        first = tuple(
            jnp.concatenate(
                [spread(data_ref[:, 16 + axis, 2 * own_seg - 1 : 2 * own_seg]), rows(mine_last, axis), rows(before_last, axis)], 0)
            for axis in range(3))
        second = tuple(
            jnp.concatenate(
                [spread(after_ref[:, axis, own_seg : own_seg + 1]), rows(mine_next, axis), rows(mine_first, axis)], 0)
            for axis in range(3))
        scales = [jnp.zeros((count, LANES), jnp.float32)] * 3
        for mode in range(8):
            left = data_ref[:, mode, :]
            scales[0] += spread(data_ref[:, 16 + mode, own_seg - 1 : own_seg]) * data_ref[0, mode : mode + 1, :]
            scales[1] += mine_weight[mode : mode + 1] * left
            scales[2] += before_weight[mode : mode + 1] * left
        segment, turn, span, span_core = segment_terms(first, second)
        normals = stacked(own_n, normal)
        rel, by_normal, by_dist2, by_along, by_span2 = pair_terms(
            stacked(own_p, point), normals, stacked(own_m, moment),
            first, segment, turn, span, span_core, jnp.concatenate(scales, 0), True)

        def down(value):
            return jnp.sum(value, axis=0, keepdims=True)

        against_own, mine, ahead = slice(0, count), slice(count, 2 * count), slice(2 * count, 3 * count)
        swung, swept = cross(rel, normals), cross(normals, segment)
        edge_s = [(by_normal * segment[axis])[against_own] for axis in range(3)]
        edge_t = [(by_normal * turn[axis])[against_own] for axis in range(3)]
        edge_point = [a for a in cross(own_n, edge_s)]
        edge_normal = [down(a - b) for a, b in zip(cross(edge_s, own_p), edge_t)]
        leaving, arriving = [], []
        for axis in range(3):
            by_s = by_normal * swung[axis] + by_along * rel[axis] + by_span2 * segment[axis]
            by_p = by_dist2 * rel[axis] + by_along * segment[axis]
            by_r = by_normal * swept[axis] + by_p
            edge_point[axis] = down(edge_point[axis] + by_p[against_own])
            leaving.append(down((by_s + by_r)[mine]))
            arriving.append(down(by_s[ahead]))
        return edge_point, edge_normal, arriving, leaving

    found = []
    pair_sums(
        data_ref, own_refs, count - count // 4, count, own_seg, scratch, old1_ref, old2_ref, new1_ref, new2_ref,
        lambda: found.extend((*edge_sums(), receiver_totals(new1_ref, own_refs[0]))))
    edge_point, edge_normal, arriving, leaving, totals = found
    for axis in range(3):
        value = totals[axis : axis + 1] + edge_point[axis]
        rcv_out[axis : axis + 1, :] = 0.2 * value if axis == 2 else value
        rcv_out[3 + axis : 4 + axis, :] = totals[3 + axis : 4 + axis] + edge_normal[axis]

    totals = segment_totals(new2_ref, own_refs[1], own_seg, arriving, leaving)
    for axis in range(3):
        by_second = totals[axis : axis + 1]
        shifted = jnp.concatenate([by_second[:, own_seg - 1 :], by_second[:, : own_seg - 1]], 1)
        result = shifted - totals[3 + axis : 4 + axis]
        vert_out[axis : axis + 1, :] = 0.2 * result if axis == 2 else result


def pair_scratch(blocks, own_seg):
    return [
        pltpu.VMEM((11, blocks // 2, LANES), jnp.float32),
        pltpu.VMEM((9, blocks, LANES), jnp.float32),
        pltpu.VMEM((LANES, blocks // 2 * LANES), jnp.float32),
        pltpu.VMEM((own_seg, blocks * LANES), jnp.float32),
    ]


def sum_shapes(own_seg):
    return [pltpu.VMEM((9, LANES, LANES), jnp.float32), pltpu.VMEM((11, own_seg, LANES), jnp.float32)]


def last_scratch(count, own_seg):
    return [pltpu.VMEM((count, 8, LANES), jnp.float32)] + sum_shapes(own_seg) + pair_scratch(count // 4, own_seg)


def pair_cost(blocks, own_seg):
    pairs = 2 * blocks * own_seg * LANES
    return pl.CostEstimate(flops=100 * pairs, bytes_accessed=blocks * ROWS * LANES * 4, transcendentals=3 * pairs)


def on_device(rcv_points, rcv_normals, left_modes, vertices, connect, right_modes, mode_weights):
    count = lax.axis_size("src")
    own_seg = vertices.shape[1]
    value = pl.pallas_call(
        functools.partial(pack_kernel, own_seg),
        out_shape=pltpu.VMEM((ROWS, LANES), jnp.float32),
        in_specs=[VMEM] * 6 + [pl.BlockSpec(memory_space=pltpu.SMEM)],
        out_specs=VMEM,
    )(rcv_points, rcv_normals, left_modes, vertices, connect, right_modes, mode_weights)[None]
    params = pltpu.CompilerParams(vmem_limit_bytes=24 << 20)
    own = pl.pallas_call(
        functools.partial(own_kernel, own_seg),
        out_shape=(
            *sum_shapes(own_seg),
            pltpu.VMEM((LANES, 32), jnp.bfloat16),
            pltpu.VMEM((own_seg, 32), jnp.bfloat16),
        ),
        in_specs=[VMEM],
        out_specs=(VMEM,) * 4,
        cost_estimate=pair_cost(2, own_seg),
        compiler_params=params,
    )(value)

    def exchange(block, mask):
        return lax.ppermute(block, "src", [(s, s ^ mask) for s in range(count)])

    def add_pairs(block, *sums):
        return pl.pallas_call(
            functools.partial(early_kernel, len(sums) > 0, own_seg),
            out_shape=tuple(sum_shapes(own_seg)),
            in_specs=[VMEM] * (5 + len(sums)),
            out_specs=(VMEM, VMEM),
            scratch_shapes=pair_scratch(block.shape[0], own_seg),
            cost_estimate=pair_cost(block.shape[0], own_seg),
            compiler_params=params,
        )(block, *own, *sums)

    masks = exchange_masks(count)
    for mask in masks[:-3]:
        value = jnp.concatenate([value, exchange(value, mask)], 0)
    arrived, early = exchange(value, masks[-3]), exchange(value, masks[-2])
    late = exchange(arrived, masks[-2])
    value = jnp.concatenate([value, arrived], 0)
    beside = exchange(value, masks[-1])
    sums = add_pairs(value)
    sums = add_pairs(beside, *sums)
    late, sums = lax.optimization_barrier((late, sums))
    across = jnp.concatenate([early, late], 0)
    opposite = exchange(across, masks[-1])
    sums = add_pairs(across, *sums)
    value = jnp.concatenate([value, across, beside, opposite], 0)
    return pl.pallas_call(
        functools.partial(last_kernel, count, own_seg),
        out_shape=(
            jax.ShapeDtypeStruct((6, LANES), jnp.float32),
            jax.ShapeDtypeStruct((3, own_seg), jnp.float32),
        ),
        in_specs=[VMEM] * 7,
        out_specs=(VMEM, VMEM),
        scratch_shapes=last_scratch(count, own_seg),
        cost_estimate=pair_cost(count // 4, own_seg),
        compiler_params=params,
    )(value, *own, *sums)


def solution(mesh):
    split = P(None, ("group", "src"))
    return jax.shard_map(
        on_device, mesh=mesh, in_specs=(split,) * 6 + (P("group"),), out_specs=(split, split), check_vma=False
    )
```

```python
import functools
import math

import jax
import jax.numpy as jnp
from jax import lax
from jax.experimental import pallas as pl
from jax.experimental.pallas import tpu as pltpu
from jax.sharding import PartitionSpec as P

core_term = 0.05
inverse_four_pi = 0.25 / math.pi

LANES = 128
ROWS = 24
CHUNK = 64
FINISH = 32
VMEM = pl.BlockSpec(memory_space=pltpu.VMEM)


def exchange_masks(count):
    masks = []
    step = count // 2
    while step > 1:
        masks.append(step + 1)
        step //= 2
    return masks + [1]


def mask_at(place, masks):
    value = 0
    for bit, mask in enumerate(masks):
        if place >> bit & 1:
            value ^= mask
    return value


def place_of(value, masks):
    place = 0
    rest = value & 1
    for bit, mask in enumerate(masks[:-1]):
        taken = lax.shift_right_logical(value, mask.bit_length() - 1) & 1
        place = place + taken * (1 << bit)
        rest = rest ^ taken
    return place + rest * (1 << (len(masks) - 1))


def high_low(value):
    high = value.astype(jnp.bfloat16).astype(jnp.float32)
    return high, value - high


def dot_nt(left, right):
    return lax.dot_general(left, right, (((1,), (1,)), ((), ())), preferred_element_type=jnp.float32)


def cross(a, b):
    return (a[1] * b[2] - a[2] * b[1], a[2] * b[0] - a[0] * b[2], a[0] * b[1] - a[1] * b[0])


def pair_terms(point, normal, moment, first, segment, turn, span, span_core, scale, want_span):
    rel = tuple(p - e for p, e in zip(point, first))
    cross_n = (moment[0] * segment[0] + moment[1] * segment[1] + moment[2] * segment[2]) - (
        normal[0] * turn[0] + normal[1] * turn[1] + normal[2] * turn[2]
    )
    dist_sq = rel[0] * rel[0] + rel[1] * rel[1] + rel[2] * rel[2]
    along = segment[0] * rel[0] + segment[1] * rel[1] + segment[2] * rel[2]
    other = along - span
    second_sq = dist_sq - along - other
    inv_first = lax.rsqrt(dist_sq)
    inv_second = lax.rsqrt(second_sq)
    inv_den = 1.0 / ((span * dist_sq + span_core) - along * along)
    part_first = along * inv_first
    part_second = other * inv_second
    line = part_first - part_second
    scaled = scale * inv_den
    by_normal = scaled * line
    by_line = scaled * cross_n
    by_den = (by_normal * cross_n) * inv_den
    by_den2 = by_den + by_den
    cube_first = part_first * (inv_first * inv_first)
    cube_second = part_second * (inv_second * inv_second)
    by_dist2 = by_line * (cube_second - cube_first) - by_den2 * span
    by_along = by_line * ((inv_first - inv_second) - cube_second) + by_den2 * along
    if not want_span:
        return rel, by_normal, by_dist2, by_along
    by_span2 = by_line * ((inv_second + inv_second) + cube_second) - by_den2 * (dist_sq + core_term)
    return rel, by_normal, by_dist2, by_along, by_span2


def segment_terms(first, second):
    segment = tuple(b - a for a, b in zip(first, second))
    span = segment[0] * segment[0] + segment[1] * segment[1] + segment[2] * segment[2]
    return segment, cross(segment, first), span, core_term * span + core_term


def pack_kernel(own_seg, points_ref, normals_ref, left_ref, vertices_ref, connect_ref, right_ref, weights_ref, out_ref):
    base = lax.axis_index("src") * own_seg
    row8 = lax.broadcasted_iota(jnp.int32, (8, LANES), 0)
    weight = jnp.zeros((8, LANES), jnp.float32)
    for mode in range(8):
        weight = jnp.where(row8 == mode, weights_ref[mode], weight)
    weighted = right_ref[...] * (weight * inverse_four_pi)
    high, rest = high_low(weighted)
    middle, low = high_low(rest)
    parts = jnp.concatenate([high, middle, low, jnp.zeros_like(low)], 0).astype(jnp.bfloat16)
    local = connect_ref[0:1, :] - base
    hit = lax.broadcasted_iota(jnp.int32, (LANES, LANES), 0) == local
    folded = dot_nt(parts, hit.astype(jnp.float32).astype(jnp.bfloat16))
    folded = folded[0:8] + (folded[8:16] + folded[16:24])
    out_ref[0:8, :] = left_ref[...]
    out_ref[8:10, :] = points_ref[0:2, :]
    out_ref[10:11, :] = 0.5 + 0.2 * points_ref[2:3, :]
    out_ref[11:14, :] = normals_ref[...]
    out_ref[14:16, :] = jnp.zeros((2, LANES), jnp.float32)
    out_ref[16:24, :] = folded
    out_ref[16:18, own_seg : 2 * own_seg] = vertices_ref[0:2, :]
    out_ref[18:19, own_seg : 2 * own_seg] = 0.2 * vertices_ref[2:3, :]


def stack_hhll(rows):
    high, low = high_low(rows)
    return jnp.transpose(jnp.concatenate([high, high, low, low], 0)).astype(jnp.bfloat16)


def stack_hlhl(rows):
    high, low = high_low(rows)
    both = jnp.concatenate([high, low], 0).astype(jnp.bfloat16)
    return jnp.concatenate([both, both], 0)


def lane_edges(own_seg):
    lane = lax.broadcasted_iota(jnp.int32, (1, LANES), 1)
    return (lane == own_seg - 1) | (lane == 2 * own_seg - 1)


def own_kernel(own_seg, data_ref, col1_ref, col2_ref, left_ref, right_ref):
    def columns(rows, out_ref):
        pad = jnp.zeros((16 - len(rows), LANES), jnp.float32)
        cols = jnp.transpose(jnp.concatenate(list(rows) + [pad], 0))
        count = out_ref.shape[1]
        for k in range(len(rows)):
            out_ref[k] = jnp.broadcast_to(cols[0:count, k : k + 1], (count, LANES))

    own_block = data_ref[0, 16:24, :]
    point, normal, moment = own_receivers(data_ref)
    columns([*point, *normal, *moment], col1_ref)
    own_e, own_s, own_t, span, span_core = own_segments(own_block, own_seg)
    columns([*own_e, *own_s, *own_t, span, span_core], col2_ref)
    left_ref[...] = stack_hhll(data_ref[0, 0:8, :])
    right_ref[...] = stack_hhll(jnp.where(lane_edges(own_seg), 0.0, own_block))[0:own_seg]


def pair_sums(data_ref, own_refs, begin, end, own_seg, scratch, old1, old2, new1, new2, between=None):
    seg_ref, rec_ref, scale1_ref, scale2_ref = scratch
    col1_ref, col2_ref, left_ref, right_ref = own_refs
    blocks = end - begin
    tiles = blocks // 2
    lane = lax.broadcasted_iota(jnp.int32, (1, LANES), 1)
    low_half = lane < own_seg
    at_edge = lane_edges(own_seg)

    folded = []
    for tile in range(tiles):
        block_a, block_b = data_ref[begin + 2 * tile, 16:24, :], data_ref[begin + 2 * tile + 1, 16:24, :]
        both = jnp.where(low_half, block_a, pltpu.roll(block_b, own_seg, 1))
        folded.append(jnp.where(at_edge, 0.0, both))
        first = jnp.where(low_half, pltpu.roll(block_a, own_seg, 1), block_b)
        second = jnp.where(at_edge, first, pltpu.roll(first, LANES - 1, 1))
        for axis in range(3):
            seg_ref[axis, tile : tile + 1, :] = first[axis : axis + 1]
            seg_ref[3 + axis, tile : tile + 1, :] = second[axis : axis + 1]
    first = tuple(seg_ref[axis] for axis in range(3))
    segment, turn, span, span_core = segment_terms(first, tuple(seg_ref[3 + axis] for axis in range(3)))
    for axis in range(3):
        seg_ref[3 + axis] = segment[axis]
        seg_ref[6 + axis] = turn[axis]
    seg_ref[9] = span
    seg_ref[10] = span_core

    point = tuple(data_ref[begin:end, 8 + axis, :] for axis in range(3))
    normal = tuple(data_ref[begin:end, 11 + axis, :] for axis in range(3))
    moment = cross(point, normal)
    for axis in range(3):
        rec_ref[axis] = point[axis]
        rec_ref[3 + axis] = normal[axis]
        rec_ref[6 + axis] = moment[axis]

    scale1_ref[...] = jnp.dot(
        left_ref[...], stack_hlhl(jnp.concatenate(folded, 1)), preferred_element_type=jnp.float32)
    scale2_ref[...] = jnp.dot(
        right_ref[...], stack_hlhl(jnp.concatenate([data_ref[b, 0:8, :] for b in range(begin, end)], 1)),
        preferred_element_type=jnp.float32)

    def initial(old, count, start):
        if old is None:
            return [jnp.zeros((CHUNK, LANES), jnp.float32) for _ in range(count)]
        return [old[k, start : start + CHUNK, :] for k in range(count)]

    for start in range(0, LANES, CHUNK):
        col = [col1_ref[k, start : start + CHUNK, :] for k in range(9)]
        sums = initial(old1, 9, start)
        for tile in range(tiles):
            row = [seg_ref[k, tile : tile + 1, :] for k in range(11)]
            scale = scale1_ref[start : start + CHUNK, tile * LANES : (tile + 1) * LANES]
            rel, by_normal, by_dist2, by_along = pair_terms(
                col[0:3], col[3:6], col[6:9], row[0:3], row[3:6], row[6:9], row[9], row[10], scale, False)
            for axis in range(3):
                sums[axis] += by_normal * row[3 + axis]
                sums[3 + axis] += by_normal * row[6 + axis]
                sums[6 + axis] += by_dist2 * rel[axis] + by_along * row[3 + axis]
        for k in range(9):
            new1[k, start : start + CHUNK, :] = sums[k]

    if between is not None:
        between()

    for start in range(0, own_seg, CHUNK):
        col = [col2_ref[k, start : start + CHUNK, :] for k in range(11)]
        sums = initial(old2, 11, start)
        for block in range(blocks):
            row = [rec_ref[k, block : block + 1, :] for k in range(9)]
            scale = scale2_ref[start : start + CHUNK, block * LANES : (block + 1) * LANES]
            rel, by_normal, by_dist2, by_along, by_span2 = pair_terms(
                row[0:3], row[3:6], row[6:9], col[0:3], col[3:6], col[6:9], col[9], col[10], scale, True)
            for axis in range(3):
                sums[axis] += by_normal * row[3 + axis]
                sums[3 + axis] += by_normal * row[6 + axis] + by_along * rel[axis]
                sums[6 + axis] += by_dist2 * rel[axis]
            sums[9] += by_along
            sums[10] += by_span2
        for k in range(11):
            new2[k, start : start + CHUNK, :] = sums[k]


def lane_sums(values):
    rows = values[0].shape[0]
    column = lax.broadcasted_iota(jnp.int32, (rows, 16), 1)
    result = jnp.zeros((rows, 16), jnp.float32)
    for index, value in enumerate(values):
        result = jnp.where(column == index, jnp.sum(value, axis=1, keepdims=True), result)
    return result


def receiver_totals(sums_ref, col_ref):
    parts = []
    for start in range(0, LANES, FINISH):
        sums = [sums_ref[k, start : start + FINISH, :] for k in range(9)]
        col = [col_ref[k, start : start + FINISH, :] for k in range(6)]
        by_point = [a + b for a, b in zip(cross(col[3:6], sums[0:3]), sums[6:9])]
        by_normal = [a - b for a, b in zip(cross(sums[0:3], col[0:3]), sums[3:6])]
        parts.append(lane_sums(by_point + by_normal))
    return jnp.transpose(jnp.concatenate(parts, 0))


def segment_totals(sums_ref, col_ref, own_seg, arriving, leaving):
    parts = []
    for start in range(0, own_seg, FINISH):
        sums = [sums_ref[k, start : start + FINISH, :] for k in range(11)]
        col = [col_ref[k, start : start + FINISH, :] for k in range(6)]
        turned, swept = cross(col[0:3], sums[0:3]), cross(sums[0:3], col[3:6])
        by_s = [sums[3 + k] - turned[k] + col[3 + k] * sums[10] for k in range(3)]
        by_both = [by_s[k] + (swept[k] + sums[6 + k] + col[3 + k] * sums[9]) for k in range(3)]
        if start + FINISH == own_seg:
            last = lax.broadcasted_iota(jnp.int32, (FINISH, LANES), 0) == FINISH - 1
            by_s = [jnp.where(last, a, b) for a, b in zip(arriving, by_s)]
            by_both = [jnp.where(last, a, b) for a, b in zip(leaving, by_both)]
        parts.append(lane_sums(by_s + by_both))
    return jnp.transpose(jnp.concatenate(parts, 0))


def own_receivers(data_ref):
    point = tuple(data_ref[0, 8 + axis : 9 + axis, :] for axis in range(3))
    normal = tuple(data_ref[0, 11 + axis : 12 + axis, :] for axis in range(3))
    return point, normal, cross(point, normal)


def own_segments(own_block, own_seg):
    lane = lax.broadcasted_iota(jnp.int32, (1, LANES), 1)
    first = pltpu.roll(own_block, own_seg, 1)
    second = jnp.where(lane == own_seg - 1, first, pltpu.roll(first, LANES - 1, 1))
    own_e = tuple(first[axis : axis + 1] for axis in range(3))
    segment, turn, span, span_core = segment_terms(own_e, tuple(second[axis : axis + 1] for axis in range(3)))
    return own_e, segment, turn, span, span_core


def early_kernel(chained, own_seg, *refs):
    data_ref, own_refs, rest = refs[0], refs[1:5], refs[5:]
    olds = rest[0:2] if chained else (None, None)
    rest = rest[2:] if chained else rest
    pair_sums(data_ref, own_refs, 0, data_ref.shape[0], own_seg, rest[2:], *olds, rest[0], rest[1])


def last_kernel(count, own_seg, *refs):
    data_ref, own_refs, old1_ref, old2_ref, rcv_out, vert_out, after_ref, new1_ref, new2_ref = (
        refs[0], refs[1:5], *refs[5:12])
    scratch = refs[12:]
    masks = exchange_masks(count)
    me = lax.axis_index("src")
    lane = lax.broadcasted_iota(jnp.int32, (1, LANES), 1)

    def place(device):
        return place_of((device & (count - 1)) ^ me, masks)

    def edge_sums():
        for block in range(count):
            after_ref[block] = data_ref[place((me ^ mask_at(block, masks)) + 1), 16:24, :]

        def spread(column):
            return jnp.broadcast_to(column, (column.shape[0], LANES))

        own_block = data_ref[0, 16:24, :]
        before = data_ref[place(me + count - 1), 16:24, :]
        own_p, own_n, own_m = own_receivers(data_ref)
        point = tuple(data_ref[:, 8 + axis, :] for axis in range(3))
        normal = tuple(data_ref[:, 11 + axis, :] for axis in range(3))
        moment = cross(point, normal)
        mine_last = spread(own_block[:, 2 * own_seg - 1 : 2 * own_seg])
        mine_next = spread(after_ref[0, :, own_seg : own_seg + 1])
        mine_weight = spread(own_block[:, own_seg - 1 : own_seg])
        before_last = spread(before[:, 2 * own_seg - 1 : 2 * own_seg])
        before_weight = spread(jnp.where(me == 0, 0.0, before[:, own_seg - 1 : own_seg]))
        mine_first = spread(own_block[:, own_seg : own_seg + 1])

        def rows(value, axis):
            return jnp.broadcast_to(value[axis : axis + 1], (count, LANES))

        def stacked(own, every):
            return tuple(
                jnp.concatenate([jnp.broadcast_to(a, (count, LANES)), b, b], 0) for a, b in zip(own, every))

        first = tuple(
            jnp.concatenate(
                [spread(data_ref[:, 16 + axis, 2 * own_seg - 1 : 2 * own_seg]), rows(mine_last, axis), rows(before_last, axis)], 0)
            for axis in range(3))
        second = tuple(
            jnp.concatenate(
                [spread(after_ref[:, axis, own_seg : own_seg + 1]), rows(mine_next, axis), rows(mine_first, axis)], 0)
            for axis in range(3))
        scales = [jnp.zeros((count, LANES), jnp.float32)] * 3
        for mode in range(8):
            left = data_ref[:, mode, :]
            scales[0] += spread(data_ref[:, 16 + mode, own_seg - 1 : own_seg]) * data_ref[0, mode : mode + 1, :]
            scales[1] += mine_weight[mode : mode + 1] * left
            scales[2] += before_weight[mode : mode + 1] * left
        segment, turn, span, span_core = segment_terms(first, second)
        normals = stacked(own_n, normal)
        rel, by_normal, by_dist2, by_along, by_span2 = pair_terms(
            stacked(own_p, point), normals, stacked(own_m, moment),
            first, segment, turn, span, span_core, jnp.concatenate(scales, 0), True)

        def down(value):
            return jnp.sum(value, axis=0, keepdims=True)

        against_own, mine, ahead = slice(0, count), slice(count, 2 * count), slice(2 * count, 3 * count)
        swung, swept = cross(rel, normals), cross(normals, segment)
        edge_s = [(by_normal * segment[axis])[against_own] for axis in range(3)]
        edge_t = [(by_normal * turn[axis])[against_own] for axis in range(3)]
        edge_point = [a for a in cross(own_n, edge_s)]
        edge_normal = [down(a - b) for a, b in zip(cross(edge_s, own_p), edge_t)]
        leaving, arriving = [], []
        for axis in range(3):
            by_s = by_normal * swung[axis] + by_along * rel[axis] + by_span2 * segment[axis]
            by_p = by_dist2 * rel[axis] + by_along * segment[axis]
            by_r = by_normal * swept[axis] + by_p
            edge_point[axis] = down(edge_point[axis] + by_p[against_own])
            leaving.append(down((by_s + by_r)[mine]))
            arriving.append(down(by_s[ahead]))
        return edge_point, edge_normal, arriving, leaving

    found = []
    pair_sums(
        data_ref, own_refs, count - count // 4, count, own_seg, scratch, old1_ref, old2_ref, new1_ref, new2_ref,
        lambda: found.extend((*edge_sums(), receiver_totals(new1_ref, own_refs[0]))))
    edge_point, edge_normal, arriving, leaving, totals = found
    for axis in range(3):
        value = totals[axis : axis + 1] + edge_point[axis]
        rcv_out[axis : axis + 1, :] = 0.2 * value if axis == 2 else value
        rcv_out[3 + axis : 4 + axis, :] = totals[3 + axis : 4 + axis] + edge_normal[axis]

    totals = segment_totals(new2_ref, own_refs[1], own_seg, arriving, leaving)
    for axis in range(3):
        by_second = totals[axis : axis + 1]
        shifted = jnp.concatenate([by_second[:, own_seg - 1 :], by_second[:, : own_seg - 1]], 1)
        result = shifted - totals[3 + axis : 4 + axis]
        vert_out[axis : axis + 1, :] = 0.2 * result if axis == 2 else result


def pair_scratch(blocks, own_seg):
    return [
        pltpu.VMEM((11, blocks // 2, LANES), jnp.float32),
        pltpu.VMEM((9, blocks, LANES), jnp.float32),
        pltpu.VMEM((LANES, blocks // 2 * LANES), jnp.float32),
        pltpu.VMEM((own_seg, blocks * LANES), jnp.float32),
    ]


def sum_shapes(own_seg):
    return [pltpu.VMEM((9, LANES, LANES), jnp.float32), pltpu.VMEM((11, own_seg, LANES), jnp.float32)]


def last_scratch(count, own_seg):
    return [pltpu.VMEM((count, 8, LANES), jnp.float32)] + sum_shapes(own_seg) + pair_scratch(count // 4, own_seg)


def pair_cost(blocks, own_seg):
    pairs = 2 * blocks * own_seg * LANES
    return pl.CostEstimate(flops=100 * pairs, bytes_accessed=blocks * ROWS * LANES * 4, transcendentals=3 * pairs)


def on_device(rcv_points, rcv_normals, left_modes, vertices, connect, right_modes, mode_weights):
    count = lax.axis_size("src")
    own_seg = vertices.shape[1]
    value = pl.pallas_call(
        functools.partial(pack_kernel, own_seg),
        out_shape=pltpu.VMEM((ROWS, LANES), jnp.float32),
        in_specs=[VMEM] * 6 + [pl.BlockSpec(memory_space=pltpu.SMEM)],
        out_specs=VMEM,
    )(rcv_points, rcv_normals, left_modes, vertices, connect, right_modes, mode_weights)[None]
    params = pltpu.CompilerParams(vmem_limit_bytes=24 << 20)
    own = pl.pallas_call(
        functools.partial(own_kernel, own_seg),
        out_shape=(
            *sum_shapes(own_seg),
            pltpu.VMEM((LANES, 32), jnp.bfloat16),
            pltpu.VMEM((own_seg, 32), jnp.bfloat16),
        ),
        in_specs=[VMEM],
        out_specs=(VMEM,) * 4,
        cost_estimate=pair_cost(2, own_seg),
        compiler_params=params,
    )(value)

    def exchange(block, mask):
        return lax.ppermute(block, "src", [(s, s ^ mask) for s in range(count)])

    def add_pairs(block, *sums):
        return pl.pallas_call(
            functools.partial(early_kernel, len(sums) > 0, own_seg),
            out_shape=tuple(sum_shapes(own_seg)),
            in_specs=[VMEM] * (5 + len(sums)),
            out_specs=(VMEM, VMEM),
            scratch_shapes=pair_scratch(block.shape[0], own_seg),
            cost_estimate=pair_cost(block.shape[0], own_seg),
            compiler_params=params,
        )(block, *own, *sums)

    masks = exchange_masks(count)
    for mask in masks[:-3]:
        value = jnp.concatenate([value, exchange(value, mask)], 0)
    arrived, early = exchange(value, masks[-3]), exchange(value, masks[-2])
    late = exchange(arrived, masks[-2])
    value = jnp.concatenate([value, arrived], 0)
    beside = exchange(value, masks[-1])
    value = jnp.concatenate([value, beside], 0)
    sums = add_pairs(value)
    late, sums = lax.optimization_barrier((late, sums))
    across = jnp.concatenate([early, late], 0)
    opposite = exchange(across, masks[-1])
    sums = add_pairs(across, *sums)
    held = count // 4
    value = jnp.concatenate([value[:held], across, value[held:], opposite], 0)
    return pl.pallas_call(
        functools.partial(last_kernel, count, own_seg),
        out_shape=(
            jax.ShapeDtypeStruct((6, LANES), jnp.float32),
            jax.ShapeDtypeStruct((3, own_seg), jnp.float32),
        ),
        in_specs=[VMEM] * 7,
        out_specs=(VMEM, VMEM),
        scratch_shapes=last_scratch(count, own_seg),
        cost_estimate=pair_cost(count // 4, own_seg),
        compiler_params=params,
    )(value, *own, *sums)


def solution(mesh):
    split = P(None, ("group", "src"))
    return jax.shard_map(
        on_device, mesh=mesh, in_specs=(split,) * 6 + (P("group"),), out_specs=(split, split), check_vma=False
    )
```

```python
import functools
import math

import jax
import jax.numpy as jnp
from jax import lax
from jax.experimental import pallas as pl
from jax.experimental.pallas import tpu as pltpu
from jax.sharding import PartitionSpec as P

core_term = 0.05
inverse_four_pi = 0.25 / math.pi

LANES = 128
ROWS = 24
CHUNK = 64
FINISH = 32
VMEM = pl.BlockSpec(memory_space=pltpu.VMEM)


def exchange_masks(count):
    masks = []
    step = count // 2
    while step > 1:
        masks.append(step + 1)
        step //= 2
    return masks + [1]


def mask_at(place, masks):
    value = 0
    for bit, mask in enumerate(masks):
        if place >> bit & 1:
            value ^= mask
    return value


def place_of(value, masks):
    place = 0
    rest = value & 1
    for bit, mask in enumerate(masks[:-1]):
        taken = lax.shift_right_logical(value, mask.bit_length() - 1) & 1
        place = place + taken * (1 << bit)
        rest = rest ^ taken
    return place + rest * (1 << (len(masks) - 1))


def high_low(value):
    high = value.astype(jnp.bfloat16).astype(jnp.float32)
    return high, value - high


def dot_nt(left, right):
    return lax.dot_general(left, right, (((1,), (1,)), ((), ())), preferred_element_type=jnp.float32)


def cross(a, b):
    return (a[1] * b[2] - a[2] * b[1], a[2] * b[0] - a[0] * b[2], a[0] * b[1] - a[1] * b[0])


def normal_cross(normal, moment, segment, turn):
    return (moment[0] * segment[0] + moment[1] * segment[1] + moment[2] * segment[2]) - (
        normal[0] * turn[0] + normal[1] * turn[1] + normal[2] * turn[2]
    )


def pair_terms(point, cross_n, first, segment, span, span_core, scale, want_span):
    rel = tuple(p - e for p, e in zip(point, first))
    dist_sq = rel[0] * rel[0] + rel[1] * rel[1] + rel[2] * rel[2]
    along = segment[0] * rel[0] + segment[1] * rel[1] + segment[2] * rel[2]
    other = along - span
    second_sq = dist_sq - along - other
    inv_first = lax.rsqrt(dist_sq)
    inv_second = lax.rsqrt(second_sq)
    inv_den = 1.0 / ((span * dist_sq + span_core) - along * along)
    part_first = along * inv_first
    part_second = other * inv_second
    line = part_first - part_second
    scaled = scale * inv_den
    by_normal = scaled * line
    by_line = scaled * cross_n
    by_den = (by_normal * cross_n) * inv_den
    by_den2 = by_den + by_den
    cube_first = part_first * (inv_first * inv_first)
    cube_second = part_second * (inv_second * inv_second)
    by_dist2 = by_line * (cube_second - cube_first) - by_den2 * span
    by_along = by_line * ((inv_first - inv_second) - cube_second) + by_den2 * along
    if not want_span:
        return rel, by_normal, by_dist2, by_along
    by_span2 = by_line * ((inv_second + inv_second) + cube_second) - by_den2 * (dist_sq + core_term)
    return rel, by_normal, by_dist2, by_along, by_span2


def segment_terms(first, second):
    segment = tuple(b - a for a, b in zip(first, second))
    span = segment[0] * segment[0] + segment[1] * segment[1] + segment[2] * segment[2]
    return segment, cross(segment, first), span, core_term * span + core_term


def pack_kernel(own_seg, points_ref, normals_ref, left_ref, vertices_ref, connect_ref, right_ref, weights_ref, out_ref):
    base = lax.axis_index("src") * own_seg
    row8 = lax.broadcasted_iota(jnp.int32, (8, LANES), 0)
    weight = jnp.zeros((8, LANES), jnp.float32)
    for mode in range(8):
        weight = jnp.where(row8 == mode, weights_ref[mode], weight)
    weighted = right_ref[...] * (weight * inverse_four_pi)
    high, rest = high_low(weighted)
    middle, low = high_low(rest)
    parts = jnp.concatenate([high, middle, low, jnp.zeros_like(low)], 0).astype(jnp.bfloat16)
    local = connect_ref[0:1, :] - base
    hit = lax.broadcasted_iota(jnp.int32, (LANES, LANES), 0) == local
    folded = dot_nt(parts, hit.astype(jnp.float32).astype(jnp.bfloat16))
    folded = folded[0:8] + (folded[8:16] + folded[16:24])
    out_ref[0:8, :] = left_ref[...]
    out_ref[8:10, :] = points_ref[0:2, :]
    out_ref[10:11, :] = 0.5 + 0.2 * points_ref[2:3, :]
    out_ref[11:14, :] = normals_ref[...]
    out_ref[14:16, :] = jnp.zeros((2, LANES), jnp.float32)
    out_ref[16:24, :] = folded
    out_ref[16:18, own_seg : 2 * own_seg] = vertices_ref[0:2, :]
    out_ref[18:19, own_seg : 2 * own_seg] = 0.2 * vertices_ref[2:3, :]


def stack_hhll(rows):
    high, low = high_low(rows)
    return jnp.transpose(jnp.concatenate([high, high, low, low], 0)).astype(jnp.bfloat16)


def stack_hlhl(rows):
    high, low = high_low(rows)
    both = jnp.concatenate([high, low], 0).astype(jnp.bfloat16)
    return jnp.concatenate([both, both], 0)


def lane_edges(own_seg):
    lane = lax.broadcasted_iota(jnp.int32, (1, LANES), 1)
    return (lane == own_seg - 1) | (lane == 2 * own_seg - 1)


def own_kernel(own_seg, data_ref, col1_ref, col2_ref, left_ref, right_ref, moment_ref, turn_ref):
    def columns(rows, out_ref):
        pad = jnp.zeros((16 - len(rows), LANES), jnp.float32)
        cols = jnp.transpose(jnp.concatenate(list(rows) + [pad], 0))
        count = out_ref.shape[1]
        for k in range(len(rows)):
            out_ref[k] = jnp.broadcast_to(cols[0:count, k : k + 1], (count, LANES))

    own_block = data_ref[0, 16:24, :]
    point, normal, moment = own_receivers(data_ref)
    columns([*point, *normal], col1_ref)
    own_e, own_s, own_t, span, span_core = own_segments(own_block, own_seg)
    columns([*own_e, *own_s, span, span_core], col2_ref)
    left_ref[...] = stack_hhll(data_ref[0, 0:8, :])
    right_ref[...] = stack_hhll(jnp.where(lane_edges(own_seg), 0.0, own_block))[0:own_seg]
    pad = jnp.zeros((2, LANES), jnp.float32)
    moment_ref[...] = stack_hhll(jnp.concatenate([*moment, *normal, pad], 0))
    turn_ref[...] = stack_hhll(jnp.concatenate([*own_s, *(-value for value in own_t), pad], 0))[0:own_seg]


def pair_sums(data_ref, own_refs, begin, end, own_seg, scratch, old1, old2, new1, new2, between=None):
    seg_ref, rec_ref, scale1_ref, scale2_ref, row1_ref, row2_ref, cross1_ref, cross2_ref = scratch
    col1_ref, col2_ref, left_ref, right_ref, moment_ref, turn_ref = own_refs
    blocks = end - begin
    tiles = blocks // 2
    lane = lax.broadcasted_iota(jnp.int32, (1, LANES), 1)
    low_half = lane < own_seg
    at_edge = lane_edges(own_seg)

    folded = []
    for tile in range(tiles):
        block_a, block_b = data_ref[begin + 2 * tile, 16:24, :], data_ref[begin + 2 * tile + 1, 16:24, :]
        both = jnp.where(low_half, block_a, pltpu.roll(block_b, own_seg, 1))
        folded.append(jnp.where(at_edge, 0.0, both))
        first = jnp.where(low_half, pltpu.roll(block_a, own_seg, 1), block_b)
        second = jnp.where(at_edge, first, pltpu.roll(first, LANES - 1, 1))
        for axis in range(3):
            seg_ref[axis, tile : tile + 1, :] = first[axis : axis + 1]
            seg_ref[3 + axis, tile : tile + 1, :] = second[axis : axis + 1]
    first = tuple(seg_ref[axis] for axis in range(3))
    segment, turn, span, span_core = segment_terms(first, tuple(seg_ref[3 + axis] for axis in range(3)))
    for axis in range(3):
        seg_ref[3 + axis] = segment[axis]
        seg_ref[6 + axis] = turn[axis]
    seg_ref[9] = span
    seg_ref[10] = span_core

    point = tuple(data_ref[begin:end, 8 + axis, :] for axis in range(3))
    normal = tuple(data_ref[begin:end, 11 + axis, :] for axis in range(3))
    moment = cross(point, normal)
    for axis in range(3):
        rec_ref[axis] = point[axis]
        rec_ref[3 + axis] = normal[axis]
        rec_ref[6 + axis] = moment[axis]

    for ref in (row1_ref, row2_ref):
        ref[6:8, :] = jnp.zeros((2, ref.shape[1]), jnp.float32)
    for axis in range(3):
        for tile in range(tiles):
            at = slice(tile * LANES, (tile + 1) * LANES)
            row1_ref[axis : axis + 1, at] = segment[axis][tile : tile + 1]
            row1_ref[3 + axis : 4 + axis, at] = -turn[axis][tile : tile + 1]
        for block in range(blocks):
            at = slice(block * LANES, (block + 1) * LANES)
            row2_ref[axis : axis + 1, at] = moment[axis][block : block + 1]
            row2_ref[3 + axis : 4 + axis, at] = normal[axis][block : block + 1]
    cross1_ref[...] = jnp.dot(moment_ref[...], stack_hlhl(row1_ref[...]), preferred_element_type=jnp.float32)
    cross2_ref[...] = jnp.dot(turn_ref[...], stack_hlhl(row2_ref[...]), preferred_element_type=jnp.float32)

    scale1_ref[...] = jnp.dot(
        left_ref[...], stack_hlhl(jnp.concatenate(folded, 1)), preferred_element_type=jnp.float32)
    scale2_ref[...] = jnp.dot(
        right_ref[...], stack_hlhl(jnp.concatenate([data_ref[b, 0:8, :] for b in range(begin, end)], 1)),
        preferred_element_type=jnp.float32)

    def initial(old, count, start):
        if old is None:
            return [jnp.zeros((CHUNK, LANES), jnp.float32) for _ in range(count)]
        return [old[k, start : start + CHUNK, :] for k in range(count)]

    for start in range(0, LANES, CHUNK):
        col = [col1_ref[k, start : start + CHUNK, :] for k in range(3)]
        sums = initial(old1, 9, start)
        for tile in range(tiles):
            row = [seg_ref[k, tile : tile + 1, :] for k in range(11)]
            scale = scale1_ref[start : start + CHUNK, tile * LANES : (tile + 1) * LANES]
            rel, by_normal, by_dist2, by_along = pair_terms(
                col, cross1_ref[start : start + CHUNK, tile * LANES : (tile + 1) * LANES],
                row[0:3], row[3:6], row[9], row[10], scale, False)
            for axis in range(3):
                sums[axis] += by_normal * row[3 + axis]
                sums[3 + axis] += by_normal * row[6 + axis]
                sums[6 + axis] += by_dist2 * rel[axis] + by_along * row[3 + axis]
        for k in range(9):
            new1[k, start : start + CHUNK, :] = sums[k]

    if between is not None:
        between()

    for start in range(0, own_seg, CHUNK):
        col = [col2_ref[k, start : start + CHUNK, :] for k in range(8)]
        sums = initial(old2, 11, start)
        for block in range(blocks):
            row = [rec_ref[k, block : block + 1, :] for k in range(9)]
            scale = scale2_ref[start : start + CHUNK, block * LANES : (block + 1) * LANES]
            rel, by_normal, by_dist2, by_along, by_span2 = pair_terms(
                row[0:3], cross2_ref[start : start + CHUNK, block * LANES : (block + 1) * LANES],
                col[0:3], col[3:6], col[6], col[7], scale, True)
            for axis in range(3):
                sums[axis] += by_normal * row[3 + axis]
                sums[3 + axis] += by_normal * row[6 + axis] + by_along * rel[axis]
                sums[6 + axis] += by_dist2 * rel[axis]
            sums[9] += by_along
            sums[10] += by_span2
        for k in range(11):
            new2[k, start : start + CHUNK, :] = sums[k]


def lane_sums(values):
    rows = values[0].shape[0]
    column = lax.broadcasted_iota(jnp.int32, (rows, 16), 1)
    result = jnp.zeros((rows, 16), jnp.float32)
    for index, value in enumerate(values):
        result = jnp.where(column == index, jnp.sum(value, axis=1, keepdims=True), result)
    return result


def receiver_totals(sums_ref, col_ref):
    parts = []
    for start in range(0, LANES, FINISH):
        sums = [sums_ref[k, start : start + FINISH, :] for k in range(9)]
        col = [col_ref[k, start : start + FINISH, :] for k in range(6)]
        by_point = [a + b for a, b in zip(cross(col[3:6], sums[0:3]), sums[6:9])]
        by_normal = [a - b for a, b in zip(cross(sums[0:3], col[0:3]), sums[3:6])]
        parts.append(lane_sums(by_point + by_normal))
    return jnp.transpose(jnp.concatenate(parts, 0))


def segment_totals(sums_ref, col_ref, own_seg, arriving, leaving):
    parts = []
    for start in range(0, own_seg, FINISH):
        sums = [sums_ref[k, start : start + FINISH, :] for k in range(11)]
        col = [col_ref[k, start : start + FINISH, :] for k in range(6)]
        turned, swept = cross(col[0:3], sums[0:3]), cross(sums[0:3], col[3:6])
        by_s = [sums[3 + k] - turned[k] + col[3 + k] * sums[10] for k in range(3)]
        by_both = [by_s[k] + (swept[k] + sums[6 + k] + col[3 + k] * sums[9]) for k in range(3)]
        if start + FINISH == own_seg:
            last = lax.broadcasted_iota(jnp.int32, (FINISH, LANES), 0) == FINISH - 1
            by_s = [jnp.where(last, a, b) for a, b in zip(arriving, by_s)]
            by_both = [jnp.where(last, a, b) for a, b in zip(leaving, by_both)]
        parts.append(lane_sums(by_s + by_both))
    return jnp.transpose(jnp.concatenate(parts, 0))


def own_receivers(data_ref):
    point = tuple(data_ref[0, 8 + axis : 9 + axis, :] for axis in range(3))
    normal = tuple(data_ref[0, 11 + axis : 12 + axis, :] for axis in range(3))
    return point, normal, cross(point, normal)


def own_segments(own_block, own_seg):
    lane = lax.broadcasted_iota(jnp.int32, (1, LANES), 1)
    first = pltpu.roll(own_block, own_seg, 1)
    second = jnp.where(lane == own_seg - 1, first, pltpu.roll(first, LANES - 1, 1))
    own_e = tuple(first[axis : axis + 1] for axis in range(3))
    segment, turn, span, span_core = segment_terms(own_e, tuple(second[axis : axis + 1] for axis in range(3)))
    return own_e, segment, turn, span, span_core


def early_kernel(chained, own_seg, *refs):
    data_ref, own_refs, rest = refs[0], refs[1:7], refs[7:]
    olds = rest[0:2] if chained else (None, None)
    rest = rest[2:] if chained else rest
    pair_sums(data_ref, own_refs, 0, data_ref.shape[0], own_seg, rest[2:], *olds, rest[0], rest[1])


def last_kernel(count, own_seg, *refs):
    data_ref, own_refs, old1_ref, old2_ref, rcv_out, vert_out, after_ref, new1_ref, new2_ref = (
        refs[0], refs[1:7], *refs[7:14])
    scratch = refs[14:]
    masks = exchange_masks(count)
    me = lax.axis_index("src")
    lane = lax.broadcasted_iota(jnp.int32, (1, LANES), 1)

    def place(device):
        return place_of((device & (count - 1)) ^ me, masks)

    def edge_sums():
        for block in range(count):
            after_ref[block] = data_ref[place((me ^ mask_at(block, masks)) + 1), 16:24, :]

        def spread(column):
            return jnp.broadcast_to(column, (column.shape[0], LANES))

        own_block = data_ref[0, 16:24, :]
        before = data_ref[place(me + count - 1), 16:24, :]
        own_p, own_n, own_m = own_receivers(data_ref)
        point = tuple(data_ref[:, 8 + axis, :] for axis in range(3))
        normal = tuple(data_ref[:, 11 + axis, :] for axis in range(3))
        moment = cross(point, normal)
        mine_last = spread(own_block[:, 2 * own_seg - 1 : 2 * own_seg])
        mine_next = spread(after_ref[0, :, own_seg : own_seg + 1])
        mine_weight = spread(own_block[:, own_seg - 1 : own_seg])
        before_last = spread(before[:, 2 * own_seg - 1 : 2 * own_seg])
        before_weight = spread(jnp.where(me == 0, 0.0, before[:, own_seg - 1 : own_seg]))
        mine_first = spread(own_block[:, own_seg : own_seg + 1])

        def rows(value, axis):
            return jnp.broadcast_to(value[axis : axis + 1], (count, LANES))

        def stacked(own, every):
            return tuple(
                jnp.concatenate([jnp.broadcast_to(a, (count, LANES)), b, b], 0) for a, b in zip(own, every))

        first = tuple(
            jnp.concatenate(
                [spread(data_ref[:, 16 + axis, 2 * own_seg - 1 : 2 * own_seg]), rows(mine_last, axis), rows(before_last, axis)], 0)
            for axis in range(3))
        second = tuple(
            jnp.concatenate(
                [spread(after_ref[:, axis, own_seg : own_seg + 1]), rows(mine_next, axis), rows(mine_first, axis)], 0)
            for axis in range(3))
        scales = [jnp.zeros((count, LANES), jnp.float32)] * 3
        for mode in range(8):
            left = data_ref[:, mode, :]
            scales[0] += spread(data_ref[:, 16 + mode, own_seg - 1 : own_seg]) * data_ref[0, mode : mode + 1, :]
            scales[1] += mine_weight[mode : mode + 1] * left
            scales[2] += before_weight[mode : mode + 1] * left
        segment, turn, span, span_core = segment_terms(first, second)
        normals = stacked(own_n, normal)
        rel, by_normal, by_dist2, by_along, by_span2 = pair_terms(
            stacked(own_p, point), normal_cross(normals, stacked(own_m, moment), segment, turn),
            first, segment, span, span_core, jnp.concatenate(scales, 0), True)

        def down(value):
            return jnp.sum(value, axis=0, keepdims=True)

        against_own, mine, ahead = slice(0, count), slice(count, 2 * count), slice(2 * count, 3 * count)
        swung, swept = cross(rel, normals), cross(normals, segment)
        edge_s = [(by_normal * segment[axis])[against_own] for axis in range(3)]
        edge_t = [(by_normal * turn[axis])[against_own] for axis in range(3)]
        edge_point = [a for a in cross(own_n, edge_s)]
        edge_normal = [down(a - b) for a, b in zip(cross(edge_s, own_p), edge_t)]
        leaving, arriving = [], []
        for axis in range(3):
            by_s = by_normal * swung[axis] + by_along * rel[axis] + by_span2 * segment[axis]
            by_p = by_dist2 * rel[axis] + by_along * segment[axis]
            by_r = by_normal * swept[axis] + by_p
            edge_point[axis] = down(edge_point[axis] + by_p[against_own])
            leaving.append(down((by_s + by_r)[mine]))
            arriving.append(down(by_s[ahead]))
        return edge_point, edge_normal, arriving, leaving

    found = []
    pair_sums(
        data_ref, own_refs, count - count // 4, count, own_seg, scratch, old1_ref, old2_ref, new1_ref, new2_ref,
        lambda: found.extend((*edge_sums(), receiver_totals(new1_ref, own_refs[0]))))
    edge_point, edge_normal, arriving, leaving, totals = found
    for axis in range(3):
        value = totals[axis : axis + 1] + edge_point[axis]
        rcv_out[axis : axis + 1, :] = 0.2 * value if axis == 2 else value
        rcv_out[3 + axis : 4 + axis, :] = totals[3 + axis : 4 + axis] + edge_normal[axis]

    totals = segment_totals(new2_ref, own_refs[1], own_seg, arriving, leaving)
    for axis in range(3):
        by_second = totals[axis : axis + 1]
        shifted = jnp.concatenate([by_second[:, own_seg - 1 :], by_second[:, : own_seg - 1]], 1)
        result = shifted - totals[3 + axis : 4 + axis]
        vert_out[axis : axis + 1, :] = 0.2 * result if axis == 2 else result


def pair_scratch(blocks, own_seg):
    return [
        pltpu.VMEM((11, blocks // 2, LANES), jnp.float32),
        pltpu.VMEM((9, blocks, LANES), jnp.float32),
        pltpu.VMEM((LANES, blocks // 2 * LANES), jnp.float32),
        pltpu.VMEM((own_seg, blocks * LANES), jnp.float32),
        pltpu.VMEM((8, blocks // 2 * LANES), jnp.float32),
        pltpu.VMEM((8, blocks * LANES), jnp.float32),
        pltpu.VMEM((LANES, blocks // 2 * LANES), jnp.float32),
        pltpu.VMEM((own_seg, blocks * LANES), jnp.float32),
    ]


def sum_shapes(own_seg):
    return [pltpu.VMEM((9, LANES, LANES), jnp.float32), pltpu.VMEM((11, own_seg, LANES), jnp.float32)]


def last_scratch(count, own_seg):
    return [pltpu.VMEM((count, 8, LANES), jnp.float32)] + sum_shapes(own_seg) + pair_scratch(count // 4, own_seg)


def pair_cost(blocks, own_seg):
    pairs = 2 * blocks * own_seg * LANES
    return pl.CostEstimate(flops=100 * pairs, bytes_accessed=blocks * ROWS * LANES * 4, transcendentals=3 * pairs)


def on_device(rcv_points, rcv_normals, left_modes, vertices, connect, right_modes, mode_weights):
    count = lax.axis_size("src")
    own_seg = vertices.shape[1]
    value = pl.pallas_call(
        functools.partial(pack_kernel, own_seg),
        out_shape=pltpu.VMEM((ROWS, LANES), jnp.float32),
        in_specs=[VMEM] * 6 + [pl.BlockSpec(memory_space=pltpu.SMEM)],
        out_specs=VMEM,
    )(rcv_points, rcv_normals, left_modes, vertices, connect, right_modes, mode_weights)[None]
    params = pltpu.CompilerParams(vmem_limit_bytes=24 << 20)
    own = pl.pallas_call(
        functools.partial(own_kernel, own_seg),
        out_shape=(
            pltpu.VMEM((6, LANES, LANES), jnp.float32),
            pltpu.VMEM((8, own_seg, LANES), jnp.float32),
            pltpu.VMEM((LANES, 32), jnp.bfloat16),
            pltpu.VMEM((own_seg, 32), jnp.bfloat16),
            pltpu.VMEM((LANES, 32), jnp.bfloat16),
            pltpu.VMEM((own_seg, 32), jnp.bfloat16),
        ),
        in_specs=[VMEM],
        out_specs=(VMEM,) * 6,
        cost_estimate=pair_cost(2, own_seg),
        compiler_params=params,
    )(value)

    def exchange(block, mask):
        return lax.ppermute(block, "src", [(s, s ^ mask) for s in range(count)])

    def add_pairs(block, *sums):
        return pl.pallas_call(
            functools.partial(early_kernel, len(sums) > 0, own_seg),
            out_shape=tuple(sum_shapes(own_seg)),
            in_specs=[VMEM] * (7 + len(sums)),
            out_specs=(VMEM, VMEM),
            scratch_shapes=pair_scratch(block.shape[0], own_seg),
            cost_estimate=pair_cost(block.shape[0], own_seg),
            compiler_params=params,
        )(block, *own, *sums)

    masks = exchange_masks(count)
    for mask in masks[:-3]:
        value = jnp.concatenate([value, exchange(value, mask)], 0)
    arrived, early = exchange(value, masks[-3]), exchange(value, masks[-2])
    late = exchange(arrived, masks[-2])
    value = jnp.concatenate([value, arrived], 0)
    beside = exchange(value, masks[-1])
    sums = add_pairs(value)
    sums = add_pairs(beside, *sums)
    late, sums = lax.optimization_barrier((late, sums))
    across = jnp.concatenate([early, late], 0)
    opposite = exchange(across, masks[-1])
    sums = add_pairs(across, *sums)
    value = jnp.concatenate([value, across, beside, opposite], 0)
    return pl.pallas_call(
        functools.partial(last_kernel, count, own_seg),
        out_shape=(
            jax.ShapeDtypeStruct((6, LANES), jnp.float32),
            jax.ShapeDtypeStruct((3, own_seg), jnp.float32),
        ),
        in_specs=[VMEM] * 9,
        out_specs=(VMEM, VMEM),
        scratch_shapes=last_scratch(count, own_seg),
        cost_estimate=pair_cost(count // 4, own_seg),
        compiler_params=params,
    )(value, *own, *sums)


def solution(mesh):
    split = P(None, ("group", "src"))
    return jax.shard_map(
        on_device, mesh=mesh, in_specs=(split,) * 6 + (P("group"),), out_specs=(split, split), check_vma=False
    )
```

```python
import functools
import math

import jax
import jax.numpy as jnp
from jax import lax
from jax.experimental import pallas as pl
from jax.experimental.pallas import tpu as pltpu
from jax.sharding import PartitionSpec as P

core_term = 0.05
inverse_four_pi = 0.25 / math.pi

LANES = 128
ROWS = 24
CHUNK = 64
FINISH = 32
VMEM = pl.BlockSpec(memory_space=pltpu.VMEM)


def exchange_masks(count):
    masks = []
    step = count // 2
    while step > 1:
        masks.append(step + 1)
        step //= 2
    return masks + [1]


def mask_at(place, masks):
    value = 0
    for bit, mask in enumerate(masks):
        if place >> bit & 1:
            value ^= mask
    return value


def place_of(value, masks):
    place = 0
    rest = value & 1
    for bit, mask in enumerate(masks[:-1]):
        taken = lax.shift_right_logical(value, mask.bit_length() - 1) & 1
        place = place + taken * (1 << bit)
        rest = rest ^ taken
    return place + rest * (1 << (len(masks) - 1))


def high_low(value):
    high = value.astype(jnp.bfloat16).astype(jnp.float32)
    return high, value - high


def dot_nt(left, right):
    return lax.dot_general(left, right, (((1,), (1,)), ((), ())), preferred_element_type=jnp.float32)


def cross(a, b):
    return (a[1] * b[2] - a[2] * b[1], a[2] * b[0] - a[0] * b[2], a[0] * b[1] - a[1] * b[0])


def normal_cross(normal, moment, segment, turn):
    return (moment[0] * segment[0] + moment[1] * segment[1] + moment[2] * segment[2]) - (
        normal[0] * turn[0] + normal[1] * turn[1] + normal[2] * turn[2]
    )


def pair_terms(point, cross_n, first, segment, span, span_core, scale, want_span):
    rel = tuple(p - e for p, e in zip(point, first))
    dist_sq = rel[0] * rel[0] + rel[1] * rel[1] + rel[2] * rel[2]
    along = segment[0] * rel[0] + segment[1] * rel[1] + segment[2] * rel[2]
    other = along - span
    second_sq = dist_sq - along - other
    inv_first = lax.rsqrt(dist_sq)
    inv_second = lax.rsqrt(second_sq)
    inv_den = 1.0 / ((span * dist_sq + span_core) - along * along)
    part_first = along * inv_first
    part_second = other * inv_second
    line = part_first - part_second
    scaled = scale * inv_den
    by_normal = scaled * line
    by_line = scaled * cross_n
    by_den = (by_normal * cross_n) * inv_den
    by_den2 = by_den + by_den
    cube_first = part_first * (inv_first * inv_first)
    cube_second = part_second * (inv_second * inv_second)
    by_dist2 = by_line * (cube_second - cube_first) - by_den2 * span
    by_along = by_line * ((inv_first - inv_second) - cube_second) + by_den2 * along
    if not want_span:
        return rel, by_normal, by_dist2, by_along
    by_span2 = by_line * ((inv_second + inv_second) + cube_second) - by_den2 * (dist_sq + core_term)
    return rel, by_normal, by_dist2, by_along, by_span2


def segment_terms(first, second):
    segment = tuple(b - a for a, b in zip(first, second))
    span = segment[0] * segment[0] + segment[1] * segment[1] + segment[2] * segment[2]
    return segment, cross(segment, first), span, core_term * span + core_term


def pack_kernel(own_seg, points_ref, normals_ref, left_ref, vertices_ref, connect_ref, right_ref, weights_ref, out_ref):
    base = lax.axis_index("src") * own_seg
    row8 = lax.broadcasted_iota(jnp.int32, (8, LANES), 0)
    weight = jnp.zeros((8, LANES), jnp.float32)
    for mode in range(8):
        weight = jnp.where(row8 == mode, weights_ref[mode], weight)
    weighted = right_ref[...] * (weight * inverse_four_pi)
    high, rest = high_low(weighted)
    middle, low = high_low(rest)
    parts = jnp.concatenate([high, middle, low, jnp.zeros_like(low)], 0).astype(jnp.bfloat16)
    local = connect_ref[0:1, :] - base
    hit = lax.broadcasted_iota(jnp.int32, (LANES, LANES), 0) == local
    folded = dot_nt(parts, hit.astype(jnp.float32).astype(jnp.bfloat16))
    folded = folded[0:8] + (folded[8:16] + folded[16:24])
    out_ref[0:8, :] = left_ref[...]
    out_ref[8:10, :] = points_ref[0:2, :]
    out_ref[10:11, :] = 0.5 + 0.2 * points_ref[2:3, :]
    out_ref[11:14, :] = normals_ref[...]
    out_ref[14:16, :] = jnp.zeros((2, LANES), jnp.float32)
    out_ref[16:24, :] = folded
    out_ref[16:18, own_seg : 2 * own_seg] = vertices_ref[0:2, :]
    out_ref[18:19, own_seg : 2 * own_seg] = 0.2 * vertices_ref[2:3, :]


def stack_hhll(rows):
    high, low = high_low(rows)
    return jnp.transpose(jnp.concatenate([high, high, low, low], 0)).astype(jnp.bfloat16)


def stack_hlhl(rows):
    high, low = high_low(rows)
    both = jnp.concatenate([high, low], 0).astype(jnp.bfloat16)
    return jnp.concatenate([both, both], 0)


def lane_edges(own_seg):
    lane = lax.broadcasted_iota(jnp.int32, (1, LANES), 1)
    return (lane == own_seg - 1) | (lane == 2 * own_seg - 1)


def own_kernel(own_seg, data_ref, col1_ref, col2_ref, left_ref, right_ref, moment_ref, turn_ref):
    def columns(rows, out_ref):
        pad = jnp.zeros((16 - len(rows), LANES), jnp.float32)
        cols = jnp.transpose(jnp.concatenate(list(rows) + [pad], 0))
        count = out_ref.shape[1]
        for k in range(len(rows)):
            out_ref[k] = jnp.broadcast_to(cols[0:count, k : k + 1], (count, LANES))

    own_block = data_ref[0, 16:24, :]
    point, normal, moment = own_receivers(data_ref)
    columns([*point, *normal], col1_ref)
    own_e, own_s, own_t, span, span_core = own_segments(own_block, own_seg)
    columns([*own_e, *own_s, span, span_core], col2_ref)
    left_ref[...] = stack_hhll(data_ref[0, 0:8, :])
    right_ref[...] = stack_hhll(jnp.where(lane_edges(own_seg), 0.0, own_block))[0:own_seg]
    pad = jnp.zeros((2, LANES), jnp.float32)
    moment_ref[...] = stack_hhll(jnp.concatenate([*moment, *normal, pad], 0))
    turn_ref[...] = stack_hhll(jnp.concatenate([*own_s, *(-value for value in own_t), pad], 0))[0:own_seg]


def pair_sums(data_ref, own_refs, begin, end, own_seg, scratch, old1, old2, new1, new2, between=None):
    seg_ref, rec_ref, scale1_ref, scale2_ref, row1_ref, row2_ref, cross1_ref, cross2_ref = scratch
    col1_ref, col2_ref, left_ref, right_ref, moment_ref, turn_ref = own_refs
    blocks = end - begin
    tiles = blocks // 2
    lane = lax.broadcasted_iota(jnp.int32, (1, LANES), 1)
    low_half = lane < own_seg
    at_edge = lane_edges(own_seg)

    folded = []
    for tile in range(tiles):
        block_a, block_b = data_ref[begin + 2 * tile, 16:24, :], data_ref[begin + 2 * tile + 1, 16:24, :]
        both = jnp.where(low_half, block_a, pltpu.roll(block_b, own_seg, 1))
        folded.append(jnp.where(at_edge, 0.0, both))
        first = jnp.where(low_half, pltpu.roll(block_a, own_seg, 1), block_b)
        second = jnp.where(at_edge, first, pltpu.roll(first, LANES - 1, 1))
        for axis in range(3):
            seg_ref[axis, tile : tile + 1, :] = first[axis : axis + 1]
            seg_ref[3 + axis, tile : tile + 1, :] = second[axis : axis + 1]
    first = tuple(seg_ref[axis] for axis in range(3))
    segment, turn, span, span_core = segment_terms(first, tuple(seg_ref[3 + axis] for axis in range(3)))
    for axis in range(3):
        seg_ref[3 + axis] = segment[axis]
        seg_ref[6 + axis] = turn[axis]
    seg_ref[9] = span
    seg_ref[10] = span_core

    point = tuple(data_ref[begin:end, 8 + axis, :] for axis in range(3))
    normal = tuple(data_ref[begin:end, 11 + axis, :] for axis in range(3))
    moment = cross(point, normal)
    for axis in range(3):
        rec_ref[axis] = point[axis]
        rec_ref[3 + axis] = normal[axis]
        rec_ref[6 + axis] = moment[axis]

    for ref in (row1_ref, row2_ref):
        ref[6:8, :] = jnp.zeros((2, ref.shape[1]), jnp.float32)
    for axis in range(3):
        for tile in range(tiles):
            at = slice(tile * LANES, (tile + 1) * LANES)
            row1_ref[axis : axis + 1, at] = segment[axis][tile : tile + 1]
            row1_ref[3 + axis : 4 + axis, at] = -turn[axis][tile : tile + 1]
        for block in range(blocks):
            at = slice(block * LANES, (block + 1) * LANES)
            row2_ref[axis : axis + 1, at] = moment[axis][block : block + 1]
            row2_ref[3 + axis : 4 + axis, at] = normal[axis][block : block + 1]
    cross1_ref[...] = jnp.dot(moment_ref[...], stack_hlhl(row1_ref[...]), preferred_element_type=jnp.float32)
    cross2_ref[...] = jnp.dot(turn_ref[...], stack_hlhl(row2_ref[...]), preferred_element_type=jnp.float32)

    scale1_ref[...] = jnp.dot(
        left_ref[...], stack_hlhl(jnp.concatenate(folded, 1)), preferred_element_type=jnp.float32)
    scale2_ref[...] = jnp.dot(
        right_ref[...], stack_hlhl(jnp.concatenate([data_ref[b, 0:8, :] for b in range(begin, end)], 1)),
        preferred_element_type=jnp.float32)

    def initial(old, count, start):
        if old is None:
            return [jnp.zeros((CHUNK, LANES), jnp.float32) for _ in range(count)]
        return [old[k, start : start + CHUNK, :] for k in range(count)]

    for start in range(0, LANES, CHUNK):
        col = [col1_ref[k, start : start + CHUNK, :] for k in range(3)]
        sums = initial(old1, 9, start)
        for tile in range(tiles):
            row = [seg_ref[k, tile : tile + 1, :] for k in range(11)]
            scale = scale1_ref[start : start + CHUNK, tile * LANES : (tile + 1) * LANES]
            rel, by_normal, by_dist2, by_along = pair_terms(
                col, cross1_ref[start : start + CHUNK, tile * LANES : (tile + 1) * LANES],
                row[0:3], row[3:6], row[9], row[10], scale, False)
            for axis in range(3):
                sums[axis] += by_normal * row[3 + axis]
                sums[3 + axis] += by_normal * row[6 + axis]
                sums[6 + axis] += by_dist2 * rel[axis] + by_along * row[3 + axis]
        for k in range(9):
            new1[k, start : start + CHUNK, :] = sums[k]

    if between is not None:
        between()

    for start in range(0, own_seg, CHUNK):
        col = [col2_ref[k, start : start + CHUNK, :] for k in range(8)]
        sums = initial(old2, 11, start)
        for block in range(blocks):
            row = [rec_ref[k, block : block + 1, :] for k in range(9)]
            scale = scale2_ref[start : start + CHUNK, block * LANES : (block + 1) * LANES]
            rel, by_normal, by_dist2, by_along, by_span2 = pair_terms(
                row[0:3], cross2_ref[start : start + CHUNK, block * LANES : (block + 1) * LANES],
                col[0:3], col[3:6], col[6], col[7], scale, True)
            for axis in range(3):
                sums[axis] += by_normal * row[3 + axis]
                sums[3 + axis] += by_normal * row[6 + axis] + by_along * rel[axis]
                sums[6 + axis] += by_dist2 * rel[axis]
            sums[9] += by_along
            sums[10] += by_span2
        for k in range(11):
            new2[k, start : start + CHUNK, :] = sums[k]


def lane_sums(values):
    rows = values[0].shape[0]
    column = lax.broadcasted_iota(jnp.int32, (rows, 16), 1)
    result = jnp.zeros((rows, 16), jnp.float32)
    for index, value in enumerate(values):
        result = jnp.where(column == index, jnp.sum(value, axis=1, keepdims=True), result)
    return result


def receiver_totals(sums_ref, col_ref):
    parts = []
    for start in range(0, LANES, FINISH):
        sums = [sums_ref[k, start : start + FINISH, :] for k in range(9)]
        col = [col_ref[k, start : start + FINISH, :] for k in range(6)]
        by_point = [a + b for a, b in zip(cross(col[3:6], sums[0:3]), sums[6:9])]
        by_normal = [a - b for a, b in zip(cross(sums[0:3], col[0:3]), sums[3:6])]
        parts.append(lane_sums(by_point + by_normal))
    return jnp.transpose(jnp.concatenate(parts, 0))


def segment_totals(sums_ref, col_ref, own_seg, arriving, leaving):
    parts = []
    for start in range(0, own_seg, FINISH):
        sums = [sums_ref[k, start : start + FINISH, :] for k in range(11)]
        col = [col_ref[k, start : start + FINISH, :] for k in range(6)]
        turned, swept = cross(col[0:3], sums[0:3]), cross(sums[0:3], col[3:6])
        by_s = [sums[3 + k] - turned[k] + col[3 + k] * sums[10] for k in range(3)]
        by_both = [by_s[k] + (swept[k] + sums[6 + k] + col[3 + k] * sums[9]) for k in range(3)]
        if start + FINISH == own_seg:
            last = lax.broadcasted_iota(jnp.int32, (FINISH, LANES), 0) == FINISH - 1
            by_s = [jnp.where(last, a, b) for a, b in zip(arriving, by_s)]
            by_both = [jnp.where(last, a, b) for a, b in zip(leaving, by_both)]
        parts.append(lane_sums(by_s + by_both))
    return jnp.transpose(jnp.concatenate(parts, 0))


def own_receivers(data_ref):
    point = tuple(data_ref[0, 8 + axis : 9 + axis, :] for axis in range(3))
    normal = tuple(data_ref[0, 11 + axis : 12 + axis, :] for axis in range(3))
    return point, normal, cross(point, normal)


def own_segments(own_block, own_seg):
    lane = lax.broadcasted_iota(jnp.int32, (1, LANES), 1)
    first = pltpu.roll(own_block, own_seg, 1)
    second = jnp.where(lane == own_seg - 1, first, pltpu.roll(first, LANES - 1, 1))
    own_e = tuple(first[axis : axis + 1] for axis in range(3))
    segment, turn, span, span_core = segment_terms(own_e, tuple(second[axis : axis + 1] for axis in range(3)))
    return own_e, segment, turn, span, span_core


def early_kernel(chained, own_seg, *refs):
    data_ref, own_refs, rest = refs[0], refs[1:7], refs[7:]
    olds = rest[0:2] if chained else (None, None)
    rest = rest[2:] if chained else rest
    pair_sums(data_ref, own_refs, 0, data_ref.shape[0], own_seg, rest[2:], *olds, rest[0], rest[1])


def last_kernel(count, own_seg, *refs):
    data_ref, own_refs, old1_ref, old2_ref, rcv_out, vert_out, after_ref, new1_ref, new2_ref = (
        refs[0], refs[1:7], *refs[7:14])
    scratch = refs[14:]
    masks = exchange_masks(count)
    me = lax.axis_index("src")
    lane = lax.broadcasted_iota(jnp.int32, (1, LANES), 1)

    def place(device):
        return place_of((device & (count - 1)) ^ me, masks)

    def edge_sums():
        for block in range(count):
            after_ref[block] = data_ref[place((me ^ mask_at(block, masks)) + 1), 16:24, :]

        def spread(column):
            return jnp.broadcast_to(column, (column.shape[0], LANES))

        own_block = data_ref[0, 16:24, :]
        before = data_ref[place(me + count - 1), 16:24, :]
        own_p, own_n, own_m = own_receivers(data_ref)
        point = tuple(data_ref[:, 8 + axis, :] for axis in range(3))
        normal = tuple(data_ref[:, 11 + axis, :] for axis in range(3))
        moment = cross(point, normal)
        mine_last = spread(own_block[:, 2 * own_seg - 1 : 2 * own_seg])
        mine_next = spread(after_ref[0, :, own_seg : own_seg + 1])
        mine_weight = spread(own_block[:, own_seg - 1 : own_seg])
        before_last = spread(before[:, 2 * own_seg - 1 : 2 * own_seg])
        before_weight = spread(jnp.where(me == 0, 0.0, before[:, own_seg - 1 : own_seg]))
        mine_first = spread(own_block[:, own_seg : own_seg + 1])

        def rows(value, axis):
            return jnp.broadcast_to(value[axis : axis + 1], (count, LANES))

        def stacked(own, every):
            return tuple(
                jnp.concatenate([jnp.broadcast_to(a, (count, LANES)), b, b], 0) for a, b in zip(own, every))

        first = tuple(
            jnp.concatenate(
                [spread(data_ref[:, 16 + axis, 2 * own_seg - 1 : 2 * own_seg]), rows(mine_last, axis), rows(before_last, axis)], 0)
            for axis in range(3))
        second = tuple(
            jnp.concatenate(
                [spread(after_ref[:, axis, own_seg : own_seg + 1]), rows(mine_next, axis), rows(mine_first, axis)], 0)
            for axis in range(3))
        scales = [jnp.zeros((count, LANES), jnp.float32)] * 3
        for mode in range(8):
            left = data_ref[:, mode, :]
            scales[0] += spread(data_ref[:, 16 + mode, own_seg - 1 : own_seg]) * data_ref[0, mode : mode + 1, :]
            scales[1] += mine_weight[mode : mode + 1] * left
            scales[2] += before_weight[mode : mode + 1] * left
        segment, turn, span, span_core = segment_terms(first, second)
        normals = stacked(own_n, normal)
        rel, by_normal, by_dist2, by_along, by_span2 = pair_terms(
            stacked(own_p, point), normal_cross(normals, stacked(own_m, moment), segment, turn),
            first, segment, span, span_core, jnp.concatenate(scales, 0), True)

        def down(value):
            return jnp.sum(value, axis=0, keepdims=True)

        against_own, mine, ahead = slice(0, count), slice(count, 2 * count), slice(2 * count, 3 * count)
        swung, swept = cross(rel, normals), cross(normals, segment)
        edge_s = [(by_normal * segment[axis])[against_own] for axis in range(3)]
        edge_t = [(by_normal * turn[axis])[against_own] for axis in range(3)]
        edge_point = [a for a in cross(own_n, edge_s)]
        edge_normal = [down(a - b) for a, b in zip(cross(edge_s, own_p), edge_t)]
        leaving, arriving = [], []
        for axis in range(3):
            by_s = by_normal * swung[axis] + by_along * rel[axis] + by_span2 * segment[axis]
            by_p = by_dist2 * rel[axis] + by_along * segment[axis]
            by_r = by_normal * swept[axis] + by_p
            edge_point[axis] = down(edge_point[axis] + by_p[against_own])
            leaving.append(down((by_s + by_r)[mine]))
            arriving.append(down(by_s[ahead]))
        return edge_point, edge_normal, arriving, leaving

    found = []
    pair_sums(
        data_ref, own_refs, count - count // 8, count, own_seg, scratch, old1_ref, old2_ref, new1_ref, new2_ref,
        lambda: found.extend((*edge_sums(), receiver_totals(new1_ref, own_refs[0]))))
    edge_point, edge_normal, arriving, leaving, totals = found
    for axis in range(3):
        value = totals[axis : axis + 1] + edge_point[axis]
        rcv_out[axis : axis + 1, :] = 0.2 * value if axis == 2 else value
        rcv_out[3 + axis : 4 + axis, :] = totals[3 + axis : 4 + axis] + edge_normal[axis]

    totals = segment_totals(new2_ref, own_refs[1], own_seg, arriving, leaving)
    for axis in range(3):
        by_second = totals[axis : axis + 1]
        shifted = jnp.concatenate([by_second[:, own_seg - 1 :], by_second[:, : own_seg - 1]], 1)
        result = shifted - totals[3 + axis : 4 + axis]
        vert_out[axis : axis + 1, :] = 0.2 * result if axis == 2 else result


def pair_scratch(blocks, own_seg):
    return [
        pltpu.VMEM((11, blocks // 2, LANES), jnp.float32),
        pltpu.VMEM((9, blocks, LANES), jnp.float32),
        pltpu.VMEM((LANES, blocks // 2 * LANES), jnp.float32),
        pltpu.VMEM((own_seg, blocks * LANES), jnp.float32),
        pltpu.VMEM((8, blocks // 2 * LANES), jnp.float32),
        pltpu.VMEM((8, blocks * LANES), jnp.float32),
        pltpu.VMEM((LANES, blocks // 2 * LANES), jnp.float32),
        pltpu.VMEM((own_seg, blocks * LANES), jnp.float32),
    ]


def sum_shapes(own_seg):
    return [pltpu.VMEM((9, LANES, LANES), jnp.float32), pltpu.VMEM((11, own_seg, LANES), jnp.float32)]


def last_scratch(count, own_seg):
    return [pltpu.VMEM((count, 8, LANES), jnp.float32)] + sum_shapes(own_seg) + pair_scratch(count // 8, own_seg)


def pair_cost(blocks, own_seg):
    pairs = 2 * blocks * own_seg * LANES
    return pl.CostEstimate(flops=100 * pairs, bytes_accessed=blocks * ROWS * LANES * 4, transcendentals=3 * pairs)


def on_device(rcv_points, rcv_normals, left_modes, vertices, connect, right_modes, mode_weights):
    count = lax.axis_size("src")
    own_seg = vertices.shape[1]
    value = pl.pallas_call(
        functools.partial(pack_kernel, own_seg),
        out_shape=pltpu.VMEM((ROWS, LANES), jnp.float32),
        in_specs=[VMEM] * 6 + [pl.BlockSpec(memory_space=pltpu.SMEM)],
        out_specs=VMEM,
    )(rcv_points, rcv_normals, left_modes, vertices, connect, right_modes, mode_weights)[None]
    params = pltpu.CompilerParams(vmem_limit_bytes=24 << 20)
    own = pl.pallas_call(
        functools.partial(own_kernel, own_seg),
        out_shape=(
            pltpu.VMEM((6, LANES, LANES), jnp.float32),
            pltpu.VMEM((8, own_seg, LANES), jnp.float32),
            pltpu.VMEM((LANES, 32), jnp.bfloat16),
            pltpu.VMEM((own_seg, 32), jnp.bfloat16),
            pltpu.VMEM((LANES, 32), jnp.bfloat16),
            pltpu.VMEM((own_seg, 32), jnp.bfloat16),
        ),
        in_specs=[VMEM],
        out_specs=(VMEM,) * 6,
        cost_estimate=pair_cost(2, own_seg),
        compiler_params=params,
    )(value)

    def exchange(block, mask):
        return lax.ppermute(block, "src", [(s, s ^ mask) for s in range(count)])

    def add_pairs(block, *sums):
        return pl.pallas_call(
            functools.partial(early_kernel, len(sums) > 0, own_seg),
            out_shape=tuple(sum_shapes(own_seg)),
            in_specs=[VMEM] * (7 + len(sums)),
            out_specs=(VMEM, VMEM),
            scratch_shapes=pair_scratch(block.shape[0], own_seg),
            cost_estimate=pair_cost(block.shape[0], own_seg),
            compiler_params=params,
        )(block, *own, *sums)

    masks = exchange_masks(count)
    for mask in masks[:-3]:
        value = jnp.concatenate([value, exchange(value, mask)], 0)
    arrived, early = exchange(value, masks[-3]), exchange(value, masks[-2])
    late = exchange(arrived, masks[-2])
    value = jnp.concatenate([value, arrived], 0)
    beside, beside_early = exchange(value, masks[-1]), exchange(early, masks[-1])
    sums = add_pairs(value)
    sums = add_pairs(beside, *sums)
    late, sums = lax.optimization_barrier((late, sums))
    beside_late = exchange(late, masks[-1])
    sums = add_pairs(jnp.concatenate([early, late, beside_early], 0), *sums)
    value = jnp.concatenate([value, early, late, beside, beside_early, beside_late], 0)
    return pl.pallas_call(
        functools.partial(last_kernel, count, own_seg),
        out_shape=(
            jax.ShapeDtypeStruct((6, LANES), jnp.float32),
            jax.ShapeDtypeStruct((3, own_seg), jnp.float32),
        ),
        in_specs=[VMEM] * 9,
        out_specs=(VMEM, VMEM),
        scratch_shapes=last_scratch(count, own_seg),
        cost_estimate=pair_cost(count // 8, own_seg),
        compiler_params=params,
    )(value, *own, *sums)


def solution(mesh):
    split = P(None, ("group", "src"))
    return jax.shard_map(
        on_device, mesh=mesh, in_specs=(split,) * 6 + (P("group"),), out_specs=(split, split), check_vma=False
    )
```

```python
import functools
import math

import jax
import jax.numpy as jnp
from jax import lax
from jax.experimental import pallas as pl
from jax.experimental.pallas import tpu as pltpu
from jax.sharding import PartitionSpec as P

core_term = 0.05
inverse_four_pi = 0.25 / math.pi

LANES = 128
ROWS = 24
CHUNK = 64
FINISH = 32
VMEM = pl.BlockSpec(memory_space=pltpu.VMEM)


def exchange_masks(count):
    masks = []
    step = count // 2
    while step > 1:
        masks.append(step + 1)
        step //= 2
    return masks + [1]


def mask_at(place, masks):
    value = 0
    for bit, mask in enumerate(masks):
        if place >> bit & 1:
            value ^= mask
    return value


def place_of(value, masks):
    place = 0
    rest = value & 1
    for bit, mask in enumerate(masks[:-1]):
        taken = lax.shift_right_logical(value, mask.bit_length() - 1) & 1
        place = place + taken * (1 << bit)
        rest = rest ^ taken
    return place + rest * (1 << (len(masks) - 1))


def high_low(value):
    high = value.astype(jnp.bfloat16).astype(jnp.float32)
    return high, value - high


def dot_nt(left, right):
    return lax.dot_general(left, right, (((1,), (1,)), ((), ())), preferred_element_type=jnp.float32)


def dot3(a, b):
    return a[0] * b[0] + a[1] * b[1] + a[2] * b[2]


def three_parts(value):
    high, rest = high_low(value)
    return high, *high_low(rest)


def stack_left(rows):
    high, middle, low = three_parts(rows)
    return jnp.transpose(jnp.concatenate([high, high, middle, high, low, middle], 0)).astype(jnp.bfloat16)


def stack_right(rows):
    high, middle, low = three_parts(rows)
    return jnp.concatenate([high, middle, high, low, high, middle], 0).astype(jnp.bfloat16)


def cross(a, b):
    return (a[1] * b[2] - a[2] * b[1], a[2] * b[0] - a[0] * b[2], a[0] * b[1] - a[1] * b[0])


def normal_cross(normal, moment, segment, turn):
    return (moment[0] * segment[0] + moment[1] * segment[1] + moment[2] * segment[2]) - (
        normal[0] * turn[0] + normal[1] * turn[1] + normal[2] * turn[2]
    )


def pair_terms(dist_sq, along, cross_n, span, span_core, scale, want_span):
    other = along - span
    second_sq = dist_sq - along - other
    inv_first = lax.rsqrt(dist_sq)
    inv_second = lax.rsqrt(second_sq)
    inv_den = 1.0 / ((span * dist_sq + span_core) - along * along)
    part_first = along * inv_first
    part_second = other * inv_second
    line = part_first - part_second
    scaled = scale * inv_den
    by_normal = scaled * line
    by_line = scaled * cross_n
    by_den = (by_normal * cross_n) * inv_den
    by_den2 = by_den + by_den
    cube_first = part_first * (inv_first * inv_first)
    cube_second = part_second * (inv_second * inv_second)
    by_dist2 = by_line * (cube_second - cube_first) - by_den2 * span
    by_along = by_line * ((inv_first - inv_second) - cube_second) + by_den2 * along
    if not want_span:
        return by_normal, by_dist2, by_along
    by_span2 = by_line * ((inv_second + inv_second) + cube_second) - by_den2 * (dist_sq + core_term)
    return by_normal, by_dist2, by_along, by_span2


def segment_terms(first, second):
    segment = tuple(b - a for a, b in zip(first, second))
    span = segment[0] * segment[0] + segment[1] * segment[1] + segment[2] * segment[2]
    return segment, cross(segment, first), span, core_term * span + core_term


def pack_kernel(own_seg, points_ref, normals_ref, left_ref, vertices_ref, connect_ref, right_ref, weights_ref, out_ref):
    base = lax.axis_index("src") * own_seg
    row8 = lax.broadcasted_iota(jnp.int32, (8, LANES), 0)
    weight = jnp.zeros((8, LANES), jnp.float32)
    for mode in range(8):
        weight = jnp.where(row8 == mode, weights_ref[mode], weight)
    weighted = right_ref[...] * (weight * inverse_four_pi)
    high, rest = high_low(weighted)
    middle, low = high_low(rest)
    parts = jnp.concatenate([high, middle, low, jnp.zeros_like(low)], 0).astype(jnp.bfloat16)
    local = connect_ref[0:1, :] - base
    hit = lax.broadcasted_iota(jnp.int32, (LANES, LANES), 0) == local
    folded = dot_nt(parts, hit.astype(jnp.float32).astype(jnp.bfloat16))
    folded = folded[0:8] + (folded[8:16] + folded[16:24])
    out_ref[0:8, :] = left_ref[...]
    out_ref[8:10, :] = points_ref[0:2, :]
    out_ref[10:11, :] = 0.5 + 0.2 * points_ref[2:3, :]
    out_ref[11:14, :] = normals_ref[...]
    out_ref[14:16, :] = jnp.zeros((2, LANES), jnp.float32)
    out_ref[16:24, :] = folded
    out_ref[16:18, own_seg : 2 * own_seg] = vertices_ref[0:2, :]
    out_ref[18:19, own_seg : 2 * own_seg] = 0.2 * vertices_ref[2:3, :]


def stack_hhll(rows):
    high, low = high_low(rows)
    return jnp.transpose(jnp.concatenate([high, high, low, low], 0)).astype(jnp.bfloat16)


def stack_hlhl(rows):
    high, low = high_low(rows)
    both = jnp.concatenate([high, low], 0).astype(jnp.bfloat16)
    return jnp.concatenate([both, both], 0)


def lane_edges(own_seg):
    lane = lax.broadcasted_iota(jnp.int32, (1, LANES), 1)
    return (lane == own_seg - 1) | (lane == 2 * own_seg - 1)


def own_kernel(own_seg, data_ref, col1_ref, col2_ref, left_ref, right_ref, moment_ref, turn_ref, point_ref, reach_ref):
    def columns(rows, out_ref):
        pad = jnp.zeros((16 - len(rows), LANES), jnp.float32)
        cols = jnp.transpose(jnp.concatenate(list(rows) + [pad], 0))
        count = out_ref.shape[1]
        for k in range(len(rows)):
            out_ref[k] = jnp.broadcast_to(cols[0:count, k : k + 1], (count, LANES))

    own_block = data_ref[0, 16:24, :]
    point, normal, moment = own_receivers(data_ref)
    columns([*point, *normal], col1_ref)
    own_e, own_s, own_t, span, span_core = own_segments(own_block, own_seg)
    columns([*own_e, *own_s, span, span_core], col2_ref)
    left_ref[...] = stack_hhll(data_ref[0, 0:8, :])
    right_ref[...] = stack_hhll(jnp.where(lane_edges(own_seg), 0.0, own_block))[0:own_seg]
    pad = jnp.zeros((2, LANES), jnp.float32)
    moment_ref[...] = stack_hhll(jnp.concatenate([*moment, *normal, pad], 0))
    turn_ref[...] = stack_hhll(jnp.concatenate([*own_s, *(-value for value in own_t), pad], 0))[0:own_seg]
    one, pad = jnp.ones((1, LANES), jnp.float32), jnp.zeros((3, LANES), jnp.float32)
    point_ref[...] = stack_left(jnp.concatenate([*point, one, dot3(point, point), pad], 0))
    along = jnp.concatenate([*own_s, -dot3(own_s, own_e), 0.0 * one, pad], 0)
    dist_sq = jnp.concatenate([*(-2.0 * value for value in own_e), dot3(own_e, own_e), one, pad], 0)
    reach_ref[0:own_seg, :] = stack_left(along)[0:own_seg]
    reach_ref[own_seg : 2 * own_seg, :] = stack_left(dist_sq)[0:own_seg]


def pair_sums(data_ref, own_refs, begin, end, own_seg, scratch, old1, old2, new1, new2, between=None):
    seg_ref, rec_ref, scale1_ref, scale2_ref, row1_ref, row2_ref, cross1_ref, cross2_ref = scratch[0:8]
    near1_ref, near2_ref, reach1_ref, reach2_ref = scratch[8:]
    col1_ref, col2_ref, left_ref, right_ref, moment_ref, turn_ref, point_ref, reach_ref = own_refs
    blocks = end - begin
    tiles = blocks // 2
    lane = lax.broadcasted_iota(jnp.int32, (1, LANES), 1)
    low_half = lane < own_seg
    at_edge = lane_edges(own_seg)

    folded = []
    for tile in range(tiles):
        block_a, block_b = data_ref[begin + 2 * tile, 16:24, :], data_ref[begin + 2 * tile + 1, 16:24, :]
        both = jnp.where(low_half, block_a, pltpu.roll(block_b, own_seg, 1))
        folded.append(jnp.where(at_edge, 0.0, both))
        first = jnp.where(low_half, pltpu.roll(block_a, own_seg, 1), block_b)
        second = jnp.where(at_edge, first, pltpu.roll(first, LANES - 1, 1))
        for axis in range(3):
            seg_ref[axis, tile : tile + 1, :] = first[axis : axis + 1]
            seg_ref[3 + axis, tile : tile + 1, :] = second[axis : axis + 1]
    first = tuple(seg_ref[axis] for axis in range(3))
    segment, turn, span, span_core = segment_terms(first, tuple(seg_ref[3 + axis] for axis in range(3)))
    for axis in range(3):
        seg_ref[3 + axis] = segment[axis]
        seg_ref[6 + axis] = turn[axis]
    seg_ref[9] = span
    seg_ref[10] = span_core

    point = tuple(data_ref[begin:end, 8 + axis, :] for axis in range(3))
    normal = tuple(data_ref[begin:end, 11 + axis, :] for axis in range(3))
    moment = cross(point, normal)
    for axis in range(3):
        rec_ref[axis] = point[axis]
        rec_ref[3 + axis] = normal[axis]
        rec_ref[6 + axis] = moment[axis]

    for ref in (row1_ref, row2_ref):
        ref[6:8, :] = jnp.zeros((2, ref.shape[1]), jnp.float32)
    for axis in range(3):
        for tile in range(tiles):
            at = slice(tile * LANES, (tile + 1) * LANES)
            row1_ref[axis : axis + 1, at] = segment[axis][tile : tile + 1]
            row1_ref[3 + axis : 4 + axis, at] = -turn[axis][tile : tile + 1]
        for block in range(blocks):
            at = slice(block * LANES, (block + 1) * LANES)
            row2_ref[axis : axis + 1, at] = moment[axis][block : block + 1]
            row2_ref[3 + axis : 4 + axis, at] = normal[axis][block : block + 1]
    cross1_ref[...] = jnp.dot(moment_ref[...], stack_hlhl(row1_ref[...]), preferred_element_type=jnp.float32)
    cross2_ref[...] = jnp.dot(turn_ref[...], stack_hlhl(row2_ref[...]), preferred_element_type=jnp.float32)

    near1_ref[3:8, :] = jnp.zeros((5, near1_ref.shape[1]), jnp.float32)
    near1_ref[4:5, tiles * LANES :] = jnp.ones((1, tiles * LANES), jnp.float32)
    near2_ref[3:4, :] = jnp.ones((1, near2_ref.shape[1]), jnp.float32)
    near2_ref[4:8, :] = jnp.zeros((4, near2_ref.shape[1]), jnp.float32)
    offset, length, reach = -dot3(segment, first), dot3(first, first), dot3(point, point)
    for tile in range(tiles):
        at, after = slice(tile * LANES, (tile + 1) * LANES), slice((tiles + tile) * LANES, (tiles + tile + 1) * LANES)
        for axis in range(3):
            near1_ref[axis : axis + 1, at] = segment[axis][tile : tile + 1]
            near1_ref[axis : axis + 1, after] = -2.0 * first[axis][tile : tile + 1]
        near1_ref[3:4, at] = offset[tile : tile + 1]
        near1_ref[3:4, after] = length[tile : tile + 1]
    for block in range(blocks):
        at = slice(block * LANES, (block + 1) * LANES)
        near2_ref[0:3, at] = data_ref[begin + block, 8:11, :]
        near2_ref[4:5, at] = reach[block : block + 1]
    reach1_ref[...] = jnp.dot(point_ref[...], stack_right(near1_ref[...]), preferred_element_type=jnp.float32)
    reach2_ref[...] = jnp.dot(reach_ref[...], stack_right(near2_ref[...]), preferred_element_type=jnp.float32)

    scale1_ref[...] = jnp.dot(
        left_ref[...], stack_hlhl(jnp.concatenate(folded, 1)), preferred_element_type=jnp.float32)
    scale2_ref[...] = jnp.dot(
        right_ref[...], stack_hlhl(jnp.concatenate([data_ref[b, 0:8, :] for b in range(begin, end)], 1)),
        preferred_element_type=jnp.float32)

    def initial(old, count, start):
        if old is None:
            return [jnp.zeros((CHUNK, LANES), jnp.float32) for _ in range(count)]
        return [old[k, start : start + CHUNK, :] for k in range(count)]

    for start in range(0, LANES, CHUNK):
        rows = slice(start, start + CHUNK)
        sums = initial(old1, 10, start)
        for tile in range(tiles):
            at, after = slice(tile * LANES, (tile + 1) * LANES), slice((tiles + tile) * LANES, (tiles + tile + 1) * LANES)
            row = [seg_ref[k, tile : tile + 1, :] for k in range(11)]
            by_normal, by_dist2, by_along = pair_terms(
                reach1_ref[rows, after], reach1_ref[rows, at], cross1_ref[rows, at], row[9], row[10],
                scale1_ref[rows, at], False)
            for axis in range(3):
                sums[axis] += by_normal * row[3 + axis]
                sums[3 + axis] += by_normal * row[6 + axis]
                sums[6 + axis] += by_along * row[3 + axis] - by_dist2 * row[axis]
            sums[9] += by_dist2
        for k in range(10):
            new1[k, rows, :] = sums[k]

    if between is not None:
        between()

    for start in range(0, own_seg, CHUNK):
        rows, under = slice(start, start + CHUNK), slice(own_seg + start, own_seg + start + CHUNK)
        span, span_core = col2_ref[6, rows, :], col2_ref[7, rows, :]
        sums = initial(old2, 12, start)
        for block in range(blocks):
            at = slice(block * LANES, (block + 1) * LANES)
            row = [rec_ref[k, block : block + 1, :] for k in range(9)]
            by_normal, by_dist2, by_along, by_span2 = pair_terms(
                reach2_ref[under, at], reach2_ref[rows, at], cross2_ref[rows, at], span, span_core,
                scale2_ref[rows, at], True)
            for axis in range(3):
                sums[axis] += by_normal * row[3 + axis]
                sums[3 + axis] += by_normal * row[6 + axis] + by_along * row[axis]
                sums[6 + axis] += by_dist2 * row[axis]
            sums[9] += by_along
            sums[10] += by_span2
            sums[11] += by_dist2
        for k in range(12):
            new2[k, rows, :] = sums[k]


def lane_sums(values):
    rows = values[0].shape[0]
    column = lax.broadcasted_iota(jnp.int32, (rows, 16), 1)
    result = jnp.zeros((rows, 16), jnp.float32)
    for index, value in enumerate(values):
        result = jnp.where(column == index, jnp.sum(value, axis=1, keepdims=True), result)
    return result


def receiver_totals(sums_ref, col_ref):
    parts = []
    for start in range(0, LANES, FINISH):
        sums = [sums_ref[k, start : start + FINISH, :] for k in range(10)]
        col = [col_ref[k, start : start + FINISH, :] for k in range(6)]
        by_point = [a + b + p * sums[9] for a, b, p in zip(cross(col[3:6], sums[0:3]), sums[6:9], col[0:3])]
        by_normal = [a - b for a, b in zip(cross(sums[0:3], col[0:3]), sums[3:6])]
        parts.append(lane_sums(by_point + by_normal))
    return jnp.transpose(jnp.concatenate(parts, 0))


def segment_totals(sums_ref, col_ref, own_seg, arriving, leaving):
    parts = []
    for start in range(0, own_seg, FINISH):
        sums = [sums_ref[k, start : start + FINISH, :] for k in range(12)]
        col = [col_ref[k, start : start + FINISH, :] for k in range(6)]
        turned, swept = cross(col[0:3], sums[0:3]), cross(sums[0:3], col[3:6])
        by_s = [sums[3 + k] - turned[k] - col[k] * sums[9] + col[3 + k] * sums[10] for k in range(3)]
        by_both = [
            by_s[k] + (swept[k] + sums[6 + k] - col[k] * sums[11] + col[3 + k] * sums[9]) for k in range(3)]
        if start + FINISH == own_seg:
            last = lax.broadcasted_iota(jnp.int32, (FINISH, LANES), 0) == FINISH - 1
            by_s = [jnp.where(last, a, b) for a, b in zip(arriving, by_s)]
            by_both = [jnp.where(last, a, b) for a, b in zip(leaving, by_both)]
        parts.append(lane_sums(by_s + by_both))
    return jnp.transpose(jnp.concatenate(parts, 0))


def own_receivers(data_ref):
    point = tuple(data_ref[0, 8 + axis : 9 + axis, :] for axis in range(3))
    normal = tuple(data_ref[0, 11 + axis : 12 + axis, :] for axis in range(3))
    return point, normal, cross(point, normal)


def own_segments(own_block, own_seg):
    lane = lax.broadcasted_iota(jnp.int32, (1, LANES), 1)
    first = pltpu.roll(own_block, own_seg, 1)
    second = jnp.where(lane == own_seg - 1, first, pltpu.roll(first, LANES - 1, 1))
    own_e = tuple(first[axis : axis + 1] for axis in range(3))
    segment, turn, span, span_core = segment_terms(own_e, tuple(second[axis : axis + 1] for axis in range(3)))
    return own_e, segment, turn, span, span_core


def early_kernel(chained, own_seg, *refs):
    data_ref, own_refs, rest = refs[0], refs[1:9], refs[9:]
    olds = rest[0:2] if chained else (None, None)
    rest = rest[2:] if chained else rest
    pair_sums(data_ref, own_refs, 0, data_ref.shape[0], own_seg, rest[2:], *olds, rest[0], rest[1])


def last_kernel(count, own_seg, *refs):
    data_ref, own_refs, old1_ref, old2_ref, rcv_out, vert_out, after_ref, new1_ref, new2_ref = (
        refs[0], refs[1:9], *refs[9:16])
    scratch = refs[16:]
    masks = exchange_masks(count)
    me = lax.axis_index("src")
    lane = lax.broadcasted_iota(jnp.int32, (1, LANES), 1)

    def place(device):
        return place_of((device & (count - 1)) ^ me, masks)

    def edge_sums():
        for block in range(count):
            after_ref[block] = data_ref[place((me ^ mask_at(block, masks)) + 1), 16:24, :]

        def spread(column):
            return jnp.broadcast_to(column, (column.shape[0], LANES))

        own_block = data_ref[0, 16:24, :]
        before = data_ref[place(me + count - 1), 16:24, :]
        own_p, own_n, own_m = own_receivers(data_ref)
        point = tuple(data_ref[:, 8 + axis, :] for axis in range(3))
        normal = tuple(data_ref[:, 11 + axis, :] for axis in range(3))
        moment = cross(point, normal)
        mine_last = spread(own_block[:, 2 * own_seg - 1 : 2 * own_seg])
        mine_next = spread(after_ref[0, :, own_seg : own_seg + 1])
        mine_weight = spread(own_block[:, own_seg - 1 : own_seg])
        before_last = spread(before[:, 2 * own_seg - 1 : 2 * own_seg])
        before_weight = spread(jnp.where(me == 0, 0.0, before[:, own_seg - 1 : own_seg]))
        mine_first = spread(own_block[:, own_seg : own_seg + 1])

        def rows(value, axis):
            return jnp.broadcast_to(value[axis : axis + 1], (count, LANES))

        def stacked(own, every):
            return tuple(
                jnp.concatenate([jnp.broadcast_to(a, (count, LANES)), b, b], 0) for a, b in zip(own, every))

        first = tuple(
            jnp.concatenate(
                [spread(data_ref[:, 16 + axis, 2 * own_seg - 1 : 2 * own_seg]), rows(mine_last, axis), rows(before_last, axis)], 0)
            for axis in range(3))
        second = tuple(
            jnp.concatenate(
                [spread(after_ref[:, axis, own_seg : own_seg + 1]), rows(mine_next, axis), rows(mine_first, axis)], 0)
            for axis in range(3))
        scales = [jnp.zeros((count, LANES), jnp.float32)] * 3
        for mode in range(8):
            left = data_ref[:, mode, :]
            scales[0] += spread(data_ref[:, 16 + mode, own_seg - 1 : own_seg]) * data_ref[0, mode : mode + 1, :]
            scales[1] += mine_weight[mode : mode + 1] * left
            scales[2] += before_weight[mode : mode + 1] * left
        segment, turn, span, span_core = segment_terms(first, second)
        normals = stacked(own_n, normal)
        rel = tuple(p - e for p, e in zip(stacked(own_p, point), first))
        by_normal, by_dist2, by_along, by_span2 = pair_terms(
            dot3(rel, rel), dot3(segment, rel), normal_cross(normals, stacked(own_m, moment), segment, turn),
            span, span_core, jnp.concatenate(scales, 0), True)

        def down(value):
            return jnp.sum(value, axis=0, keepdims=True)

        against_own, mine, ahead = slice(0, count), slice(count, 2 * count), slice(2 * count, 3 * count)
        swung, swept = cross(rel, normals), cross(normals, segment)
        edge_s = [(by_normal * segment[axis])[against_own] for axis in range(3)]
        edge_t = [(by_normal * turn[axis])[against_own] for axis in range(3)]
        edge_point = [a for a in cross(own_n, edge_s)]
        edge_normal = [down(a - b) for a, b in zip(cross(edge_s, own_p), edge_t)]
        leaving, arriving = [], []
        for axis in range(3):
            by_s = by_normal * swung[axis] + by_along * rel[axis] + by_span2 * segment[axis]
            by_p = by_dist2 * rel[axis] + by_along * segment[axis]
            by_r = by_normal * swept[axis] + by_p
            edge_point[axis] = down(edge_point[axis] + by_p[against_own])
            leaving.append(down((by_s + by_r)[mine]))
            arriving.append(down(by_s[ahead]))
        return edge_point, edge_normal, arriving, leaving

    found = []
    pair_sums(
        data_ref, own_refs, count - count // 8, count, own_seg, scratch, old1_ref, old2_ref, new1_ref, new2_ref,
        lambda: found.extend((*edge_sums(), receiver_totals(new1_ref, own_refs[0]))))
    edge_point, edge_normal, arriving, leaving, totals = found
    for axis in range(3):
        value = totals[axis : axis + 1] + edge_point[axis]
        rcv_out[axis : axis + 1, :] = 0.2 * value if axis == 2 else value
        rcv_out[3 + axis : 4 + axis, :] = totals[3 + axis : 4 + axis] + edge_normal[axis]

    totals = segment_totals(new2_ref, own_refs[1], own_seg, arriving, leaving)
    for axis in range(3):
        by_second = totals[axis : axis + 1]
        shifted = jnp.concatenate([by_second[:, own_seg - 1 :], by_second[:, : own_seg - 1]], 1)
        result = shifted - totals[3 + axis : 4 + axis]
        vert_out[axis : axis + 1, :] = 0.2 * result if axis == 2 else result


def pair_scratch(blocks, own_seg):
    return [
        pltpu.VMEM((11, blocks // 2, LANES), jnp.float32),
        pltpu.VMEM((9, blocks, LANES), jnp.float32),
        pltpu.VMEM((LANES, blocks // 2 * LANES), jnp.float32),
        pltpu.VMEM((own_seg, blocks * LANES), jnp.float32),
        pltpu.VMEM((8, blocks // 2 * LANES), jnp.float32),
        pltpu.VMEM((8, blocks * LANES), jnp.float32),
        pltpu.VMEM((LANES, blocks // 2 * LANES), jnp.float32),
        pltpu.VMEM((own_seg, blocks * LANES), jnp.float32),
        pltpu.VMEM((8, blocks * LANES), jnp.float32),
        pltpu.VMEM((8, blocks * LANES), jnp.float32),
        pltpu.VMEM((LANES, blocks * LANES), jnp.float32),
        pltpu.VMEM((2 * own_seg, blocks * LANES), jnp.float32),
    ]


def sum_shapes(own_seg):
    return [pltpu.VMEM((10, LANES, LANES), jnp.float32), pltpu.VMEM((12, own_seg, LANES), jnp.float32)]


def last_scratch(count, own_seg):
    return [pltpu.VMEM((count, 8, LANES), jnp.float32)] + sum_shapes(own_seg) + pair_scratch(count // 8, own_seg)


def pair_cost(blocks, own_seg):
    pairs = 2 * blocks * own_seg * LANES
    return pl.CostEstimate(flops=100 * pairs, bytes_accessed=blocks * ROWS * LANES * 4, transcendentals=3 * pairs)


def on_device(rcv_points, rcv_normals, left_modes, vertices, connect, right_modes, mode_weights):
    count = lax.axis_size("src")
    own_seg = vertices.shape[1]
    value = pl.pallas_call(
        functools.partial(pack_kernel, own_seg),
        out_shape=pltpu.VMEM((ROWS, LANES), jnp.float32),
        in_specs=[VMEM] * 6 + [pl.BlockSpec(memory_space=pltpu.SMEM)],
        out_specs=VMEM,
    )(rcv_points, rcv_normals, left_modes, vertices, connect, right_modes, mode_weights)[None]
    params = pltpu.CompilerParams(vmem_limit_bytes=24 << 20)
    own = pl.pallas_call(
        functools.partial(own_kernel, own_seg),
        out_shape=(
            pltpu.VMEM((6, LANES, LANES), jnp.float32),
            pltpu.VMEM((8, own_seg, LANES), jnp.float32),
            pltpu.VMEM((LANES, 32), jnp.bfloat16),
            pltpu.VMEM((own_seg, 32), jnp.bfloat16),
            pltpu.VMEM((LANES, 32), jnp.bfloat16),
            pltpu.VMEM((own_seg, 32), jnp.bfloat16),
            pltpu.VMEM((LANES, 48), jnp.bfloat16),
            pltpu.VMEM((2 * own_seg, 48), jnp.bfloat16),
        ),
        in_specs=[VMEM],
        out_specs=(VMEM,) * 8,
        cost_estimate=pair_cost(2, own_seg),
        compiler_params=params,
    )(value)

    def exchange(block, mask):
        return lax.ppermute(block, "src", [(s, s ^ mask) for s in range(count)])

    def add_pairs(block, *sums):
        return pl.pallas_call(
            functools.partial(early_kernel, len(sums) > 0, own_seg),
            out_shape=tuple(sum_shapes(own_seg)),
            in_specs=[VMEM] * (9 + len(sums)),
            out_specs=(VMEM, VMEM),
            scratch_shapes=pair_scratch(block.shape[0], own_seg),
            cost_estimate=pair_cost(block.shape[0], own_seg),
            compiler_params=params,
        )(block, *own, *sums)

    masks = exchange_masks(count)
    for mask in masks[:-3]:
        value = jnp.concatenate([value, exchange(value, mask)], 0)
    arrived, early = exchange(value, masks[-3]), exchange(value, masks[-2])
    late = exchange(arrived, masks[-2])
    value = jnp.concatenate([value, arrived], 0)
    beside, beside_early = exchange(value, masks[-1]), exchange(early, masks[-1])
    sums = add_pairs(value)
    sums = add_pairs(beside, *sums)
    late, sums = lax.optimization_barrier((late, sums))
    beside_late = exchange(late, masks[-1])
    sums = add_pairs(jnp.concatenate([early, late, beside_early], 0), *sums)
    value = jnp.concatenate([value, early, late, beside, beside_early, beside_late], 0)
    return pl.pallas_call(
        functools.partial(last_kernel, count, own_seg),
        out_shape=(
            jax.ShapeDtypeStruct((6, LANES), jnp.float32),
            jax.ShapeDtypeStruct((3, own_seg), jnp.float32),
        ),
        in_specs=[VMEM] * 11,
        out_specs=(VMEM, VMEM),
        scratch_shapes=last_scratch(count, own_seg),
        cost_estimate=pair_cost(count // 8, own_seg),
        compiler_params=params,
    )(value, *own, *sums)


def solution(mesh):
    split = P(None, ("group", "src"))
    return jax.shard_map(
        on_device, mesh=mesh, in_specs=(split,) * 6 + (P("group"),), out_specs=(split, split), check_vma=False
    )
```

```python
import functools
import math

import jax
import jax.numpy as jnp
from jax import lax
from jax.experimental import pallas as pl
from jax.experimental.pallas import tpu as pltpu
from jax.sharding import PartitionSpec as P

core_term = 0.05
inverse_four_pi = 0.25 / math.pi

LANES = 128
ROWS = 24
CHUNK = 64
FINISH = 32
VMEM = pl.BlockSpec(memory_space=pltpu.VMEM)


def exchange_masks(count):
    masks = []
    step = count // 2
    while step > 1:
        masks.append(step + 1)
        step //= 2
    return masks + [1]


def mask_at(place, masks):
    value = 0
    for bit, mask in enumerate(masks):
        if place >> bit & 1:
            value ^= mask
    return value


def place_of(value, masks):
    place = 0
    rest = value & 1
    for bit, mask in enumerate(masks[:-1]):
        taken = lax.shift_right_logical(value, mask.bit_length() - 1) & 1
        place = place + taken * (1 << bit)
        rest = rest ^ taken
    return place + rest * (1 << (len(masks) - 1))


def high_low(value):
    high = value.astype(jnp.bfloat16).astype(jnp.float32)
    return high, value - high


def dot_nt(left, right):
    return lax.dot_general(left, right, (((1,), (1,)), ((), ())), preferred_element_type=jnp.float32)


def cross(a, b):
    return (a[1] * b[2] - a[2] * b[1], a[2] * b[0] - a[0] * b[2], a[0] * b[1] - a[1] * b[0])


def normal_cross(normal, moment, segment, turn):
    return (moment[0] * segment[0] + moment[1] * segment[1] + moment[2] * segment[2]) - (
        normal[0] * turn[0] + normal[1] * turn[1] + normal[2] * turn[2]
    )


def pair_terms(point, cross_n, first, segment, span, span_core, scale, want_span):
    rel = tuple(p - e for p, e in zip(point, first))
    dist_sq = rel[0] * rel[0] + rel[1] * rel[1] + rel[2] * rel[2]
    along = segment[0] * rel[0] + segment[1] * rel[1] + segment[2] * rel[2]
    other = along - span
    second_sq = dist_sq - along - other
    inv_first = lax.rsqrt(dist_sq)
    inv_second = lax.rsqrt(second_sq)
    inv_den = 1.0 / ((span * dist_sq + span_core) - along * along)
    part_first = along * inv_first
    part_second = other * inv_second
    line = part_first - part_second
    scaled = scale * inv_den
    by_normal = scaled * line
    by_line = scaled * cross_n
    by_den = (by_normal * cross_n) * inv_den
    by_den2 = by_den + by_den
    cube_first = part_first * (inv_first * inv_first)
    cube_second = part_second * (inv_second * inv_second)
    by_dist2 = by_line * (cube_second - cube_first) - by_den2 * span
    by_along = by_line * ((inv_first - inv_second) - cube_second) + by_den2 * along
    if not want_span:
        return rel, by_normal, by_dist2, by_along
    by_span2 = by_line * ((inv_second + inv_second) + cube_second) - by_den2 * (dist_sq + core_term)
    return rel, by_normal, by_dist2, by_along, by_span2


def segment_terms(first, second):
    segment = tuple(b - a for a, b in zip(first, second))
    span = segment[0] * segment[0] + segment[1] * segment[1] + segment[2] * segment[2]
    return segment, cross(segment, first), span, core_term * span + core_term


def pack_kernel(own_seg, points_ref, normals_ref, left_ref, vertices_ref, connect_ref, right_ref, weights_ref, out_ref):
    base = lax.axis_index("src") * own_seg
    row8 = lax.broadcasted_iota(jnp.int32, (8, LANES), 0)
    weight = jnp.zeros((8, LANES), jnp.float32)
    for mode in range(8):
        weight = jnp.where(row8 == mode, weights_ref[mode], weight)
    weighted = right_ref[...] * (weight * inverse_four_pi)
    high, rest = high_low(weighted)
    middle, low = high_low(rest)
    parts = jnp.concatenate([high, middle, low, jnp.zeros_like(low)], 0).astype(jnp.bfloat16)
    local = connect_ref[0:1, :] - base
    hit = lax.broadcasted_iota(jnp.int32, (LANES, LANES), 0) == local
    folded = dot_nt(parts, hit.astype(jnp.float32).astype(jnp.bfloat16))
    folded = folded[0:8] + (folded[8:16] + folded[16:24])
    out_ref[0:8, :] = left_ref[...]
    out_ref[8:10, :] = points_ref[0:2, :]
    out_ref[10:11, :] = 0.5 + 0.2 * points_ref[2:3, :]
    out_ref[11:14, :] = normals_ref[...]
    out_ref[14:16, :] = jnp.zeros((2, LANES), jnp.float32)
    out_ref[16:24, :] = folded
    out_ref[16:18, own_seg : 2 * own_seg] = vertices_ref[0:2, :]
    out_ref[18:19, own_seg : 2 * own_seg] = 0.2 * vertices_ref[2:3, :]


def stack_hhll(rows):
    high, low = high_low(rows)
    return jnp.transpose(jnp.concatenate([high, high, low, low], 0)).astype(jnp.bfloat16)


def stack_hlhl(rows):
    high, low = high_low(rows)
    both = jnp.concatenate([high, low], 0).astype(jnp.bfloat16)
    return jnp.concatenate([both, both], 0)


def lane_edges(own_seg):
    lane = lax.broadcasted_iota(jnp.int32, (1, LANES), 1)
    return (lane == own_seg - 1) | (lane == 2 * own_seg - 1)


def own_kernel(own_seg, data_ref, col1_ref, col2_ref, left_ref, right_ref, moment_ref, turn_ref):
    def columns(rows, out_ref):
        pad = jnp.zeros((16 - len(rows), LANES), jnp.float32)
        cols = jnp.transpose(jnp.concatenate(list(rows) + [pad], 0))
        count = out_ref.shape[1]
        for k in range(len(rows)):
            out_ref[k] = jnp.broadcast_to(cols[0:count, k : k + 1], (count, LANES))

    own_block = data_ref[0, 16:24, :]
    point, normal, moment = own_receivers(data_ref)
    columns([*point, *normal], col1_ref)
    own_e, own_s, own_t, span, span_core = own_segments(own_block, own_seg)
    columns([*own_e, *own_s, span, span_core], col2_ref)
    left_ref[...] = stack_hhll(data_ref[0, 0:8, :])
    right_ref[...] = stack_hhll(jnp.where(lane_edges(own_seg), 0.0, own_block))[0:own_seg]
    pad = jnp.zeros((2, LANES), jnp.float32)
    moment_ref[...] = stack_hhll(jnp.concatenate([*moment, *normal, pad], 0))
    turn_ref[...] = stack_hhll(jnp.concatenate([*own_s, *(-value for value in own_t), pad], 0))[0:own_seg]


def pair_sums(data_ref, own_refs, begin, end, own_seg, scratch, old1, old2, new1, new2, between=None):
    seg_ref, rec_ref, scale1_ref, scale2_ref, row1_ref, row2_ref, cross1_ref, cross2_ref = scratch
    col1_ref, col2_ref, left_ref, right_ref, moment_ref, turn_ref = own_refs
    blocks = end - begin
    tiles = blocks // 2
    lane = lax.broadcasted_iota(jnp.int32, (1, LANES), 1)
    low_half = lane < own_seg
    at_edge = lane_edges(own_seg)

    folded = []
    for tile in range(tiles):
        block_a, block_b = data_ref[begin + 2 * tile, 16:24, :], data_ref[begin + 2 * tile + 1, 16:24, :]
        both = jnp.where(low_half, block_a, pltpu.roll(block_b, own_seg, 1))
        folded.append(jnp.where(at_edge, 0.0, both))
        first = jnp.where(low_half, pltpu.roll(block_a, own_seg, 1), block_b)
        second = jnp.where(at_edge, first, pltpu.roll(first, LANES - 1, 1))
        for axis in range(3):
            seg_ref[axis, tile : tile + 1, :] = first[axis : axis + 1]
            seg_ref[3 + axis, tile : tile + 1, :] = second[axis : axis + 1]
    first = tuple(seg_ref[axis] for axis in range(3))
    segment, turn, span, span_core = segment_terms(first, tuple(seg_ref[3 + axis] for axis in range(3)))
    for axis in range(3):
        seg_ref[3 + axis] = segment[axis]
        seg_ref[6 + axis] = turn[axis]
    seg_ref[9] = span
    seg_ref[10] = span_core

    point = tuple(data_ref[begin:end, 8 + axis, :] for axis in range(3))
    normal = tuple(data_ref[begin:end, 11 + axis, :] for axis in range(3))
    moment = cross(point, normal)
    for axis in range(3):
        rec_ref[axis] = point[axis]
        rec_ref[3 + axis] = normal[axis]
        rec_ref[6 + axis] = moment[axis]

    for ref in (row1_ref, row2_ref):
        ref[6:8, :] = jnp.zeros((2, ref.shape[1]), jnp.float32)
    for axis in range(3):
        for tile in range(tiles):
            at = slice(tile * LANES, (tile + 1) * LANES)
            row1_ref[axis : axis + 1, at] = segment[axis][tile : tile + 1]
            row1_ref[3 + axis : 4 + axis, at] = -turn[axis][tile : tile + 1]
        for block in range(blocks):
            at = slice(block * LANES, (block + 1) * LANES)
            row2_ref[axis : axis + 1, at] = moment[axis][block : block + 1]
            row2_ref[3 + axis : 4 + axis, at] = normal[axis][block : block + 1]
    cross1_ref[...] = jnp.dot(moment_ref[...], stack_hlhl(row1_ref[...]), preferred_element_type=jnp.float32)
    cross2_ref[...] = jnp.dot(turn_ref[...], stack_hlhl(row2_ref[...]), preferred_element_type=jnp.float32)

    scale1_ref[...] = jnp.dot(
        left_ref[...], stack_hlhl(jnp.concatenate(folded, 1)), preferred_element_type=jnp.float32)
    scale2_ref[...] = jnp.dot(
        right_ref[...], stack_hlhl(jnp.concatenate([data_ref[b, 0:8, :] for b in range(begin, end)], 1)),
        preferred_element_type=jnp.float32)

    def initial(old, count, start):
        if old is None:
            return [jnp.zeros((CHUNK, LANES), jnp.float32) for _ in range(count)]
        return [old[k, start : start + CHUNK, :] for k in range(count)]

    for start in range(0, LANES, CHUNK):
        col = [col1_ref[k, start : start + CHUNK, :] for k in range(3)]
        sums = initial(old1, 9, start)
        for tile in range(tiles):
            row = [seg_ref[k, tile : tile + 1, :] for k in range(11)]
            scale = scale1_ref[start : start + CHUNK, tile * LANES : (tile + 1) * LANES]
            rel, by_normal, by_dist2, by_along = pair_terms(
                col, cross1_ref[start : start + CHUNK, tile * LANES : (tile + 1) * LANES],
                row[0:3], row[3:6], row[9], row[10], scale, False)
            for axis in range(3):
                sums[axis] += by_normal * row[3 + axis]
                sums[3 + axis] += by_normal * row[6 + axis]
                sums[6 + axis] += by_dist2 * rel[axis] + by_along * row[3 + axis]
        for k in range(9):
            new1[k, start : start + CHUNK, :] = sums[k]

    if between is not None:
        between()

    for start in range(0, own_seg, CHUNK):
        col = [col2_ref[k, start : start + CHUNK, :] for k in range(8)]
        sums = initial(old2, 11, start)
        for block in range(blocks):
            row = [rec_ref[k, block : block + 1, :] for k in range(9)]
            scale = scale2_ref[start : start + CHUNK, block * LANES : (block + 1) * LANES]
            rel, by_normal, by_dist2, by_along, by_span2 = pair_terms(
                row[0:3], cross2_ref[start : start + CHUNK, block * LANES : (block + 1) * LANES],
                col[0:3], col[3:6], col[6], col[7], scale, True)
            for axis in range(3):
                sums[axis] += by_normal * row[3 + axis]
                sums[3 + axis] += by_normal * row[6 + axis] + by_along * rel[axis]
                sums[6 + axis] += by_dist2 * rel[axis]
            sums[9] += by_along
            sums[10] += by_span2
        for k in range(11):
            new2[k, start : start + CHUNK, :] = sums[k]


def lane_sums(values):
    rows = values[0].shape[0]
    column = lax.broadcasted_iota(jnp.int32, (rows, 16), 1)
    result = jnp.zeros((rows, 16), jnp.float32)
    for index, value in enumerate(values):
        result = jnp.where(column == index, jnp.sum(value, axis=1, keepdims=True), result)
    return result


def receiver_totals(sums_ref, col_ref):
    parts = []
    for start in range(0, LANES, FINISH):
        sums = [sums_ref[k, start : start + FINISH, :] for k in range(9)]
        col = [col_ref[k, start : start + FINISH, :] for k in range(6)]
        by_point = [a + b for a, b in zip(cross(col[3:6], sums[0:3]), sums[6:9])]
        by_normal = [a - b for a, b in zip(cross(sums[0:3], col[0:3]), sums[3:6])]
        parts.append(lane_sums(by_point + by_normal))
    return jnp.transpose(jnp.concatenate(parts, 0))


def segment_totals(sums_ref, col_ref, own_seg, arriving, leaving):
    parts = []
    for start in range(0, own_seg, FINISH):
        sums = [sums_ref[k, start : start + FINISH, :] for k in range(11)]
        col = [col_ref[k, start : start + FINISH, :] for k in range(6)]
        turned, swept = cross(col[0:3], sums[0:3]), cross(sums[0:3], col[3:6])
        by_s = [sums[3 + k] - turned[k] + col[3 + k] * sums[10] for k in range(3)]
        by_both = [by_s[k] + (swept[k] + sums[6 + k] + col[3 + k] * sums[9]) for k in range(3)]
        if start + FINISH == own_seg:
            last = lax.broadcasted_iota(jnp.int32, (FINISH, LANES), 0) == FINISH - 1
            by_s = [jnp.where(last, a, b) for a, b in zip(arriving, by_s)]
            by_both = [jnp.where(last, a, b) for a, b in zip(leaving, by_both)]
        parts.append(lane_sums(by_s + by_both))
    return jnp.transpose(jnp.concatenate(parts, 0))


def own_receivers(data_ref):
    point = tuple(data_ref[0, 8 + axis : 9 + axis, :] for axis in range(3))
    normal = tuple(data_ref[0, 11 + axis : 12 + axis, :] for axis in range(3))
    return point, normal, cross(point, normal)


def own_segments(own_block, own_seg):
    lane = lax.broadcasted_iota(jnp.int32, (1, LANES), 1)
    first = pltpu.roll(own_block, own_seg, 1)
    second = jnp.where(lane == own_seg - 1, first, pltpu.roll(first, LANES - 1, 1))
    own_e = tuple(first[axis : axis + 1] for axis in range(3))
    segment, turn, span, span_core = segment_terms(own_e, tuple(second[axis : axis + 1] for axis in range(3)))
    return own_e, segment, turn, span, span_core


def early_kernel(chained, own_seg, *refs):
    data_ref, own_refs, rest = refs[0], refs[1:7], refs[7:]
    olds = rest[0:2] if chained else (None, None)
    rest = rest[2:] if chained else rest
    pair_sums(data_ref, own_refs, 0, data_ref.shape[0], own_seg, rest[2:], *olds, rest[0], rest[1])


def last_kernel(count, own_seg, *refs):
    data_ref, own_refs, old1_ref, old2_ref, rcv_out, vert_out, after_ref, new1_ref, new2_ref = (
        refs[0], refs[1:7], *refs[7:14])
    scratch = refs[14:]
    masks = exchange_masks(count)
    me = lax.axis_index("src")
    lane = lax.broadcasted_iota(jnp.int32, (1, LANES), 1)

    def place(device):
        return place_of((device & (count - 1)) ^ me, masks)

    def edge_sums():
        for block in range(count):
            after_ref[block] = data_ref[place((me ^ mask_at(block, masks)) + 1), 16:24, :]

        def spread(column):
            return jnp.broadcast_to(column, (column.shape[0], LANES))

        own_block = data_ref[0, 16:24, :]
        before = data_ref[place(me + count - 1), 16:24, :]
        own_p, own_n, own_m = own_receivers(data_ref)
        point = tuple(data_ref[:, 8 + axis, :] for axis in range(3))
        normal = tuple(data_ref[:, 11 + axis, :] for axis in range(3))
        moment = cross(point, normal)
        mine_last = spread(own_block[:, 2 * own_seg - 1 : 2 * own_seg])
        mine_next = spread(after_ref[0, :, own_seg : own_seg + 1])
        mine_weight = spread(own_block[:, own_seg - 1 : own_seg])
        before_last = spread(before[:, 2 * own_seg - 1 : 2 * own_seg])
        before_weight = spread(jnp.where(me == 0, 0.0, before[:, own_seg - 1 : own_seg]))
        mine_first = spread(own_block[:, own_seg : own_seg + 1])

        def rows(value, axis):
            return jnp.broadcast_to(value[axis : axis + 1], (count, LANES))

        def stacked(own, every):
            return tuple(
                jnp.concatenate([jnp.broadcast_to(a, (count, LANES)), b, b], 0) for a, b in zip(own, every))

        first = tuple(
            jnp.concatenate(
                [spread(data_ref[:, 16 + axis, 2 * own_seg - 1 : 2 * own_seg]), rows(mine_last, axis), rows(before_last, axis)], 0)
            for axis in range(3))
        second = tuple(
            jnp.concatenate(
                [spread(after_ref[:, axis, own_seg : own_seg + 1]), rows(mine_next, axis), rows(mine_first, axis)], 0)
            for axis in range(3))
        scales = [jnp.zeros((count, LANES), jnp.float32)] * 3
        for mode in range(8):
            left = data_ref[:, mode, :]
            scales[0] += spread(data_ref[:, 16 + mode, own_seg - 1 : own_seg]) * data_ref[0, mode : mode + 1, :]
            scales[1] += mine_weight[mode : mode + 1] * left
            scales[2] += before_weight[mode : mode + 1] * left
        segment, turn, span, span_core = segment_terms(first, second)
        normals = stacked(own_n, normal)
        rel, by_normal, by_dist2, by_along, by_span2 = pair_terms(
            stacked(own_p, point), normal_cross(normals, stacked(own_m, moment), segment, turn),
            first, segment, span, span_core, jnp.concatenate(scales, 0), True)

        def down(value):
            return jnp.sum(value, axis=0, keepdims=True)

        against_own, mine, ahead = slice(0, count), slice(count, 2 * count), slice(2 * count, 3 * count)
        swung, swept = cross(rel, normals), cross(normals, segment)
        edge_s = [(by_normal * segment[axis])[against_own] for axis in range(3)]
        edge_t = [(by_normal * turn[axis])[against_own] for axis in range(3)]
        edge_point = [a for a in cross(own_n, edge_s)]
        edge_normal = [down(a - b) for a, b in zip(cross(edge_s, own_p), edge_t)]
        leaving, arriving = [], []
        for axis in range(3):
            by_s = by_normal * swung[axis] + by_along * rel[axis] + by_span2 * segment[axis]
            by_p = by_dist2 * rel[axis] + by_along * segment[axis]
            by_r = by_normal * swept[axis] + by_p
            edge_point[axis] = down(edge_point[axis] + by_p[against_own])
            leaving.append(down((by_s + by_r)[mine]))
            arriving.append(down(by_s[ahead]))
        return edge_point, edge_normal, arriving, leaving

    found = []
    pair_sums(
        data_ref, own_refs, count - count // 4, count, own_seg, scratch, old1_ref, old2_ref, new1_ref, new2_ref,
        lambda: found.extend((*edge_sums(), receiver_totals(new1_ref, own_refs[0]))))
    edge_point, edge_normal, arriving, leaving, totals = found
    for axis in range(3):
        value = totals[axis : axis + 1] + edge_point[axis]
        rcv_out[axis : axis + 1, :] = 0.2 * value if axis == 2 else value
        rcv_out[3 + axis : 4 + axis, :] = totals[3 + axis : 4 + axis] + edge_normal[axis]

    totals = segment_totals(new2_ref, own_refs[1], own_seg, arriving, leaving)
    for axis in range(3):
        by_second = totals[axis : axis + 1]
        shifted = jnp.concatenate([by_second[:, own_seg - 1 :], by_second[:, : own_seg - 1]], 1)
        result = shifted - totals[3 + axis : 4 + axis]
        vert_out[axis : axis + 1, :] = 0.2 * result if axis == 2 else result


def pair_scratch(blocks, own_seg):
    return [
        pltpu.VMEM((11, blocks // 2, LANES), jnp.float32),
        pltpu.VMEM((9, blocks, LANES), jnp.float32),
        pltpu.VMEM((LANES, blocks // 2 * LANES), jnp.float32),
        pltpu.VMEM((own_seg, blocks * LANES), jnp.float32),
        pltpu.VMEM((8, blocks // 2 * LANES), jnp.float32),
        pltpu.VMEM((8, blocks * LANES), jnp.float32),
        pltpu.VMEM((LANES, blocks // 2 * LANES), jnp.float32),
        pltpu.VMEM((own_seg, blocks * LANES), jnp.float32),
    ]


def sum_shapes(own_seg):
    return [pltpu.VMEM((9, LANES, LANES), jnp.float32), pltpu.VMEM((11, own_seg, LANES), jnp.float32)]


def last_scratch(count, own_seg):
    return [pltpu.VMEM((count, 8, LANES), jnp.float32)] + sum_shapes(own_seg) + pair_scratch(count // 4, own_seg)


def pair_cost(blocks, own_seg):
    pairs = 2 * blocks * own_seg * LANES
    return pl.CostEstimate(flops=100 * pairs, bytes_accessed=blocks * ROWS * LANES * 4, transcendentals=3 * pairs)


def on_device(rcv_points, rcv_normals, left_modes, vertices, connect, right_modes, mode_weights):
    count = lax.axis_size("src")
    own_seg = vertices.shape[1]
    value = pl.pallas_call(
        functools.partial(pack_kernel, own_seg),
        out_shape=pltpu.VMEM((ROWS, LANES), jnp.float32),
        in_specs=[VMEM] * 6 + [pl.BlockSpec(memory_space=pltpu.SMEM)],
        out_specs=VMEM,
    )(rcv_points, rcv_normals, left_modes, vertices, connect, right_modes, mode_weights)[None]
    params = pltpu.CompilerParams(vmem_limit_bytes=24 << 20)
    own = pl.pallas_call(
        functools.partial(own_kernel, own_seg),
        out_shape=(
            pltpu.VMEM((6, LANES, LANES), jnp.float32),
            pltpu.VMEM((8, own_seg, LANES), jnp.float32),
            pltpu.VMEM((LANES, 32), jnp.bfloat16),
            pltpu.VMEM((own_seg, 32), jnp.bfloat16),
            pltpu.VMEM((LANES, 32), jnp.bfloat16),
            pltpu.VMEM((own_seg, 32), jnp.bfloat16),
        ),
        in_specs=[VMEM],
        out_specs=(VMEM,) * 6,
        cost_estimate=pair_cost(2, own_seg),
        compiler_params=params,
    )(value)

    def exchange(block, mask):
        return lax.ppermute(block, "src", [(s, s ^ mask) for s in range(count)])

    def add_pairs(block, *sums):
        return pl.pallas_call(
            functools.partial(early_kernel, len(sums) > 0, own_seg),
            out_shape=tuple(sum_shapes(own_seg)),
            in_specs=[VMEM] * (7 + len(sums)),
            out_specs=(VMEM, VMEM),
            scratch_shapes=pair_scratch(block.shape[0], own_seg),
            cost_estimate=pair_cost(block.shape[0], own_seg),
            compiler_params=params,
        )(block, *own, *sums)

    masks = exchange_masks(count)
    for mask in masks[:-3]:
        value = jnp.concatenate([value, exchange(value, mask)], 0)
    arrived, early = exchange(value, masks[-3]), exchange(value, masks[-2])
    late = exchange(arrived, masks[-2])
    value = jnp.concatenate([value, arrived], 0)
    beside = exchange(value, masks[-1])
    sums = add_pairs(value)
    sums = add_pairs(early, *sums)
    late, sums = lax.optimization_barrier((late, sums))
    across = jnp.concatenate([early, late], 0)
    opposite = exchange(across, masks[-1])
    sums = add_pairs(jnp.concatenate([beside, late], 0), *sums)
    value = jnp.concatenate([value, across, beside, opposite], 0)
    return pl.pallas_call(
        functools.partial(last_kernel, count, own_seg),
        out_shape=(
            jax.ShapeDtypeStruct((6, LANES), jnp.float32),
            jax.ShapeDtypeStruct((3, own_seg), jnp.float32),
        ),
        in_specs=[VMEM] * 9,
        out_specs=(VMEM, VMEM),
        scratch_shapes=last_scratch(count, own_seg),
        cost_estimate=pair_cost(count // 4, own_seg),
        compiler_params=params,
    )(value, *own, *sums)


def solution(mesh):
    split = P(None, ("group", "src"))
    return jax.shard_map(
        on_device, mesh=mesh, in_specs=(split,) * 6 + (P("group"),), out_specs=(split, split), check_vma=False
    )
```

```python
import functools
import math

import jax
import jax.numpy as jnp
from jax import lax
from jax.experimental import pallas as pl
from jax.experimental.pallas import tpu as pltpu
from jax.sharding import PartitionSpec as P

core_term = 0.05
inverse_four_pi = 0.25 / math.pi

LANES = 128
ROWS = 24
CHUNK = 16
FINISH = 16
VMEM = pl.BlockSpec(memory_space=pltpu.VMEM)


def exchange_masks(count):
    masks = []
    step = count // 2
    while step > 1:
        masks.append(step + 1)
        step //= 2
    return masks + [1]


def mask_at(place, masks):
    value = 0
    for bit, mask in enumerate(masks):
        if place >> bit & 1:
            value ^= mask
    return value


def place_of(value, masks):
    place = 0
    rest = value & 1
    for bit, mask in enumerate(masks[:-1]):
        taken = lax.shift_right_logical(value, mask.bit_length() - 1) & 1
        place = place + taken * (1 << bit)
        rest = rest ^ taken
    return place + rest * (1 << (len(masks) - 1))


def high_low(value):
    high = value.astype(jnp.bfloat16).astype(jnp.float32)
    return high, value - high


def dot_nt(left, right):
    return lax.dot_general(left, right, (((1,), (1,)), ((), ())), preferred_element_type=jnp.float32)


def cross(a, b):
    return (a[1] * b[2] - a[2] * b[1], a[2] * b[0] - a[0] * b[2], a[0] * b[1] - a[1] * b[0])


def normal_cross(normal, moment, segment, turn):
    return (moment[0] * segment[0] + moment[1] * segment[1] + moment[2] * segment[2]) - (
        normal[0] * turn[0] + normal[1] * turn[1] + normal[2] * turn[2]
    )


def pair_terms(point, cross_n, first, segment, span, span_core, scale, want_span):
    rel = tuple(p - e for p, e in zip(point, first))
    dist_sq = rel[0] * rel[0] + rel[1] * rel[1] + rel[2] * rel[2]
    along = segment[0] * rel[0] + segment[1] * rel[1] + segment[2] * rel[2]
    other = along - span
    second_sq = dist_sq - along - other
    inv_first = lax.rsqrt(dist_sq)
    inv_second = lax.rsqrt(second_sq)
    inv_den = 1.0 / ((span * dist_sq + span_core) - along * along)
    part_first = along * inv_first
    part_second = other * inv_second
    line = part_first - part_second
    scaled = scale * inv_den
    by_normal = scaled * line
    by_line = scaled * cross_n
    by_den = (by_normal * cross_n) * inv_den
    by_den2 = by_den + by_den
    cube_first = part_first * (inv_first * inv_first)
    cube_second = part_second * (inv_second * inv_second)
    by_dist2 = by_line * (cube_second - cube_first) - by_den2 * span
    by_along = by_line * ((inv_first - inv_second) - cube_second) + by_den2 * along
    if not want_span:
        return rel, by_normal, by_dist2, by_along
    by_span2 = by_line * ((inv_second + inv_second) + cube_second) - by_den2 * (dist_sq + core_term)
    return rel, by_normal, by_dist2, by_along, by_span2


def segment_terms(first, second):
    segment = tuple(b - a for a, b in zip(first, second))
    span = segment[0] * segment[0] + segment[1] * segment[1] + segment[2] * segment[2]
    return segment, cross(segment, first), span, core_term * span + core_term


def pack_kernel(own_seg, points_ref, normals_ref, left_ref, vertices_ref, connect_ref, right_ref, weights_ref, out_ref):
    base = lax.axis_index("src") * own_seg
    row8 = lax.broadcasted_iota(jnp.int32, (8, LANES), 0)
    weight = jnp.zeros((8, LANES), jnp.float32)
    for mode in range(8):
        weight = jnp.where(row8 == mode, weights_ref[mode], weight)
    weighted = right_ref[...] * (weight * inverse_four_pi)
    high, rest = high_low(weighted)
    middle, low = high_low(rest)
    parts = jnp.concatenate([high, middle, low, jnp.zeros_like(low)], 0).astype(jnp.bfloat16)
    local = connect_ref[0:1, :] - base
    hit = lax.broadcasted_iota(jnp.int32, (LANES, LANES), 0) == local
    folded = dot_nt(parts, hit.astype(jnp.float32).astype(jnp.bfloat16))
    folded = folded[0:8] + (folded[8:16] + folded[16:24])
    out_ref[0:8, :] = left_ref[...]
    out_ref[8:10, :] = points_ref[0:2, :]
    out_ref[10:11, :] = 0.5 + 0.2 * points_ref[2:3, :]
    out_ref[11:14, :] = normals_ref[...]
    out_ref[14:16, :] = jnp.zeros((2, LANES), jnp.float32)
    out_ref[16:24, :] = folded
    out_ref[16:18, own_seg : 2 * own_seg] = vertices_ref[0:2, :]
    out_ref[18:19, own_seg : 2 * own_seg] = 0.2 * vertices_ref[2:3, :]


def stack_hhll(rows):
    high, low = high_low(rows)
    return jnp.transpose(jnp.concatenate([high, high, low, low], 0)).astype(jnp.bfloat16)


def stack_hlhl(rows):
    high, low = high_low(rows)
    both = jnp.concatenate([high, low], 0).astype(jnp.bfloat16)
    return jnp.concatenate([both, both], 0)


def lane_edges(own_seg):
    lane = lax.broadcasted_iota(jnp.int32, (1, LANES), 1)
    return (lane == own_seg - 1) | (lane == 2 * own_seg - 1)


def own_kernel(own_seg, data_ref, col1_ref, col2_ref, left_ref, right_ref, moment_ref, turn_ref):
    def columns(rows, out_ref):
        pad = jnp.zeros((16 - len(rows), LANES), jnp.float32)
        cols = jnp.transpose(jnp.concatenate(list(rows) + [pad], 0))
        count = out_ref.shape[1]
        for k in range(len(rows)):
            out_ref[k] = jnp.broadcast_to(cols[0:count, k : k + 1], (count, LANES))

    own_block = data_ref[0, 16:24, :]
    point, normal, moment = own_receivers(data_ref)
    columns([*point, *normal], col1_ref)
    own_e, own_s, own_t, span, span_core = own_segments(own_block, own_seg)
    columns([*own_e, *own_s, span, span_core], col2_ref)
    left_ref[...] = stack_hhll(data_ref[0, 0:8, :])
    right_ref[...] = stack_hhll(jnp.where(lane_edges(own_seg), 0.0, own_block))[0:own_seg]
    pad = jnp.zeros((2, LANES), jnp.float32)
    moment_ref[...] = stack_hhll(jnp.concatenate([*moment, *normal, pad], 0))
    turn_ref[...] = stack_hhll(jnp.concatenate([*own_s, *(-value for value in own_t), pad], 0))[0:own_seg]


def pair_sums(data_ref, own_refs, begin, end, own_seg, scratch, old1, old2, new1, new2, between=None):
    seg_ref, rec_ref, scale1_ref, scale2_ref, row1_ref, row2_ref, cross1_ref, cross2_ref = scratch
    col1_ref, col2_ref, left_ref, right_ref, moment_ref, turn_ref = own_refs
    blocks = end - begin
    tiles = blocks // 2
    lane = lax.broadcasted_iota(jnp.int32, (1, LANES), 1)
    low_half = lane < own_seg
    at_edge = lane_edges(own_seg)

    folded = []
    for tile in range(tiles):
        block_a, block_b = data_ref[begin + 2 * tile, 16:24, :], data_ref[begin + 2 * tile + 1, 16:24, :]
        both = jnp.where(low_half, block_a, pltpu.roll(block_b, own_seg, 1))
        folded.append(jnp.where(at_edge, 0.0, both))
        first = jnp.where(low_half, pltpu.roll(block_a, own_seg, 1), block_b)
        second = jnp.where(at_edge, first, pltpu.roll(first, LANES - 1, 1))
        for axis in range(3):
            seg_ref[axis, tile : tile + 1, :] = first[axis : axis + 1]
            seg_ref[3 + axis, tile : tile + 1, :] = second[axis : axis + 1]
    first = tuple(seg_ref[axis] for axis in range(3))
    segment, turn, span, span_core = segment_terms(first, tuple(seg_ref[3 + axis] for axis in range(3)))
    for axis in range(3):
        seg_ref[3 + axis] = segment[axis]
        seg_ref[6 + axis] = turn[axis]
    seg_ref[9] = span
    seg_ref[10] = span_core

    point = tuple(data_ref[begin:end, 8 + axis, :] for axis in range(3))
    normal = tuple(data_ref[begin:end, 11 + axis, :] for axis in range(3))
    moment = cross(point, normal)
    for axis in range(3):
        rec_ref[axis] = point[axis]
        rec_ref[3 + axis] = normal[axis]
        rec_ref[6 + axis] = moment[axis]

    for ref in (row1_ref, row2_ref):
        ref[6:8, :] = jnp.zeros((2, ref.shape[1]), jnp.float32)
    for axis in range(3):
        for tile in range(tiles):
            at = slice(tile * LANES, (tile + 1) * LANES)
            row1_ref[axis : axis + 1, at] = segment[axis][tile : tile + 1]
            row1_ref[3 + axis : 4 + axis, at] = -turn[axis][tile : tile + 1]
        for block in range(blocks):
            at = slice(block * LANES, (block + 1) * LANES)
            row2_ref[axis : axis + 1, at] = moment[axis][block : block + 1]
            row2_ref[3 + axis : 4 + axis, at] = normal[axis][block : block + 1]
    cross1_ref[...] = jnp.dot(moment_ref[...], stack_hlhl(row1_ref[...]), preferred_element_type=jnp.float32)
    cross2_ref[...] = jnp.dot(turn_ref[...], stack_hlhl(row2_ref[...]), preferred_element_type=jnp.float32)

    scale1_ref[...] = jnp.dot(
        left_ref[...], stack_hlhl(jnp.concatenate(folded, 1)), preferred_element_type=jnp.float32)
    scale2_ref[...] = jnp.dot(
        right_ref[...], stack_hlhl(jnp.concatenate([data_ref[b, 0:8, :] for b in range(begin, end)], 1)),
        preferred_element_type=jnp.float32)

    def initial(old, count, start):
        if old is None:
            return [jnp.zeros((CHUNK, LANES), jnp.float32) for _ in range(count)]
        return [old[k, start : start + CHUNK, :] for k in range(count)]

    for start in range(0, LANES, CHUNK):
        col = [col1_ref[k, start : start + CHUNK, :] for k in range(3)]
        sums = initial(old1, 9, start)
        for tile in range(tiles):
            row = [seg_ref[k, tile : tile + 1, :] for k in range(11)]
            scale = scale1_ref[start : start + CHUNK, tile * LANES : (tile + 1) * LANES]
            rel, by_normal, by_dist2, by_along = pair_terms(
                col, cross1_ref[start : start + CHUNK, tile * LANES : (tile + 1) * LANES],
                row[0:3], row[3:6], row[9], row[10], scale, False)
            for axis in range(3):
                sums[axis] += by_normal * row[3 + axis]
                sums[3 + axis] += by_normal * row[6 + axis]
                sums[6 + axis] += by_dist2 * rel[axis] + by_along * row[3 + axis]
        for k in range(9):
            new1[k, start : start + CHUNK, :] = sums[k]

    if between is not None:
        between()

    for start in range(0, own_seg, CHUNK):
        col = [col2_ref[k, start : start + CHUNK, :] for k in range(8)]
        sums = initial(old2, 11, start)
        for block in range(blocks):
            row = [rec_ref[k, block : block + 1, :] for k in range(9)]
            scale = scale2_ref[start : start + CHUNK, block * LANES : (block + 1) * LANES]
            rel, by_normal, by_dist2, by_along, by_span2 = pair_terms(
                row[0:3], cross2_ref[start : start + CHUNK, block * LANES : (block + 1) * LANES],
                col[0:3], col[3:6], col[6], col[7], scale, True)
            for axis in range(3):
                sums[axis] += by_normal * row[3 + axis]
                sums[3 + axis] += by_normal * row[6 + axis] + by_along * rel[axis]
                sums[6 + axis] += by_dist2 * rel[axis]
            sums[9] += by_along
            sums[10] += by_span2
        for k in range(11):
            new2[k, start : start + CHUNK, :] = sums[k]


def lane_sums(values):
    rows = values[0].shape[0]
    column = lax.broadcasted_iota(jnp.int32, (rows, 16), 1)
    result = jnp.zeros((rows, 16), jnp.float32)
    for index, value in enumerate(values):
        result = jnp.where(column == index, jnp.sum(value, axis=1, keepdims=True), result)
    return result


def receiver_totals(sums_ref, col_ref):
    parts = []
    for start in range(0, LANES, FINISH):
        sums = [sums_ref[k, start : start + FINISH, :] for k in range(9)]
        col = [col_ref[k, start : start + FINISH, :] for k in range(6)]
        by_point = [a + b for a, b in zip(cross(col[3:6], sums[0:3]), sums[6:9])]
        by_normal = [a - b for a, b in zip(cross(sums[0:3], col[0:3]), sums[3:6])]
        parts.append(lane_sums(by_point + by_normal))
    return jnp.transpose(jnp.concatenate(parts, 0))


def segment_totals(sums_ref, col_ref, own_seg, arriving, leaving):
    parts = []
    for start in range(0, own_seg, FINISH):
        sums = [sums_ref[k, start : start + FINISH, :] for k in range(11)]
        col = [col_ref[k, start : start + FINISH, :] for k in range(6)]
        turned, swept = cross(col[0:3], sums[0:3]), cross(sums[0:3], col[3:6])
        by_s = [sums[3 + k] - turned[k] + col[3 + k] * sums[10] for k in range(3)]
        by_both = [by_s[k] + (swept[k] + sums[6 + k] + col[3 + k] * sums[9]) for k in range(3)]
        if start + FINISH == own_seg:
            last = lax.broadcasted_iota(jnp.int32, (FINISH, LANES), 0) == FINISH - 1
            by_s = [jnp.where(last, a, b) for a, b in zip(arriving, by_s)]
            by_both = [jnp.where(last, a, b) for a, b in zip(leaving, by_both)]
        parts.append(lane_sums(by_s + by_both))
    return jnp.transpose(jnp.concatenate(parts, 0))


def own_receivers(data_ref):
    point = tuple(data_ref[0, 8 + axis : 9 + axis, :] for axis in range(3))
    normal = tuple(data_ref[0, 11 + axis : 12 + axis, :] for axis in range(3))
    return point, normal, cross(point, normal)


def own_segments(own_block, own_seg):
    lane = lax.broadcasted_iota(jnp.int32, (1, LANES), 1)
    first = pltpu.roll(own_block, own_seg, 1)
    second = jnp.where(lane == own_seg - 1, first, pltpu.roll(first, LANES - 1, 1))
    own_e = tuple(first[axis : axis + 1] for axis in range(3))
    segment, turn, span, span_core = segment_terms(own_e, tuple(second[axis : axis + 1] for axis in range(3)))
    return own_e, segment, turn, span, span_core


def early_kernel(chained, own_seg, *refs):
    data_ref, own_refs, rest = refs[0], refs[1:7], refs[7:]
    olds = rest[0:2] if chained else (None, None)
    rest = rest[2:] if chained else rest
    pair_sums(data_ref, own_refs, 0, data_ref.shape[0], own_seg, rest[2:], *olds, rest[0], rest[1])


def last_kernel(count, own_seg, *refs):
    data_ref, own_refs, old1_ref, old2_ref, rcv_out, vert_out, after_ref, new1_ref, new2_ref = (
        refs[0], refs[1:7], *refs[7:14])
    scratch = refs[14:]
    masks = exchange_masks(count)
    me = lax.axis_index("src")
    lane = lax.broadcasted_iota(jnp.int32, (1, LANES), 1)

    def place(device):
        return place_of((device & (count - 1)) ^ me, masks)

    def edge_sums():
        for block in range(count):
            after_ref[block] = data_ref[place((me ^ mask_at(block, masks)) + 1), 16:24, :]

        def spread(column):
            return jnp.broadcast_to(column, (column.shape[0], LANES))

        own_block = data_ref[0, 16:24, :]
        before = data_ref[place(me + count - 1), 16:24, :]
        own_p, own_n, own_m = own_receivers(data_ref)
        point = tuple(data_ref[:, 8 + axis, :] for axis in range(3))
        normal = tuple(data_ref[:, 11 + axis, :] for axis in range(3))
        moment = cross(point, normal)
        mine_last = spread(own_block[:, 2 * own_seg - 1 : 2 * own_seg])
        mine_next = spread(after_ref[0, :, own_seg : own_seg + 1])
        mine_weight = spread(own_block[:, own_seg - 1 : own_seg])
        before_last = spread(before[:, 2 * own_seg - 1 : 2 * own_seg])
        before_weight = spread(jnp.where(me == 0, 0.0, before[:, own_seg - 1 : own_seg]))
        mine_first = spread(own_block[:, own_seg : own_seg + 1])

        def rows(value, axis):
            return jnp.broadcast_to(value[axis : axis + 1], (count, LANES))

        def stacked(own, every):
            return tuple(
                jnp.concatenate([jnp.broadcast_to(a, (count, LANES)), b, b], 0) for a, b in zip(own, every))

        first = tuple(
            jnp.concatenate(
                [spread(data_ref[:, 16 + axis, 2 * own_seg - 1 : 2 * own_seg]), rows(mine_last, axis), rows(before_last, axis)], 0)
            for axis in range(3))
        second = tuple(
            jnp.concatenate(
                [spread(after_ref[:, axis, own_seg : own_seg + 1]), rows(mine_next, axis), rows(mine_first, axis)], 0)
            for axis in range(3))
        scales = [jnp.zeros((count, LANES), jnp.float32)] * 3
        for mode in range(8):
            left = data_ref[:, mode, :]
            scales[0] += spread(data_ref[:, 16 + mode, own_seg - 1 : own_seg]) * data_ref[0, mode : mode + 1, :]
            scales[1] += mine_weight[mode : mode + 1] * left
            scales[2] += before_weight[mode : mode + 1] * left
        segment, turn, span, span_core = segment_terms(first, second)
        normals = stacked(own_n, normal)
        rel, by_normal, by_dist2, by_along, by_span2 = pair_terms(
            stacked(own_p, point), normal_cross(normals, stacked(own_m, moment), segment, turn),
            first, segment, span, span_core, jnp.concatenate(scales, 0), True)

        def down(value):
            return jnp.sum(value, axis=0, keepdims=True)

        against_own, mine, ahead = slice(0, count), slice(count, 2 * count), slice(2 * count, 3 * count)
        swung, swept = cross(rel, normals), cross(normals, segment)
        edge_s = [(by_normal * segment[axis])[against_own] for axis in range(3)]
        edge_t = [(by_normal * turn[axis])[against_own] for axis in range(3)]
        edge_point = [a for a in cross(own_n, edge_s)]
        edge_normal = [down(a - b) for a, b in zip(cross(edge_s, own_p), edge_t)]
        leaving, arriving = [], []
        for axis in range(3):
            by_s = by_normal * swung[axis] + by_along * rel[axis] + by_span2 * segment[axis]
            by_p = by_dist2 * rel[axis] + by_along * segment[axis]
            by_r = by_normal * swept[axis] + by_p
            edge_point[axis] = down(edge_point[axis] + by_p[against_own])
            leaving.append(down((by_s + by_r)[mine]))
            arriving.append(down(by_s[ahead]))
        return edge_point, edge_normal, arriving, leaving

    found = []
    pair_sums(
        data_ref, own_refs, count - count // 4, count, own_seg, scratch, old1_ref, old2_ref, new1_ref, new2_ref)
    found.extend((*edge_sums(), receiver_totals(new1_ref, own_refs[0])))
    edge_point, edge_normal, arriving, leaving, totals = found
    for axis in range(3):
        value = totals[axis : axis + 1] + edge_point[axis]
        rcv_out[axis : axis + 1, :] = 0.2 * value if axis == 2 else value
        rcv_out[3 + axis : 4 + axis, :] = totals[3 + axis : 4 + axis] + edge_normal[axis]

    totals = segment_totals(new2_ref, own_refs[1], own_seg, arriving, leaving)
    for axis in range(3):
        by_second = totals[axis : axis + 1]
        shifted = jnp.concatenate([by_second[:, own_seg - 1 :], by_second[:, : own_seg - 1]], 1)
        result = shifted - totals[3 + axis : 4 + axis]
        vert_out[axis : axis + 1, :] = 0.2 * result if axis == 2 else result


def pair_scratch(blocks, own_seg):
    return [
        pltpu.VMEM((11, blocks // 2, LANES), jnp.float32),
        pltpu.VMEM((9, blocks, LANES), jnp.float32),
        pltpu.VMEM((LANES, blocks // 2 * LANES), jnp.float32),
        pltpu.VMEM((own_seg, blocks * LANES), jnp.float32),
        pltpu.VMEM((8, blocks // 2 * LANES), jnp.float32),
        pltpu.VMEM((8, blocks * LANES), jnp.float32),
        pltpu.VMEM((LANES, blocks // 2 * LANES), jnp.float32),
        pltpu.VMEM((own_seg, blocks * LANES), jnp.float32),
    ]


def sum_shapes(own_seg):
    return [pltpu.VMEM((9, LANES, LANES), jnp.float32), pltpu.VMEM((11, own_seg, LANES), jnp.float32)]


def last_scratch(count, own_seg):
    return [pltpu.VMEM((count, 8, LANES), jnp.float32)] + sum_shapes(own_seg) + pair_scratch(count // 4, own_seg)


def pair_cost(blocks, own_seg):
    pairs = 2 * blocks * own_seg * LANES
    return pl.CostEstimate(flops=100 * pairs, bytes_accessed=blocks * ROWS * LANES * 4, transcendentals=3 * pairs)


def on_device(rcv_points, rcv_normals, left_modes, vertices, connect, right_modes, mode_weights):
    count = lax.axis_size("src")
    own_seg = vertices.shape[1]
    value = pl.pallas_call(
        functools.partial(pack_kernel, own_seg),
        out_shape=pltpu.VMEM((ROWS, LANES), jnp.float32),
        in_specs=[VMEM] * 6 + [pl.BlockSpec(memory_space=pltpu.SMEM)],
        out_specs=VMEM,
    )(rcv_points, rcv_normals, left_modes, vertices, connect, right_modes, mode_weights)[None]
    params = pltpu.CompilerParams(vmem_limit_bytes=24 << 20)
    own = pl.pallas_call(
        functools.partial(own_kernel, own_seg),
        out_shape=(
            pltpu.VMEM((6, LANES, LANES), jnp.float32),
            pltpu.VMEM((8, own_seg, LANES), jnp.float32),
            pltpu.VMEM((LANES, 32), jnp.bfloat16),
            pltpu.VMEM((own_seg, 32), jnp.bfloat16),
            pltpu.VMEM((LANES, 32), jnp.bfloat16),
            pltpu.VMEM((own_seg, 32), jnp.bfloat16),
        ),
        in_specs=[VMEM],
        out_specs=(VMEM,) * 6,
        cost_estimate=pair_cost(2, own_seg),
        compiler_params=params,
    )(value)

    def exchange(block, mask):
        return lax.ppermute(block, "src", [(s, s ^ mask) for s in range(count)])

    def add_pairs(block, *sums):
        return pl.pallas_call(
            functools.partial(early_kernel, len(sums) > 0, own_seg),
            out_shape=tuple(sum_shapes(own_seg)),
            in_specs=[VMEM] * (7 + len(sums)),
            out_specs=(VMEM, VMEM),
            scratch_shapes=pair_scratch(block.shape[0], own_seg),
            cost_estimate=pair_cost(block.shape[0], own_seg),
            compiler_params=params,
        )(block, *own, *sums)

    masks = exchange_masks(count)
    for mask in masks[:-3]:
        value = jnp.concatenate([value, exchange(value, mask)], 0)
    arrived, early = exchange(value, masks[-3]), exchange(value, masks[-2])
    late = exchange(arrived, masks[-2])
    value = jnp.concatenate([value, arrived], 0)
    beside = exchange(value, masks[-1])
    sums = add_pairs(value)
    sums = add_pairs(beside, *sums)
    late, sums = lax.optimization_barrier((late, sums))
    across = jnp.concatenate([early, late], 0)
    opposite = exchange(across, masks[-1])
    sums = add_pairs(across, *sums)
    value = jnp.concatenate([value, across, beside, opposite], 0)
    return pl.pallas_call(
        functools.partial(last_kernel, count, own_seg),
        out_shape=(
            jax.ShapeDtypeStruct((6, LANES), jnp.float32),
            jax.ShapeDtypeStruct((3, own_seg), jnp.float32),
        ),
        in_specs=[VMEM] * 9,
        out_specs=(VMEM, VMEM),
        scratch_shapes=last_scratch(count, own_seg),
        cost_estimate=pair_cost(count // 4, own_seg),
        compiler_params=params,
    )(value, *own, *sums)


def solution(mesh):
    split = P(None, ("group", "src"))
    return jax.shard_map(
        on_device, mesh=mesh, in_specs=(split,) * 6 + (P("group"),), out_specs=(split, split), check_vma=False
    )
```

```python
import functools
import math

import jax
import jax.numpy as jnp
from jax import lax
from jax.experimental import pallas as pl
from jax.experimental.pallas import tpu as pltpu
from jax.sharding import PartitionSpec as P

core_term = 0.05
inverse_four_pi = 0.25 / math.pi

LANES = 128
ROWS = 24
CHUNK = 64
FINISH = 32
VMEM = pl.BlockSpec(memory_space=pltpu.VMEM)


def exchange_masks(count):
    masks = []
    step = count // 2
    while step > 1:
        masks.append(step + 1)
        step //= 2
    return masks[:-2] + [masks[-1], masks[-2], 1]


def mask_at(place, masks):
    value = 0
    for bit, mask in enumerate(masks):
        if place >> bit & 1:
            value ^= mask
    return value


def place_of(value, masks):
    place = 0
    rest = value & 1
    for bit, mask in enumerate(masks[:-1]):
        taken = lax.shift_right_logical(value, mask.bit_length() - 1) & 1
        place = place + taken * (1 << bit)
        rest = rest ^ taken
    return place + rest * (1 << (len(masks) - 1))


def high_low(value):
    high = value.astype(jnp.bfloat16).astype(jnp.float32)
    return high, value - high


def dot_nt(left, right):
    return lax.dot_general(left, right, (((1,), (1,)), ((), ())), preferred_element_type=jnp.float32)


def cross(a, b):
    return (a[1] * b[2] - a[2] * b[1], a[2] * b[0] - a[0] * b[2], a[0] * b[1] - a[1] * b[0])


def normal_cross(normal, moment, segment, turn):
    return (moment[0] * segment[0] + moment[1] * segment[1] + moment[2] * segment[2]) - (
        normal[0] * turn[0] + normal[1] * turn[1] + normal[2] * turn[2]
    )


def pair_terms(point, cross_n, first, segment, span, span_core, scale, want_span):
    rel = tuple(p - e for p, e in zip(point, first))
    dist_sq = rel[0] * rel[0] + rel[1] * rel[1] + rel[2] * rel[2]
    along = segment[0] * rel[0] + segment[1] * rel[1] + segment[2] * rel[2]
    other = along - span
    second_sq = dist_sq - along - other
    inv_first = lax.rsqrt(dist_sq)
    inv_second = lax.rsqrt(second_sq)
    inv_den = 1.0 / ((span * dist_sq + span_core) - along * along)
    part_first = along * inv_first
    part_second = other * inv_second
    line = part_first - part_second
    scaled = scale * inv_den
    by_normal = scaled * line
    by_line = scaled * cross_n
    by_den = (by_normal * cross_n) * inv_den
    by_den2 = by_den + by_den
    cube_first = part_first * (inv_first * inv_first)
    cube_second = part_second * (inv_second * inv_second)
    by_dist2 = by_line * (cube_second - cube_first) - by_den2 * span
    by_along = by_line * ((inv_first - inv_second) - cube_second) + by_den2 * along
    if not want_span:
        return rel, by_normal, by_dist2, by_along
    by_span2 = by_line * ((inv_second + inv_second) + cube_second) - by_den2 * (dist_sq + core_term)
    return rel, by_normal, by_dist2, by_along, by_span2


def segment_terms(first, second):
    segment = tuple(b - a for a, b in zip(first, second))
    span = segment[0] * segment[0] + segment[1] * segment[1] + segment[2] * segment[2]
    return segment, cross(segment, first), span, core_term * span + core_term


def pack_kernel(own_seg, points_ref, normals_ref, left_ref, vertices_ref, connect_ref, right_ref, weights_ref, out_ref):
    base = lax.axis_index("src") * own_seg
    row8 = lax.broadcasted_iota(jnp.int32, (8, LANES), 0)
    weight = jnp.zeros((8, LANES), jnp.float32)
    for mode in range(8):
        weight = jnp.where(row8 == mode, weights_ref[mode], weight)
    weighted = right_ref[...] * (weight * inverse_four_pi)
    high, rest = high_low(weighted)
    middle, low = high_low(rest)
    parts = jnp.concatenate([high, middle, low, jnp.zeros_like(low)], 0).astype(jnp.bfloat16)
    local = connect_ref[0:1, :] - base
    hit = lax.broadcasted_iota(jnp.int32, (LANES, LANES), 0) == local
    folded = dot_nt(parts, hit.astype(jnp.float32).astype(jnp.bfloat16))
    folded = folded[0:8] + (folded[8:16] + folded[16:24])
    out_ref[0:8, :] = left_ref[...]
    out_ref[8:10, :] = points_ref[0:2, :]
    out_ref[10:11, :] = 0.5 + 0.2 * points_ref[2:3, :]
    out_ref[11:14, :] = normals_ref[...]
    out_ref[14:16, :] = jnp.zeros((2, LANES), jnp.float32)
    out_ref[16:24, :] = folded
    out_ref[16:18, own_seg : 2 * own_seg] = vertices_ref[0:2, :]
    out_ref[18:19, own_seg : 2 * own_seg] = 0.2 * vertices_ref[2:3, :]


def stack_hhll(rows):
    high, low = high_low(rows)
    return jnp.transpose(jnp.concatenate([high, high, low, low], 0)).astype(jnp.bfloat16)


def stack_hlhl(rows):
    high, low = high_low(rows)
    both = jnp.concatenate([high, low], 0).astype(jnp.bfloat16)
    return jnp.concatenate([both, both], 0)


def lane_edges(own_seg):
    lane = lax.broadcasted_iota(jnp.int32, (1, LANES), 1)
    return (lane == own_seg - 1) | (lane == 2 * own_seg - 1)


def own_kernel(own_seg, data_ref, col1_ref, col2_ref, left_ref, right_ref, moment_ref, turn_ref):
    def columns(rows, out_ref):
        pad = jnp.zeros((16 - len(rows), LANES), jnp.float32)
        cols = jnp.transpose(jnp.concatenate(list(rows) + [pad], 0))
        count = out_ref.shape[1]
        for k in range(len(rows)):
            out_ref[k] = jnp.broadcast_to(cols[0:count, k : k + 1], (count, LANES))

    own_block = data_ref[0, 16:24, :]
    point, normal, moment = own_receivers(data_ref)
    columns([*point, *normal], col1_ref)
    own_e, own_s, own_t, span, span_core = own_segments(own_block, own_seg)
    columns([*own_e, *own_s, span, span_core], col2_ref)
    left_ref[...] = stack_hhll(data_ref[0, 0:8, :])
    right_ref[...] = stack_hhll(jnp.where(lane_edges(own_seg), 0.0, own_block))[0:own_seg]
    pad = jnp.zeros((2, LANES), jnp.float32)
    moment_ref[...] = stack_hhll(jnp.concatenate([*moment, *normal, pad], 0))
    turn_ref[...] = stack_hhll(jnp.concatenate([*own_s, *(-value for value in own_t), pad], 0))[0:own_seg]


def pair_sums(data_ref, own_refs, begin, end, own_seg, scratch, old1, old2, new1, new2, between=None):
    seg_ref, rec_ref, scale1_ref, scale2_ref, row1_ref, row2_ref, cross1_ref, cross2_ref = scratch
    col1_ref, col2_ref, left_ref, right_ref, moment_ref, turn_ref = own_refs
    blocks = end - begin
    tiles = blocks // 2
    lane = lax.broadcasted_iota(jnp.int32, (1, LANES), 1)
    low_half = lane < own_seg
    at_edge = lane_edges(own_seg)

    folded = []
    for tile in range(tiles):
        block_a, block_b = data_ref[begin + 2 * tile, 16:24, :], data_ref[begin + 2 * tile + 1, 16:24, :]
        both = jnp.where(low_half, block_a, pltpu.roll(block_b, own_seg, 1))
        folded.append(jnp.where(at_edge, 0.0, both))
        first = jnp.where(low_half, pltpu.roll(block_a, own_seg, 1), block_b)
        second = jnp.where(at_edge, first, pltpu.roll(first, LANES - 1, 1))
        for axis in range(3):
            seg_ref[axis, tile : tile + 1, :] = first[axis : axis + 1]
            seg_ref[3 + axis, tile : tile + 1, :] = second[axis : axis + 1]
    first = tuple(seg_ref[axis] for axis in range(3))
    segment, turn, span, span_core = segment_terms(first, tuple(seg_ref[3 + axis] for axis in range(3)))
    for axis in range(3):
        seg_ref[3 + axis] = segment[axis]
        seg_ref[6 + axis] = turn[axis]
    seg_ref[9] = span
    seg_ref[10] = span_core

    point = tuple(data_ref[begin:end, 8 + axis, :] for axis in range(3))
    normal = tuple(data_ref[begin:end, 11 + axis, :] for axis in range(3))
    moment = cross(point, normal)
    for axis in range(3):
        rec_ref[axis] = point[axis]
        rec_ref[3 + axis] = normal[axis]
        rec_ref[6 + axis] = moment[axis]

    for ref in (row1_ref, row2_ref):
        ref[6:8, :] = jnp.zeros((2, ref.shape[1]), jnp.float32)
    for axis in range(3):
        for tile in range(tiles):
            at = slice(tile * LANES, (tile + 1) * LANES)
            row1_ref[axis : axis + 1, at] = segment[axis][tile : tile + 1]
            row1_ref[3 + axis : 4 + axis, at] = -turn[axis][tile : tile + 1]
        for block in range(blocks):
            at = slice(block * LANES, (block + 1) * LANES)
            row2_ref[axis : axis + 1, at] = moment[axis][block : block + 1]
            row2_ref[3 + axis : 4 + axis, at] = normal[axis][block : block + 1]
    cross1_ref[...] = jnp.dot(moment_ref[...], stack_hlhl(row1_ref[...]), preferred_element_type=jnp.float32)
    cross2_ref[...] = jnp.dot(turn_ref[...], stack_hlhl(row2_ref[...]), preferred_element_type=jnp.float32)

    scale1_ref[...] = jnp.dot(
        left_ref[...], stack_hlhl(jnp.concatenate(folded, 1)), preferred_element_type=jnp.float32)
    scale2_ref[...] = jnp.dot(
        right_ref[...], stack_hlhl(jnp.concatenate([data_ref[b, 0:8, :] for b in range(begin, end)], 1)),
        preferred_element_type=jnp.float32)

    def initial(old, count, start):
        if old is None:
            return [jnp.zeros((CHUNK, LANES), jnp.float32) for _ in range(count)]
        return [old[k, start : start + CHUNK, :] for k in range(count)]

    for start in range(0, LANES, CHUNK):
        col = [col1_ref[k, start : start + CHUNK, :] for k in range(3)]
        sums = initial(old1, 9, start)
        for tile in range(tiles):
            row = [seg_ref[k, tile : tile + 1, :] for k in range(11)]
            scale = scale1_ref[start : start + CHUNK, tile * LANES : (tile + 1) * LANES]
            rel, by_normal, by_dist2, by_along = pair_terms(
                col, cross1_ref[start : start + CHUNK, tile * LANES : (tile + 1) * LANES],
                row[0:3], row[3:6], row[9], row[10], scale, False)
            for axis in range(3):
                sums[axis] += by_normal * row[3 + axis]
                sums[3 + axis] += by_normal * row[6 + axis]
                sums[6 + axis] += by_dist2 * rel[axis] + by_along * row[3 + axis]
        for k in range(9):
            new1[k, start : start + CHUNK, :] = sums[k]

    if between is not None:
        between()

    for start in range(0, own_seg, CHUNK):
        col = [col2_ref[k, start : start + CHUNK, :] for k in range(8)]
        sums = initial(old2, 11, start)
        for block in range(blocks):
            row = [rec_ref[k, block : block + 1, :] for k in range(9)]
            scale = scale2_ref[start : start + CHUNK, block * LANES : (block + 1) * LANES]
            rel, by_normal, by_dist2, by_along, by_span2 = pair_terms(
                row[0:3], cross2_ref[start : start + CHUNK, block * LANES : (block + 1) * LANES],
                col[0:3], col[3:6], col[6], col[7], scale, True)
            for axis in range(3):
                sums[axis] += by_normal * row[3 + axis]
                sums[3 + axis] += by_normal * row[6 + axis] + by_along * rel[axis]
                sums[6 + axis] += by_dist2 * rel[axis]
            sums[9] += by_along
            sums[10] += by_span2
        for k in range(11):
            new2[k, start : start + CHUNK, :] = sums[k]


def lane_sums(values):
    rows = values[0].shape[0]
    column = lax.broadcasted_iota(jnp.int32, (rows, 16), 1)
    result = jnp.zeros((rows, 16), jnp.float32)
    for index, value in enumerate(values):
        result = jnp.where(column == index, jnp.sum(value, axis=1, keepdims=True), result)
    return result


def receiver_totals(sums_ref, col_ref):
    parts = []
    for start in range(0, LANES, FINISH):
        sums = [sums_ref[k, start : start + FINISH, :] for k in range(9)]
        col = [col_ref[k, start : start + FINISH, :] for k in range(6)]
        by_point = [a + b for a, b in zip(cross(col[3:6], sums[0:3]), sums[6:9])]
        by_normal = [a - b for a, b in zip(cross(sums[0:3], col[0:3]), sums[3:6])]
        parts.append(lane_sums(by_point + by_normal))
    return jnp.transpose(jnp.concatenate(parts, 0))


def segment_totals(sums_ref, col_ref, own_seg, arriving, leaving):
    parts = []
    for start in range(0, own_seg, FINISH):
        sums = [sums_ref[k, start : start + FINISH, :] for k in range(11)]
        col = [col_ref[k, start : start + FINISH, :] for k in range(6)]
        turned, swept = cross(col[0:3], sums[0:3]), cross(sums[0:3], col[3:6])
        by_s = [sums[3 + k] - turned[k] + col[3 + k] * sums[10] for k in range(3)]
        by_both = [by_s[k] + (swept[k] + sums[6 + k] + col[3 + k] * sums[9]) for k in range(3)]
        if start + FINISH == own_seg:
            last = lax.broadcasted_iota(jnp.int32, (FINISH, LANES), 0) == FINISH - 1
            by_s = [jnp.where(last, a, b) for a, b in zip(arriving, by_s)]
            by_both = [jnp.where(last, a, b) for a, b in zip(leaving, by_both)]
        parts.append(lane_sums(by_s + by_both))
    return jnp.transpose(jnp.concatenate(parts, 0))


def own_receivers(data_ref):
    point = tuple(data_ref[0, 8 + axis : 9 + axis, :] for axis in range(3))
    normal = tuple(data_ref[0, 11 + axis : 12 + axis, :] for axis in range(3))
    return point, normal, cross(point, normal)


def own_segments(own_block, own_seg):
    lane = lax.broadcasted_iota(jnp.int32, (1, LANES), 1)
    first = pltpu.roll(own_block, own_seg, 1)
    second = jnp.where(lane == own_seg - 1, first, pltpu.roll(first, LANES - 1, 1))
    own_e = tuple(first[axis : axis + 1] for axis in range(3))
    segment, turn, span, span_core = segment_terms(own_e, tuple(second[axis : axis + 1] for axis in range(3)))
    return own_e, segment, turn, span, span_core


def early_kernel(chained, own_seg, *refs):
    data_ref, own_refs, rest = refs[0], refs[1:7], refs[7:]
    olds = rest[0:2] if chained else (None, None)
    rest = rest[2:] if chained else rest
    pair_sums(data_ref, own_refs, 0, data_ref.shape[0], own_seg, rest[2:], *olds, rest[0], rest[1])


def last_kernel(count, own_seg, *refs):
    data_ref, own_refs, old1_ref, old2_ref, rcv_out, vert_out, after_ref, new1_ref, new2_ref = (
        refs[0], refs[1:7], *refs[7:14])
    scratch = refs[14:]
    masks = exchange_masks(count)
    me = lax.axis_index("src")
    lane = lax.broadcasted_iota(jnp.int32, (1, LANES), 1)

    def place(device):
        return place_of((device & (count - 1)) ^ me, masks)

    def edge_sums():
        for block in range(count):
            after_ref[block] = data_ref[place((me ^ mask_at(block, masks)) + 1), 16:24, :]

        def spread(column):
            return jnp.broadcast_to(column, (column.shape[0], LANES))

        own_block = data_ref[0, 16:24, :]
        before = data_ref[place(me + count - 1), 16:24, :]
        own_p, own_n, own_m = own_receivers(data_ref)
        point = tuple(data_ref[:, 8 + axis, :] for axis in range(3))
        normal = tuple(data_ref[:, 11 + axis, :] for axis in range(3))
        moment = cross(point, normal)
        mine_last = spread(own_block[:, 2 * own_seg - 1 : 2 * own_seg])
        mine_next = spread(after_ref[0, :, own_seg : own_seg + 1])
        mine_weight = spread(own_block[:, own_seg - 1 : own_seg])
        before_last = spread(before[:, 2 * own_seg - 1 : 2 * own_seg])
        before_weight = spread(jnp.where(me == 0, 0.0, before[:, own_seg - 1 : own_seg]))
        mine_first = spread(own_block[:, own_seg : own_seg + 1])

        def rows(value, axis):
            return jnp.broadcast_to(value[axis : axis + 1], (count, LANES))

        def stacked(own, every):
            return tuple(
                jnp.concatenate([jnp.broadcast_to(a, (count, LANES)), b, b], 0) for a, b in zip(own, every))

        first = tuple(
            jnp.concatenate(
                [spread(data_ref[:, 16 + axis, 2 * own_seg - 1 : 2 * own_seg]), rows(mine_last, axis), rows(before_last, axis)], 0)
            for axis in range(3))
        second = tuple(
            jnp.concatenate(
                [spread(after_ref[:, axis, own_seg : own_seg + 1]), rows(mine_next, axis), rows(mine_first, axis)], 0)
            for axis in range(3))
        scales = [jnp.zeros((count, LANES), jnp.float32)] * 3
        for mode in range(8):
            left = data_ref[:, mode, :]
            scales[0] += spread(data_ref[:, 16 + mode, own_seg - 1 : own_seg]) * data_ref[0, mode : mode + 1, :]
            scales[1] += mine_weight[mode : mode + 1] * left
            scales[2] += before_weight[mode : mode + 1] * left
        segment, turn, span, span_core = segment_terms(first, second)
        normals = stacked(own_n, normal)
        rel, by_normal, by_dist2, by_along, by_span2 = pair_terms(
            stacked(own_p, point), normal_cross(normals, stacked(own_m, moment), segment, turn),
            first, segment, span, span_core, jnp.concatenate(scales, 0), True)

        def down(value):
            return jnp.sum(value, axis=0, keepdims=True)

        against_own, mine, ahead = slice(0, count), slice(count, 2 * count), slice(2 * count, 3 * count)
        swung, swept = cross(rel, normals), cross(normals, segment)
        edge_s = [(by_normal * segment[axis])[against_own] for axis in range(3)]
        edge_t = [(by_normal * turn[axis])[against_own] for axis in range(3)]
        edge_point = [a for a in cross(own_n, edge_s)]
        edge_normal = [down(a - b) for a, b in zip(cross(edge_s, own_p), edge_t)]
        leaving, arriving = [], []
        for axis in range(3):
            by_s = by_normal * swung[axis] + by_along * rel[axis] + by_span2 * segment[axis]
            by_p = by_dist2 * rel[axis] + by_along * segment[axis]
            by_r = by_normal * swept[axis] + by_p
            edge_point[axis] = down(edge_point[axis] + by_p[against_own])
            leaving.append(down((by_s + by_r)[mine]))
            arriving.append(down(by_s[ahead]))
        return edge_point, edge_normal, arriving, leaving

    found = []
    pair_sums(
        data_ref, own_refs, count - count // 4, count, own_seg, scratch, old1_ref, old2_ref, new1_ref, new2_ref,
        lambda: found.extend((*edge_sums(), receiver_totals(new1_ref, own_refs[0]))))
    edge_point, edge_normal, arriving, leaving, totals = found
    for axis in range(3):
        value = totals[axis : axis + 1] + edge_point[axis]
        rcv_out[axis : axis + 1, :] = 0.2 * value if axis == 2 else value
        rcv_out[3 + axis : 4 + axis, :] = totals[3 + axis : 4 + axis] + edge_normal[axis]

    totals = segment_totals(new2_ref, own_refs[1], own_seg, arriving, leaving)
    for axis in range(3):
        by_second = totals[axis : axis + 1]
        shifted = jnp.concatenate([by_second[:, own_seg - 1 :], by_second[:, : own_seg - 1]], 1)
        result = shifted - totals[3 + axis : 4 + axis]
        vert_out[axis : axis + 1, :] = 0.2 * result if axis == 2 else result


def pair_scratch(blocks, own_seg):
    return [
        pltpu.VMEM((11, blocks // 2, LANES), jnp.float32),
        pltpu.VMEM((9, blocks, LANES), jnp.float32),
        pltpu.VMEM((LANES, blocks // 2 * LANES), jnp.float32),
        pltpu.VMEM((own_seg, blocks * LANES), jnp.float32),
        pltpu.VMEM((8, blocks // 2 * LANES), jnp.float32),
        pltpu.VMEM((8, blocks * LANES), jnp.float32),
        pltpu.VMEM((LANES, blocks // 2 * LANES), jnp.float32),
        pltpu.VMEM((own_seg, blocks * LANES), jnp.float32),
    ]


def sum_shapes(own_seg):
    return [pltpu.VMEM((9, LANES, LANES), jnp.float32), pltpu.VMEM((11, own_seg, LANES), jnp.float32)]


def last_scratch(count, own_seg):
    return [pltpu.VMEM((count, 8, LANES), jnp.float32)] + sum_shapes(own_seg) + pair_scratch(count // 4, own_seg)


def pair_cost(blocks, own_seg):
    pairs = 2 * blocks * own_seg * LANES
    return pl.CostEstimate(flops=100 * pairs, bytes_accessed=blocks * ROWS * LANES * 4, transcendentals=3 * pairs)


def on_device(rcv_points, rcv_normals, left_modes, vertices, connect, right_modes, mode_weights):
    count = lax.axis_size("src")
    own_seg = vertices.shape[1]
    value = pl.pallas_call(
        functools.partial(pack_kernel, own_seg),
        out_shape=pltpu.VMEM((ROWS, LANES), jnp.float32),
        in_specs=[VMEM] * 6 + [pl.BlockSpec(memory_space=pltpu.SMEM)],
        out_specs=VMEM,
    )(rcv_points, rcv_normals, left_modes, vertices, connect, right_modes, mode_weights)[None]
    params = pltpu.CompilerParams(vmem_limit_bytes=24 << 20)
    own = pl.pallas_call(
        functools.partial(own_kernel, own_seg),
        out_shape=(
            pltpu.VMEM((6, LANES, LANES), jnp.float32),
            pltpu.VMEM((8, own_seg, LANES), jnp.float32),
            pltpu.VMEM((LANES, 32), jnp.bfloat16),
            pltpu.VMEM((own_seg, 32), jnp.bfloat16),
            pltpu.VMEM((LANES, 32), jnp.bfloat16),
            pltpu.VMEM((own_seg, 32), jnp.bfloat16),
        ),
        in_specs=[VMEM],
        out_specs=(VMEM,) * 6,
        cost_estimate=pair_cost(2, own_seg),
        compiler_params=params,
    )(value)

    def exchange(block, mask):
        return lax.ppermute(block, "src", [(s, s ^ mask) for s in range(count)])

    def add_pairs(block, *sums):
        return pl.pallas_call(
            functools.partial(early_kernel, len(sums) > 0, own_seg),
            out_shape=tuple(sum_shapes(own_seg)),
            in_specs=[VMEM] * (7 + len(sums)),
            out_specs=(VMEM, VMEM),
            scratch_shapes=pair_scratch(block.shape[0], own_seg),
            cost_estimate=pair_cost(block.shape[0], own_seg),
            compiler_params=params,
        )(block, *own, *sums)

    masks = exchange_masks(count)
    for mask in masks[:-3]:
        value = jnp.concatenate([value, exchange(value, mask)], 0)
    arrived, early = exchange(value, masks[-3]), exchange(value, masks[-2])
    late = exchange(arrived, masks[-2])
    value = jnp.concatenate([value, arrived], 0)
    beside = exchange(value, masks[-1])
    sums = add_pairs(value)
    sums = add_pairs(beside, *sums)
    late, sums = lax.optimization_barrier((late, sums))
    across = jnp.concatenate([early, late], 0)
    opposite = exchange(across, masks[-1])
    sums = add_pairs(across, *sums)
    value = jnp.concatenate([value, across, beside, opposite], 0)
    return pl.pallas_call(
        functools.partial(last_kernel, count, own_seg),
        out_shape=(
            jax.ShapeDtypeStruct((6, LANES), jnp.float32),
            jax.ShapeDtypeStruct((3, own_seg), jnp.float32),
        ),
        in_specs=[VMEM] * 9,
        out_specs=(VMEM, VMEM),
        scratch_shapes=last_scratch(count, own_seg),
        cost_estimate=pair_cost(count // 4, own_seg),
        compiler_params=params,
    )(value, *own, *sums)


def solution(mesh):
    split = P(None, ("group", "src"))
    return jax.shard_map(
        on_device, mesh=mesh, in_specs=(split,) * 6 + (P("group"),), out_specs=(split, split), check_vma=False
    )
```
